32 devices in a mesh: fsdp: 8 (over z, y), seq: 4 (over x, core).
Axes of the slice: x: 2, y: 2, z: 4, core: 2. Of those that a mesh axis runs over, the one named last changes fastest.
Arguments:
- tokens: bfloat16 [16, 1024, 512], P('fsdp', 'seq'), may hold values from -6 to 6
- placement_order: int32 [16], P('fsdp'), may hold values from 0 to 15, each once
- group_lengths: int32 [16, 3], replicated, may hold values from 0 to 896, as said below
- first_gain: bfloat16 [512], P('fsdp'), may hold values from 0.5 to 1.5
- first_shift: bfloat16 [512], P('fsdp'), may hold values from -1.75 to 1.75
- attention_in: bfloat16 [512, 1536], P('fsdp'), may hold values from -0.25 to 0.25
- query_bias: bfloat16 [512], P('fsdp'), may hold values from -3 to 3
- value_bias: bfloat16 [512], P('fsdp'), may hold values from -0.625 to 0.625
- attention_out: bfloat16 [512, 512], P('fsdp'), may hold values from -2 to 2
- attention_bias: bfloat16 [512], P('fsdp'), may hold values from -1.75 to 1.75
- second_gain: bfloat16 [512], P('fsdp'), may hold values from 0.5 to 1.5
- second_shift: bfloat16 [512], P('fsdp'), may hold values from -1.75 to 1.75
- expand_weight: bfloat16 [512, 2048], P('fsdp'), may hold values from -0.25 to 0.25
- expand_bias: bfloat16 [2048], P('fsdp'), may hold values from -3 to 3
- contract_weight: bfloat16 [2048, 512], P('fsdp'), may hold values from -0.125 to 0.125
- contract_bias: bfloat16 [512], P('fsdp'), may hold values from -1.75 to 1.75
- cotangent: bfloat16 [16, 1024, 512], P('fsdp', 'seq'), may hold values from -6 to 6
Outputs:
- layer_out: bfloat16 [16, 1024, 512], P('fsdp', 'seq')
- grad_tokens: bfloat16 [16, 1024, 512], P('fsdp', 'seq')
- grad_first_gain: float32 [512], P('fsdp')
- grad_first_shift: float32 [512], P('fsdp')
- grad_attention_in: float32 [512, 1536], P('fsdp')
- grad_query_bias: float32 [512], P('fsdp')
- grad_value_bias: float32 [512], P('fsdp')
- grad_attention_out: float32 [512, 512], P('fsdp')
- grad_attention_bias: float32 [512], P('fsdp')
- grad_second_gain: float32 [512], P('fsdp')
- grad_second_shift: float32 [512], P('fsdp')
- grad_expand_weight: float32 [512, 2048], P('fsdp')
- grad_expand_bias: float32 [2048], P('fsdp')
- grad_contract_weight: float32 [2048, 512], P('fsdp')
- grad_contract_bias: float32 [512], P('fsdp')
The draws below stay inside these ranges and needn't reach their ends.
Inputs may be any that keep to these rules, and one draw needn't show every extreme that they name: `group_lengths`: row g gives group g's prompt length, first continuation length and second continuation length (0 when the group has one continuation); the three sum to 1024; a prompt has 128 to 512 positions and every present continuation at least one; some group has one continuation and some has two. Slot b, the slot of micro-batch b % 2 on index b // 2 of fsdp, holds group placement_order[b]; each group once.
All inputs are finite; a program needn't handle non-finite values.
Results may differ from the reference program's by a relative error of at most 0.019.
Values may be sent and summed in bfloat16 or wider, within the bound.
A program may use at most 128 MiB of HBM per device.

```python
import math
import jax
import jax.numpy as jnp
from jax import lax

D = 512
HEADS = 8
HD = 64
FF = 2048
SEQ_LEN = 1024
GROUPS = 16


def draw_group_lengths(key, part):
    keys = jax.random.split(key, 5)
    rows = jnp.arange(GROUPS, dtype=jnp.int32)
    count = 1 + jax.random.randint(keys[0], (GROUPS,), 0, 2)
    prompt = jax.random.randint(keys[1], (GROUPS,), SEQ_LEN // 8, SEQ_LEN // 2 + 1)
    first_single = jax.random.randint(keys[2], (), 0, GROUPS)
    first_double = (first_single + 1 + jax.random.randint(keys[3], (), 0, GROUPS - 1)) % GROUPS
    count = jnp.where(rows == first_single, 1, jnp.where(rows == first_double, 2, count))
    prompt = jnp.where(rows == first_single, SEQ_LEN // 8, prompt)
    split_len = jax.random.randint(keys[4], (GROUPS,), 1, SEQ_LEN - prompt)
    first_len = jnp.where(count == 1, SEQ_LEN - prompt, split_len)
    second_len = SEQ_LEN - prompt - first_len
    return jnp.stack([prompt, first_len, second_len], axis=1).astype(jnp.int32)


def shard_levels(rng, extent, shards, least, top_value):
    level = 1.0
    for dim, shards_of in shards:
        steps = jax.random.uniform(jax.random.fold_in(jax.random.fold_in(rng, 6), dim), (shards_of,), jnp.float32, least / len(shards), top_value / len(shards))
        level = level * jnp.repeat(jnp.exp(steps), extent[dim] // shards_of).reshape((-1,) + (1,) * (len(extent) - 1 - dim))
    return level


def gaussian(stream_key, shape, width, limit, cuts=(), kind=jnp.bfloat16):
    array = width * jax.random.normal(stream_key, shape, jnp.float32)
    if cuts:
        array = array * shard_levels(stream_key, shape, cuts, -0.22, 0.18)
    return jnp.clip(array, -limit, limit).astype(kind)


def setup_inputs(seed: int = 0) -> dict:
    streams_of = jax.random.split(jax.random.key(seed), 18)
    tokens = gaussian(streams_of[0], (GROUPS, SEQ_LEN, D), 1.0, 6.0, ((0, 8), (1, 4)))
    placement_order = jax.random.permutation(streams_of[1], GROUPS).astype(jnp.int32)
    group_lengths = draw_group_lengths(jax.random.fold_in(streams_of[17], 71), 0)
    first_gain = jnp.clip(0.5 + 1.0 * jax.random.uniform(streams_of[3], (D,), jnp.float32) ** shard_levels(streams_of[3], (D,), ((0, 8),), -0.2, 0.2), 0.5, 1.5).astype(jnp.bfloat16)
    first_shift = gaussian(streams_of[4], (D,), 0.3, 1.75, ((0, 8),))
    attention_in = gaussian(streams_of[5], (D, 3 * D), D ** -0.5, 0.25, ((0, 8),))
    query_bias = gaussian(streams_of[6], (D,), 0.5, 3.0, ((0, 8),))
    value_bias = gaussian(streams_of[7], (D,), 0.1, 0.625, ((0, 8),))
    attention_out = gaussian(streams_of[8], (D, D), (D // 64) ** -0.5, 2.0, ((0, 8),))
    attention_bias = gaussian(streams_of[9], (D,), 0.3, 1.75, ((0, 8),))
    second_gain = jnp.clip(0.5 + 1.0 * jax.random.uniform(streams_of[10], (D,), jnp.float32) ** shard_levels(streams_of[10], (D,), ((0, 8),), -0.2, 0.2), 0.5, 1.5).astype(jnp.bfloat16)
    second_shift = gaussian(streams_of[11], (D,), 0.3, 1.75, ((0, 8),))
    expand_weight = gaussian(streams_of[12], (D, FF), D ** -0.5, 0.25, ((0, 8),))
    expand_bias = gaussian(streams_of[13], (FF,), 0.5, 3.0, ((0, 8),))
    contract_weight = gaussian(streams_of[14], (FF, D), FF ** -0.5, 0.125, ((0, 8),))
    contract_bias = gaussian(streams_of[15], (D,), 0.3, 1.75, ((0, 8),))
    cotangent = gaussian(streams_of[16], (GROUPS, SEQ_LEN, D), 1.0, 6.0, ((0, 8), (1, 4)))
    return dict(tokens=tokens, placement_order=placement_order, group_lengths=group_lengths, first_gain=first_gain, first_shift=first_shift, attention_in=attention_in, query_bias=query_bias, value_bias=value_bias, attention_out=attention_out, attention_bias=attention_bias, second_gain=second_gain, second_shift=second_shift, expand_weight=expand_weight, expand_bias=expand_bias, contract_weight=contract_weight, contract_bias=contract_bias, cotangent=cotangent)


norm_eps = 1e-05

@jax.custom_vjp
def low(v):
    return lax.optimization_barrier(v.astype(jnp.bfloat16)).astype(jnp.float32)

@jax.custom_vjp
def low_back(v):
    return v

def low_keep(v):
    return (low(v), None)

def low_pass(kept, grad):
    return (grad,)

def back_keep(v):
    return (v, None)

def back_low(kept, grad):
    return (low(grad),)
low.defvjp(low_keep, low_pass)
low_back.defvjp(back_keep, back_low)

def matmul(left, right):
    return jnp.dot(left, right, precision=lax.Precision.HIGHEST, preferred_element_type=jnp.float32)

def layer_norm(values, gain, shift):
    mean = lax.optimization_barrier(jnp.mean(values, axis=-1, keepdims=True))
    centred = values - mean
    variance = lax.optimization_barrier(jnp.mean(centred * centred, axis=-1, keepdims=True))
    return centred * lax.rsqrt(variance + norm_eps) * gain + shift

def attend(query, keys, values, segment):
    scale = 1.0 / math.sqrt(HD)
    block = min(512, SEQ_LEN)
    key_pos = jnp.arange(SEQ_LEN, dtype=jnp.int32)

    def one_block(start):
        query_blk = lax.dynamic_slice_in_dim(query, start, block, 0)
        query_pos = start + jnp.arange(block, dtype=jnp.int32)
        query_seg = lax.dynamic_slice_in_dim(segment, start, block, 0)
        scores = jnp.einsum('qhd,khd->hqk', query_blk, keys, precision=lax.Precision.HIGHEST) * scale
        scores = low_back(scores)
        allowed = (key_pos[None, :] <= query_pos[:, None]) & ((segment[None, :] == query_seg[:, None]) | (segment[None, :] == 0))
        scores = jnp.where(allowed[None], scores, -1e+30)
        weights = low(jax.nn.softmax(scores, axis=-1))
        return jnp.einsum('hqk,khd->qhd', weights, values, precision=lax.Precision.HIGHEST)
    starts = jnp.arange(SEQ_LEN // block, dtype=jnp.int32) * block
    mixed = lax.map(jax.checkpoint(one_block), starts)
    return mixed.reshape(SEQ_LEN, D)

def group_forward(inputs, segment, params):
    gain_one, shift_one, w_in, bias_query, bias_value, w_out, bias_attention, gain_two, shift_two, w_expand, bias_expand, w_contract, bias_contract = params
    normed = low(layer_norm(inputs, gain_one, shift_one))
    bias_in = jnp.concatenate([bias_query, jnp.zeros_like(bias_query), bias_value])
    projected = low_back(low(matmul(normed, w_in) + bias_in))
    query = projected[:, :D].reshape(SEQ_LEN, HEADS, HD)
    keys = projected[:, D:2 * D].reshape(SEQ_LEN, HEADS, HD)
    values = projected[:, 2 * D:].reshape(SEQ_LEN, HEADS, HD)
    mixed = low_back(low(attend(query, keys, values, segment)))
    branch = low_back(matmul(mixed, w_out) + bias_attention)
    hidden = inputs + branch
    normed_two = low(layer_norm(hidden, gain_two, shift_two))
    expanded = low_back(matmul(normed_two, w_expand) + bias_expand)
    activated = low(jax.nn.gelu(expanded, approximate=True))
    return hidden + matmul(activated, w_contract) + bias_contract

def reference(tokens, placement_order, group_lengths, first_gain, first_shift, attention_in, query_bias, value_bias, attention_out, attention_bias, second_gain, second_shift, expand_weight, expand_bias, contract_weight, contract_bias, cotangent):
    lengths = group_lengths[placement_order]
    positions = jnp.arange(SEQ_LEN, dtype=jnp.int32)
    first_end = lengths[:, 0:1]
    second_end = first_end + lengths[:, 1:2]
    segment = (positions[None, :] >= first_end).astype(jnp.int32) + (positions[None, :] >= second_end).astype(jnp.int32)
    params = tuple((item.astype(jnp.float32) for item in (first_gain, first_shift, attention_in, query_bias, value_bias, attention_out, attention_bias, second_gain, second_shift, expand_weight, expand_bias, contract_weight, contract_bias)))

    def forward(inputs, weights):

        def one_group(pair):
            return group_forward(pair[0], pair[1], weights)
        return lax.map(jax.checkpoint(one_group), (inputs, segment))
    result, pull = jax.vjp(forward, tokens.astype(jnp.float32), params)
    grad_in, grads = pull(cotangent.astype(jnp.float32))
    return (result.astype(jnp.bfloat16), grad_in.astype(jnp.bfloat16), grads[0], grads[1], grads[2], grads[3], grads[4], grads[5], grads[6], grads[7], grads[8], grads[9], grads[10], grads[11], grads[12])
```

```python
import math

import jax
import jax.numpy as jnp
from jax import lax
from jax.experimental import pallas as pl
from jax.experimental.pallas import tpu as pltpu
from jax.sharding import PartitionSpec as P

HD = 64


norm_eps = 1e-05


def layer_norm(values, gain, shift):
    mean = jnp.mean(values, axis=-1, keepdims=True)
    centred = values - mean
    variance = jnp.mean(centred * centred, axis=-1, keepdims=True)
    return centred * lax.rsqrt(variance + norm_eps) * gain + shift


def gelu_tanh(values):
    return jax.nn.gelu(values, approximate=True)


def masked_scores(query_blk, keys, start, segment, scale):
    count = query_blk.shape[0]
    scores = jnp.einsum("qhd,khd->hqk", query_blk, keys, preferred_element_type=jnp.float32) * scale
    query_pos = start + jnp.arange(count, dtype=jnp.int32)
    key_pos = jnp.arange(keys.shape[0], dtype=jnp.int32)
    query_seg = lax.dynamic_slice_in_dim(segment, start, count, 0)
    allowed = (key_pos[None, :] <= query_pos[:, None]) & (
        (segment[None, :] == query_seg[:, None]) | (segment[None, :] == 0)
    )
    return jnp.where(allowed[None], scores, -1e30)


def forward_heads(query, keys, values, segment, block, scale):
    starts = jnp.arange(query.shape[0] // block, dtype=jnp.int32) * block

    def forward_one_block(start):
        query_blk = lax.dynamic_slice_in_dim(query, start, block, 0)
        scores = masked_scores(query_blk, keys, start, segment, scale)
        top = jnp.max(scores, axis=-1, keepdims=True)
        raised = jnp.exp(scores - top)
        total = jnp.sum(raised, axis=-1, keepdims=True)
        weights = (raised / total).astype(jnp.bfloat16)
        mixed = jnp.einsum("hqk,khd->qhd", weights, values, preferred_element_type=jnp.float32)
        return (mixed.astype(jnp.bfloat16), (top + jnp.log(total))[..., 0])

    return lax.map(forward_one_block, starts)


def backward_heads(query, keys, values, segment, log_total, grad_out, block, scale):
    count = query.shape[0] // block
    starts = jnp.arange(count, dtype=jnp.int32) * block
    grad_blocks = grad_out.reshape((count, block) + grad_out.shape[1:])

    def backward_one_block(carry, inputs):
        grad_keys, grad_values = carry
        start, total_blk, grad_blk = inputs
        query_blk = lax.dynamic_slice_in_dim(query, start, block, 0)
        scores = masked_scores(query_blk, keys, start, segment, scale)
        probs = jnp.exp(scores - total_blk[:, :, None])
        grad_probs = jnp.einsum(
            "qhd,khd->hqk", grad_blk, values, preferred_element_type=jnp.float32
        )
        inner = jnp.sum(probs * grad_probs, axis=-1, keepdims=True)
        grad_scores = (probs * (grad_probs - inner)).astype(jnp.bfloat16)
        grad_query = (
            jnp.einsum("hqk,khd->qhd", grad_scores, keys, preferred_element_type=jnp.float32)
            * scale
        )
        grad_keys = (
            grad_keys
            + jnp.einsum("hqk,qhd->khd", grad_scores, query_blk, preferred_element_type=jnp.float32)
            * scale
        )
        grad_values = grad_values + jnp.einsum(
            "hqk,qhd->khd", probs.astype(jnp.bfloat16), grad_blk, preferred_element_type=jnp.float32
        )
        return ((grad_keys, grad_values), grad_query)

    zeros = jnp.zeros(keys.shape, jnp.float32)
    (grad_keys, grad_values), grad_query = lax.scan(
        backward_one_block, (zeros, zeros), (starts, log_total, grad_blocks)
    )
    return (grad_query.reshape(query.shape), grad_keys, grad_values)


def shards(
    tokens,
    placement_order,
    group_lengths,
    first_gain,
    first_shift,
    attention_in,
    query_bias,
    value_bias,
    attention_out,
    attention_bias,
    second_gain,
    second_shift,
    expand_weight,
    expand_bias,
    contract_weight,
    contract_bias,
    cotangent,
):
    batch, rows, width = tokens.shape
    seq_count = lax.axis_size("seq")
    seq_len = rows * seq_count
    block = min(512, seq_len)
    scale = 1.0 / math.sqrt(HD)
    gathered = (
        lax.all_gather(attention_in, "fsdp", axis=0, tiled=True),
        lax.all_gather(attention_out, "fsdp", axis=0, tiled=True),
        lax.all_gather(expand_weight, "fsdp", axis=0, tiled=True),
        lax.all_gather(contract_weight, "fsdp", axis=0, tiled=True),
        lax.all_gather(first_gain, "fsdp", axis=0, tiled=True),
        lax.all_gather(first_shift, "fsdp", axis=0, tiled=True),
        lax.all_gather(query_bias, "fsdp", axis=0, tiled=True),
        lax.all_gather(value_bias, "fsdp", axis=0, tiled=True),
        lax.all_gather(attention_bias, "fsdp", axis=0, tiled=True),
        lax.all_gather(second_gain, "fsdp", axis=0, tiled=True),
        lax.all_gather(second_shift, "fsdp", axis=0, tiled=True),
        lax.all_gather(expand_bias, "fsdp", axis=0, tiled=True),
        lax.all_gather(contract_bias, "fsdp", axis=0, tiled=True),
    )
    in_full, out_full, expand_full, contract_full = (
        gathered[0],
        gathered[1],
        gathered[2],
        gathered[3],
    )
    small = [item.astype(jnp.float32) for item in gathered[4:]]
    (
        gain_one,
        shift_one,
        bias_query,
        bias_value,
        bias_attention,
        gain_two,
        shift_two,
        bias_expand,
        bias_contract,
    ) = small
    groups = group_lengths.shape[0]
    picked = (placement_order[:, None] == jnp.arange(groups, dtype=jnp.int32)[None, :]).astype(
        jnp.int32
    )
    lengths = jnp.sum(picked[:, :, None] * group_lengths[None, :, :], axis=1)
    positions = jnp.arange(seq_len, dtype=jnp.int32)
    first_end = lengths[:, 0:1]
    second_end = first_end + lengths[:, 1:2]
    segment = (positions[None, :] >= first_end).astype(jnp.int32) + (
        positions[None, :] >= second_end
    ).astype(jnp.int32)
    tok_rows = tokens.reshape(batch * rows, width).astype(jnp.float32)
    normed, norm_one_pull = jax.vjp(layer_norm, tok_rows, gain_one, shift_one)
    normed_low = normed.astype(jnp.bfloat16)
    bias_in = jnp.concatenate([bias_query, jnp.zeros((width,), jnp.float32), bias_value])
    projected = (jnp.dot(normed_low, in_full, preferred_element_type=jnp.float32) + bias_in).astype(
        jnp.bfloat16
    )
    heads_in = lax.all_to_all(
        projected.reshape(batch, rows, 3, width), "seq", split_axis=3, concat_axis=1, tiled=True
    )
    head_cols = heads_in.shape[3]
    per_device = head_cols // HD
    mixed_list = []
    total_list = []
    for index in range(batch):
        query = heads_in[index, :, 0].reshape(seq_len, per_device, HD)
        keys = heads_in[index, :, 1].reshape(seq_len, per_device, HD)
        values = heads_in[index, :, 2].reshape(seq_len, per_device, HD)
        mixed_blocks, log_total = forward_heads(query, keys, values, segment[index], block, scale)
        mixed_list.append(mixed_blocks.reshape(seq_len, head_cols))
        total_list.append(log_total)
    mixed = lax.all_to_all(jnp.stack(mixed_list), "seq", split_axis=1, concat_axis=2, tiled=True)
    mixed_rows = mixed.reshape(batch * rows, width)
    hidden = (
        tok_rows
        + jnp.dot(mixed_rows, out_full, preferred_element_type=jnp.float32)
        + bias_attention
    )
    normed_two, norm_two_pull = jax.vjp(layer_norm, hidden, gain_two, shift_two)
    normed_two_low = normed_two.astype(jnp.bfloat16)
    expanded = (
        jnp.dot(normed_two_low, expand_full, preferred_element_type=jnp.float32) + bias_expand
    )
    activated, gelu_pull = jax.vjp(gelu_tanh, expanded)
    activated_low = activated.astype(jnp.bfloat16)
    result = (
        hidden
        + jnp.dot(activated_low, contract_full, preferred_element_type=jnp.float32)
        + bias_contract
    )
    layer_out = result.astype(jnp.bfloat16).reshape(batch, rows, width)
    grad_low = cotangent.reshape(batch * rows, width)
    grad_res = grad_low.astype(jnp.float32)
    grad_contract = jnp.dot(activated_low.T, grad_low, preferred_element_type=jnp.float32)
    grad_bias_contract = jnp.sum(grad_res, axis=0)
    (grad_expanded,) = gelu_pull(
        jnp.dot(grad_low, contract_full.T, preferred_element_type=jnp.float32)
    )
    grad_expanded_low = grad_expanded.astype(jnp.bfloat16)
    grad_expand = jnp.dot(normed_two_low.T, grad_expanded_low, preferred_element_type=jnp.float32)
    grad_bias_expand = jnp.sum(grad_expanded_low.astype(jnp.float32), axis=0)
    grad_hidden, grad_gain_two, grad_shift_two = norm_two_pull(
        jnp.dot(grad_expanded_low, expand_full.T, preferred_element_type=jnp.float32)
    )
    grad_hidden = grad_hidden + grad_res
    grad_branch_low = grad_hidden.astype(jnp.bfloat16)
    grad_out_proj = jnp.dot(mixed_rows.T, grad_branch_low, preferred_element_type=jnp.float32)
    grad_bias_attention = jnp.sum(grad_branch_low.astype(jnp.float32), axis=0)
    grad_mixed = jnp.dot(grad_branch_low, out_full.T, preferred_element_type=jnp.float32).astype(
        jnp.bfloat16
    )
    grad_heads = lax.all_to_all(
        grad_mixed.reshape(batch, rows, width), "seq", split_axis=2, concat_axis=1, tiled=True
    )
    grad_list = []
    for index in range(batch):
        query = heads_in[index, :, 0].reshape(seq_len, per_device, HD)
        keys = heads_in[index, :, 1].reshape(seq_len, per_device, HD)
        values = heads_in[index, :, 2].reshape(seq_len, per_device, HD)
        grad_out = grad_heads[index].reshape(seq_len, per_device, HD)
        grad_query, grad_keys, grad_values = backward_heads(
            query, keys, values, segment[index], total_list[index], grad_out, block, scale
        )
        stacked = jnp.stack(
            [
                grad_query.reshape(seq_len, head_cols),
                grad_keys.reshape(seq_len, head_cols),
                grad_values.reshape(seq_len, head_cols),
            ],
            axis=1,
        )
        grad_list.append(stacked.astype(jnp.bfloat16))
    grad_proj = lax.all_to_all(jnp.stack(grad_list), "seq", split_axis=1, concat_axis=3, tiled=True)
    grad_proj_rows = grad_proj.reshape(batch * rows, 3 * width)
    grad_in_proj = jnp.dot(normed_low.T, grad_proj_rows, preferred_element_type=jnp.float32)
    grad_proj_wide = grad_proj_rows.astype(jnp.float32)
    grad_bias_query = jnp.sum(grad_proj_wide[:, :width], axis=0)
    grad_bias_value = jnp.sum(grad_proj_wide[:, 2 * width :], axis=0)
    grad_tok, grad_gain_one, grad_shift_one = norm_one_pull(
        jnp.dot(grad_proj_rows, in_full.T, preferred_element_type=jnp.float32)
    )
    grad_tokens = (grad_tok + grad_hidden).astype(jnp.bfloat16).reshape(batch, rows, width)
    shares = (
        lax.psum_scatter(
            grad_in_proj.astype(jnp.bfloat16), "fsdp", scatter_dimension=0, tiled=True
        ).astype(jnp.float32),
        lax.psum_scatter(
            grad_out_proj.astype(jnp.bfloat16), "fsdp", scatter_dimension=0, tiled=True
        ).astype(jnp.float32),
        lax.psum_scatter(
            grad_expand.astype(jnp.bfloat16), "fsdp", scatter_dimension=0, tiled=True
        ).astype(jnp.float32),
        lax.psum_scatter(
            grad_contract.astype(jnp.bfloat16), "fsdp", scatter_dimension=0, tiled=True
        ).astype(jnp.float32),
        lax.psum_scatter(
            grad_gain_one.astype(jnp.bfloat16), "fsdp", scatter_dimension=0, tiled=True
        ).astype(jnp.float32),
        lax.psum_scatter(
            grad_shift_one.astype(jnp.bfloat16), "fsdp", scatter_dimension=0, tiled=True
        ).astype(jnp.float32),
        lax.psum_scatter(
            grad_bias_query.astype(jnp.bfloat16), "fsdp", scatter_dimension=0, tiled=True
        ).astype(jnp.float32),
        lax.psum_scatter(
            grad_bias_value.astype(jnp.bfloat16), "fsdp", scatter_dimension=0, tiled=True
        ).astype(jnp.float32),
        lax.psum_scatter(
            grad_bias_attention.astype(jnp.bfloat16), "fsdp", scatter_dimension=0, tiled=True
        ).astype(jnp.float32),
        lax.psum_scatter(
            grad_gain_two.astype(jnp.bfloat16), "fsdp", scatter_dimension=0, tiled=True
        ).astype(jnp.float32),
        lax.psum_scatter(
            grad_shift_two.astype(jnp.bfloat16), "fsdp", scatter_dimension=0, tiled=True
        ).astype(jnp.float32),
        lax.psum_scatter(
            grad_bias_expand.astype(jnp.bfloat16), "fsdp", scatter_dimension=0, tiled=True
        ).astype(jnp.float32),
        lax.psum_scatter(
            grad_bias_contract.astype(jnp.bfloat16), "fsdp", scatter_dimension=0, tiled=True
        ).astype(jnp.float32),
    )
    totals = (
        lax.psum(shares[0].astype(jnp.bfloat16), "seq").astype(jnp.float32),
        lax.psum(shares[1].astype(jnp.bfloat16), "seq").astype(jnp.float32),
        lax.psum(shares[2].astype(jnp.bfloat16), "seq").astype(jnp.float32),
        lax.psum(shares[3].astype(jnp.bfloat16), "seq").astype(jnp.float32),
        lax.psum(shares[4].astype(jnp.bfloat16), "seq").astype(jnp.float32),
        lax.psum(shares[5].astype(jnp.bfloat16), "seq").astype(jnp.float32),
        lax.psum(shares[6].astype(jnp.bfloat16), "seq").astype(jnp.float32),
        lax.psum(shares[7].astype(jnp.bfloat16), "seq").astype(jnp.float32),
        lax.psum(shares[8].astype(jnp.bfloat16), "seq").astype(jnp.float32),
        lax.psum(shares[9].astype(jnp.bfloat16), "seq").astype(jnp.float32),
        lax.psum(shares[10].astype(jnp.bfloat16), "seq").astype(jnp.float32),
        lax.psum(shares[11].astype(jnp.bfloat16), "seq").astype(jnp.float32),
        lax.psum(shares[12].astype(jnp.bfloat16), "seq").astype(jnp.float32),
    )
    return (
        layer_out,
        grad_tokens,
        totals[4],
        totals[5],
        totals[0],
        totals[6],
        totals[7],
        totals[1],
        totals[8],
        totals[9],
        totals[10],
        totals[2],
        totals[11],
        totals[3],
        totals[12],
    )


MESH = pl.DeviceIdType.MESH
BF = jnp.bfloat16
F32 = jnp.float32
NEG = -1e30
GELU_A = math.sqrt(2.0 / math.pi)
GELU_B = 0.044715


def dot_nn(a, b):
    return lax.dot_general(a, b, (((1,), (0,)), ((), ())), preferred_element_type=F32)


def dot_nt(a, b):
    return lax.dot_general(a, b, (((1,), (1,)), ((), ())), preferred_element_type=F32)


def dot_tn(a, b):
    return lax.dot_general(a, b, (((0,), (0,)), ((), ())), preferred_element_type=F32)


def normalize(v):
    mean = jnp.mean(v, axis=-1, keepdims=True)
    centred = v - mean
    var = jnp.mean(centred * centred, axis=-1, keepdims=True)
    rstd = lax.rsqrt(var + norm_eps)
    return centred * rstd, rstd


def normalize_back(grad, gain, hat, rstd):
    g = grad * gain
    return rstd * (
        g
        - jnp.mean(g, axis=-1, keepdims=True)
        - hat * jnp.mean(g * hat, axis=-1, keepdims=True)
    )


def col_sum(v):
    return jnp.sum(v, axis=0, keepdims=True)


def layer_kernel(
    po, gl, tok, cot, win, wout, wexp, wcon, small,
    lo, gt, g_in, g_out, g_e, g_c, g_sm,
    wi_a, wo_a, we_a, wc_a, sm_a, vec, ebv, lane_mask,
    x_a, e_a, a_a, qkv, bias, p0, p1, p2, p3, o_a, h_own, b_a, g_a, du_a,
    part, db, part_r, db_r, dr_a, dh_own, do_a, dd, acc_k, acc_v, stage,
    vec_g, eb_g,
    st_c, st_e, st_o, st_i, st_s,
    ry_c, ry_e, ry_o, ry_i, ry_s,
    zb_c, zb_e, zb_o, zb_i, zb_s,
    rz_c, rz_e, rz_o, rz_i, rz_s,
    xb_c, xb_e, xb_o, xb_i, xb_s,
    rx_c, rx_e, rx_o, rx_i, rx_s,
    fc_c, fc_e, fc_o, fc_i, fc_s,
    rc_c, rc_e, rc_o, rc_i, rc_s,
    ag_s, ag_r, tk_s, tk_r, loc, ex_s, ex_r, rs_s, rs_r, out_s, out_r,
):
    f = lax.axis_index("fsdp")
    s = lax.axis_index("seq")
    z = f // 2
    y = f % 2
    x = s // 2
    c = s % 2
    dev_y = (z * 2 + 1 - y, s)
    dev_x = (f, (1 - x) * 2 + c)
    dev_c = (f, x * 2 + 1 - c)
    chunks, rows, width = x_a.shape
    length = chunks * rows

    def dev_z(zo):
        return (zo * 2 + y, s)

    def rcopy(src, dst, ssem, rsem, dev):
        return pltpu.make_async_remote_copy(
            src_ref=src, dst_ref=dst, send_sem=ssem, recv_sem=rsem, device_id=dev, device_id_type=MESH
        )

    barrier = pltpu.get_barrier_semaphore()
    for dev in (dev_z((z + 1) % 4), dev_z((z + 2) % 4), dev_z((z + 3) % 4), dev_y, dev_x, dev_c):
        pl.semaphore_signal(barrier, inc=1, device_id=dev, device_id_type=MESH)

    for pr in range(2):
        for part_i in range(3):
            col = pl.multiple_of(part_i * width + c * 256 + pr * 128, 128)
            dst = pr * 384 + part_i * 128
            wi_a[f, :, dst : dst + 128] = win[:, pl.ds(col, 128)]
    wo_a[f] = wout[...]
    for ff in range(8):
        col = pl.multiple_of(ff * 256 + c * 128, 128)
        we_a[f, :, ff * 128 : ff * 128 + 128] = wexp[:, pl.ds(col, 128)]
    wc_a[f] = wcon[pl.ds(pl.multiple_of(c * 128, 128), 128), :]
    sm_a[f] = small[...]
    pl.semaphore_wait(barrier, 6)

    gathered = (wi_a, sm_a, wo_a, we_a, wc_a)

    def ag_copy(g, origin, sem, dev):
        ref = gathered[g]
        return rcopy(ref.at[origin], ref.at[origin], ag_s.at[g, sem], ag_r.at[g, origin], dev)

    def ag_start(g):
        for d in range(1, 4):
            ag_copy(g, f, d - 1, dev_z((z + d) % 4)).start()
        ag_copy(g, f, 3, dev_y).start()

    def ag_forward(g):
        for d in range(1, 4):
            origin = ((z + d) % 4) * 2 + y
            cp = ag_copy(g, origin, 3 + d, dev_y)
            cp.wait_recv()
            cp.start()

    def ag_finish(g):
        for zo in range(4):
            ag_copy(g, zo * 2 + 1 - y, 3, dev_y).wait_recv()

    def ag_drain(g):
        for i in range(7):
            ag_copy(g, f, i, dev_y).wait_send()

    def swap_start(n, src, ref):
        pltpu.make_async_copy(src.at[x], ref.at[s], loc.at[n]).start()
        rcopy(src.at[1 - x], ref.at[s], tk_s.at[n, 0], tk_r.at[n, 0], dev_x).start()
        rcopy(src.at[x], ref.at[s], tk_s.at[n, 1], tk_r.at[n, 1], dev_c).start()

    def swap_forward(n, src, ref):
        k = (1 - x) * 2 + c
        rcopy(src.at[1 - x], ref.at[k], tk_s.at[n, 0], tk_r.at[n, 0], dev_x).wait_recv()
        rcopy(ref.at[k], ref.at[k], tk_s.at[n, 2], tk_r.at[n, 2], dev_c).start()

    def swap_finish(n, src, ref):
        pltpu.make_async_copy(src.at[x], ref.at[s], loc.at[n]).wait()
        k = s
        rcopy(src.at[x], ref.at[k], tk_s.at[n, 1], tk_r.at[n, 1], dev_c).wait_recv()
        rcopy(ref.at[k], ref.at[k], tk_s.at[n, 2], tk_r.at[n, 2], dev_c).wait_recv()

    def swap_drain(n, src, ref):
        rcopy(src.at[1 - x], ref.at[s], tk_s.at[n, 0], tk_r.at[n, 0], dev_x).wait_send()
        rcopy(src.at[x], ref.at[s], tk_s.at[n, 1], tk_r.at[n, 1], dev_c).wait_send()
        rcopy(ref.at[s], ref.at[s], tk_s.at[n, 2], tk_r.at[n, 2], dev_c).wait_send()

    ag_start(1)
    ag_start(0)
    swap_start(0, tok, x_a)
    for g in (2, 3, 4):
        ag_start(g)
    swap_start(1, cot, e_a)

    group = po[x]
    first_end = gl[group, 0]
    second_end = first_end + gl[group, 1]

    def mask_block(k, carry):
        qp = k * rows + lax.broadcasted_iota(jnp.int32, (rows, length), 0)
        kp = lax.broadcasted_iota(jnp.int32, (rows, length), 1)
        hidden_key = (kp >= first_end) & (kp < second_end) & (qp >= second_end)
        bad = (kp > qp) | hidden_key
        bias[k] = jnp.where(bad, NEG, 0.0).astype(F32)
        return carry

    lax.fori_loop(0, chunks, mask_block, 0)
    lanes = lax.broadcasted_iota(jnp.int32, (8, 128), 1)
    lane_row = lax.broadcasted_iota(jnp.int32, (8, 128), 0)
    lane_mask[...] = jnp.where((lanes < 64) == (lane_row < 1), 1.0, 0.0).astype(F32)
    vec_g[...] = jnp.zeros_like(vec_g)
    eb_g[...] = jnp.zeros_like(eb_g)

    ag_forward(1)
    swap_forward(0, tok, x_a)
    ag_forward(0)
    ag_finish(1)
    for r in range(4):
        low_half = sm_a[2 * r, 0:8, :]
        high_half = pltpu.roll(sm_a[2 * r + 1, 0:8, :], 64, 1)
        vec[:, r * 128 : r * 128 + 128] = jnp.where(lanes < 64, low_half, high_half)
    for ff in range(8):
        ebv[:, ff * 128 : ff * 128 + 128] = sm_a[ff, pl.ds(8 + c, 1), :]
    swap_finish(0, tok, x_a)

    def norm_one(k, carry):
        hat, _ = normalize(x_a[k].astype(F32))
        a_a[k] = (hat * vec[0:1, :] + vec[1:2, :]).astype(BF)
        return carry

    lax.fori_loop(0, chunks, norm_one, 0)
    ag_finish(0)

    def project(k, carry):
        row0 = pl.multiple_of(k * rows, rows)
        for pr in range(2):
            w = wi_a[:, :, pr * 384 : pr * 384 + 384].reshape(width, 384)
            out = dot_nn(a_a[k], w)
            col = pl.multiple_of(c * 256 + pr * 128, 128)
            qkv[pr, pl.ds(row0, rows), 0:128] = (out[:, 0:128] + vec[2:3, pl.ds(col, 128)]).astype(BF)
            qkv[pr, pl.ds(row0, rows), 128:256] = out[:, 128:256].astype(BF)
            qkv[pr, pl.ds(row0, rows), 256:384] = (out[:, 256:384] + vec[3:4, pl.ds(col, 128)]).astype(BF)
        return carry

    lax.fori_loop(0, chunks, project, 0)

    probs = (p0, p1, p2, p3)
    masks = [lane_mask[i : i + 1, :] for i in range(2)]
    masks_low = [m.astype(BF) for m in masks]
    scaled_low = [(m * 0.125).astype(BF) for m in masks]

    def attend_pair(pr, carry):
        for i in range(chunks):
            span = (i + 1) * rows
            q = qkv[pr, i * rows : i * rows + rows, 0:128]
            k = qkv[pr, 0:span, 128:256]
            v = qkv[pr, 0:span, 256:384]
            mixed = []
            for hh in range(2):
                sc = dot_nt(q * scaled_low[hh], k) + bias[i, :, 0:span]
                top = jnp.max(sc, axis=-1, keepdims=True)
                ex = jnp.exp(sc - top)
                tot = jnp.sum(ex, axis=-1, keepdims=True)
                pb = (ex * (1.0 / tot)).astype(BF)
                probs[i][pr, hh] = pb
                mixed.append(dot_nn(pb, v) * masks[hh])
            col = pl.multiple_of(c * 256 + pr * 128, 128)
            o_a[i, :, pl.ds(col, 128)] = (mixed[0] + mixed[1]).astype(BF)
        return carry

    def o_copy(pr):
        col = pl.multiple_of(c * 256 + pr * 128, 128)
        ref = o_a.at[:, :, pl.ds(col, 128)]
        return rcopy(ref, ref, ex_s.at[pr], ex_r.at[pr], dev_c)

    attend_pair(0, 0)
    o_copy(0).start()
    ag_forward(2)
    ag_forward(3)
    swap_forward(1, cot, e_a)
    attend_pair(1, 0)
    o_copy(1).start()
    ag_forward(4)
    ag_finish(2)
    for pr in range(2):
        o_copy(pr).wait_recv()

    def b_copy(j):
        ref = b_a.at[c + 2 * j]
        return rcopy(ref, ref, ex_s.at[2 + j], ex_r.at[2 + j], dev_c)

    for j in range(2):
        k = c + 2 * j
        out = dot_nn(o_a[k], wo_a[...].reshape(width, width))
        h = x_a[k].astype(F32) + out + vec[4:5, :]
        h_own[j] = h
        hat, _ = normalize(h)
        b_a[k] = (hat * vec[5:6, :] + vec[6:7, :]).astype(BF)
        b_copy(j).start()
    swap_finish(1, cot, e_a)
    ag_finish(3)
    ag_finish(4)
    we_full = lambda: we_a[...].reshape(width, we_a.shape[2])
    wc_full = lambda: wc_a[...].reshape(we_a.shape[2], width)

    def mlp_chunk(j, k):
        u = dot_nn(b_a[k], we_full()) + ebv[...]
        u2 = u * u
        th = jnp.tanh(GELU_A * (u + GELU_B * (u2 * u)))
        half = 0.5 * (1.0 + th)
        g = (u * half).astype(BF)
        g_a[k] = g
        slope = half + (0.5 * GELU_A) * u * (1.0 - th * th) * (1.0 + (3.0 * GELU_B) * u2)
        du = (slope * dot_nt(e_a[k], wc_full())).astype(BF)
        du_a[k] = du
        eb_g[...] += col_sum(du.astype(F32))
        part[j] = dot_nn(g, wc_full())
        db[j] = dot_nt(du, we_full())

    def part_copy(j):
        return rcopy(part.at[j], part_r.at[j - 2], ex_s.at[4 + j - 2], ex_r.at[4 + j - 2], dev_c)

    def db_copy(j):
        return rcopy(db.at[j], db_r.at[j - 2], ex_s.at[6 + j - 2], ex_r.at[6 + j - 2], dev_c)

    def mlp_own(j, carry):
        mlp_chunk(j, c + 2 * j)
        return carry

    lax.fori_loop(0, 2, mlp_own, 0)
    for j in range(2):
        ref = b_a.at[1 - c + 2 * j]
        rcopy(ref, ref, ex_s.at[2 + j], ex_r.at[2 + j], dev_c).wait_recv()
    for j in range(2, 4):
        mlp_chunk(j, (1 - c) + 2 * (j - 2))
        part_copy(j).start()
        db_copy(j).start()

    def grad_con(r, carry):
        col = pl.multiple_of(r * 256, 256)
        out = dot_tn(g_a[:, :, pl.ds(col, 256)].reshape(length, 256), e_a[...].reshape(length, width))
        st_c[0, r] = out[0:128].astype(BF)
        st_c[1, r] = out[128:256].astype(BF)
        return carry

    lax.fori_loop(0, 4, grad_con, 0)

    def rs_names(g):
        return (
            (st_c, ry_c, zb_c, rz_c, xb_c, rx_c, fc_c, rc_c),
            (st_e, ry_e, zb_e, rz_e, xb_e, rx_e, fc_e, rc_e),
            (st_o, ry_o, zb_o, rz_o, xb_o, rx_o, fc_o, rc_o),
            tuple(r.at[0] for r in (st_i, ry_i, zb_i, rz_i, xb_i, rx_i, fc_i, rc_i)),
            tuple(r.at[1] for r in (st_i, ry_i, zb_i, rz_i, xb_i, rx_i, fc_i, rc_i)),
            (st_s, ry_s, zb_s, rz_s, xb_s, rx_s, fc_s, rc_s),
        )[g]

    def rs_y(g):
        st, ry = rs_names(g)[:2]
        return rcopy(st.at[1 - y], ry, rs_s.at[g, 0], rs_r.at[g, 4], dev_y)

    def rs_z(g, d):
        zb, rz = rs_names(g)[2:4]
        zo = (z + d) % 4
        return rcopy(zb.at[zo], rz.at[z], rs_s.at[g, d], rs_r.at[g, z], dev_z(zo))

    def rs_x(g):
        xb, rx = rs_names(g)[4:6]
        return rcopy(xb, rx, rs_s.at[g, 4], rs_r.at[g, 5], dev_x)

    def rs_c(g):
        fc, rc = rs_names(g)[6:8]
        return rcopy(fc, rc, rs_s.at[g, 5], rs_r.at[g, 6], dev_c)

    def rs_z_start(g):
        st, ry, zb = rs_names(g)[:3]
        rs_y(g).wait_recv()
        for d in range(1, 4):
            zo = (z + d) % 4
            zb[zo] = (st[y, zo].astype(F32) + ry[zo].astype(F32)).astype(zb.dtype)
            rs_z(g, d).start()

    def rs_x_start(g):
        st, ry, zb, rz, xb = rs_names(g)[:5]
        total = st[y, z].astype(F32) + ry[z].astype(F32)
        for d in range(1, 4):
            zo = (z + d) % 4
            rcopy(zb.at[zo], rz.at[zo], rs_s.at[g, d], rs_r.at[g, zo], dev_z(zo)).wait_recv()
            total = total + rz[zo].astype(F32)
        xb[...] = total.astype(xb.dtype)
        rs_x(g).start()

    def write_out(g, side, value):
        if g == 0:
            g_c[pl.ds(pl.multiple_of(side * 128, 128), 128), :] = value
        elif g == 1:
            for ff in range(8):
                col = pl.multiple_of(ff * 256 + side * 128, 128)
                g_e[:, pl.ds(col, 128)] = value[:, ff * 128 : ff * 128 + 128]
        elif g == 2:
            g_out[:, pl.ds(pl.multiple_of(side * 256, 256), 256)] = value
        else:
            for part_i in range(3):
                col = pl.multiple_of(part_i * width + side * 256 + (g - 3) * 128, 128)
                g_in[:, pl.ds(col, 128)] = value[:, part_i * 128 : part_i * 128 + 128]

    def rs_c_start(g):
        xb, rx, fc = rs_names(g)[4:7]
        rs_x(g).wait_recv()
        fc[...] = xb[...].astype(F32) + rx[...].astype(F32)
        rs_c(g).start()
        if g < 5:
            write_out(g, c, fc[...])

    def rs_finish(g):
        fc, rc = rs_names(g)[6:8]
        rs_c(g).wait_recv()
        if g < 5:
            write_out(g, 1 - c, rc[...])
        else:
            g_sm[...] = fc[...] + rc[...]

    def rs_drain(g):
        rs_y(g).wait_send()
        for d in range(1, 4):
            rs_z(g, d).wait_send()
        rs_x(g).wait_send()
        rs_c(g).wait_send()

    rs_y(0).start()

    def grad_exp(r, carry):
        col = pl.multiple_of(r * 512, 512)
        out = dot_tn(b_a[...].reshape(length, width), du_a[:, :, pl.ds(col, 512)].reshape(length, 512))
        for ff in range(8):
            st_e[ff % 2, ff // 2, :, pl.ds(col, 512)] = out[ff * 64 : ff * 64 + 64].astype(BF)
        return carry

    lax.fori_loop(0, we_a.shape[2] // 512, grad_exp, 0)
    rs_y(1).start()

    def send_rows(n, ref, out):
        k_far = (1 - x) * 2 + c
        far = rcopy(stage.at[n, 1 - x], out.at[x], out_s.at[n, 0], out_r.at[n], dev_x)
        near = pltpu.make_async_copy(stage.at[n, x], out.at[x], out_s.at[n, 1])
        return far, near

    def dr_copy(j):
        ref = dr_a.at[c + 2 * j]
        return rcopy(ref, ref, ex_s.at[8 + j], ex_r.at[8 + j], dev_c)

    for j in range(2):
        k = c + 2 * j
        h = h_own[j]
        e = e_a[k].astype(F32)
        rcopy(db.at[j + 2], db_r.at[j], ex_s.at[6 + j], ex_r.at[6 + j], dev_c).wait_recv()
        grad_b = db[j] + db_r[j]
        hat, rstd = normalize(h)
        dh = e + normalize_back(grad_b, vec[5:6, :], hat, rstd)
        dh_own[j] = dh
        dr = dh.astype(BF)
        dr_a[k] = dr
        dr_copy(j).start()
        vec_g[4:5, :] += col_sum(dr.astype(F32))
        vec_g[5:6, :] += col_sum(grad_b * hat)
        vec_g[6:7, :] += col_sum(grad_b)
        vec_g[7:8, :] += col_sum(e)
        rcopy(part.at[j + 2], part_r.at[j], ex_s.at[4 + j], ex_r.at[4 + j], dev_c).wait_recv()
        stage[0, j] = (h + part[j] + part_r[j] + vec[7:8, :]).astype(BF)
    for cp in send_rows(0, stage, lo):
        cp.start()
    rs_z_start(0)

    head_row = pl.multiple_of(c * 4, 4)

    def grad_mixed(k):
        w = wo_a[pl.ds(head_row, 4)].reshape(256, width)
        do_a[k] = dot_nt(dr_a[k], w).astype(BF)

    for j in range(2):
        grad_mixed(c + 2 * j)
    for j in range(2):
        ref = dr_a.at[1 - c + 2 * j]
        rcopy(ref, ref, ex_s.at[8 + j], ex_r.at[8 + j], dev_c).wait_recv()
        grad_mixed(1 - c + 2 * j)
    rs_z_start(1)
    col_c = pl.multiple_of(c * 256, 256)
    out = dot_tn(o_a[...].reshape(length, width), dr_a[:, :, pl.ds(col_c, 256)].reshape(length, 256))
    for ff in range(8):
        st_o[ff % 2, ff // 2] = out[ff * 64 : ff * 64 + 64].astype(BF)
    rs_y(2).start()

    def attend_back(pr, carry):
        acc_k[...] = jnp.zeros_like(acc_k)
        acc_v[...] = jnp.zeros_like(acc_v)
        for i in range(chunks):
            span = (i + 1) * rows
            q = qkv[pr, i * rows : i * rows + rows, 0:128]
            k = qkv[pr, 0:span, 128:256]
            v = qkv[pr, 0:span, 256:384]
            do = do_a[i, :, pr * 128 : pr * 128 + 128]
            grad_q = None
            for hh in range(2):
                dom = do * masks_low[hh]
                pb = probs[i][pr, hh]
                pf = pb.astype(F32)
                t = pf * dot_nt(dom, v)
                inner = jnp.sum(t, axis=-1, keepdims=True)
                ds = (t - pf * inner).astype(BF)
                acc_v[0:span] += dot_tn(pb, dom)
                acc_k[0:span] += dot_tn(ds, q * scaled_low[hh])
                gq = dot_nn(ds, k * scaled_low[hh])
                grad_q = gq if grad_q is None else grad_q + gq
            dd[pr, i * rows : i * rows + rows, 0:128] = grad_q.astype(BF)
        dd[pr, :, 128:256] = acc_k[...].astype(BF)
        dd[pr, :, 256:384] = acc_v[...].astype(BF)
        col = pl.multiple_of(c * 256 + pr * 128, 128)
        vec_g[2:3, pl.ds(col, 128)] = col_sum(dd[pr, :, 0:128].astype(F32))
        vec_g[3:4, pl.ds(col, 128)] = col_sum(dd[pr, :, 256:384].astype(F32))
        return carry

    def grad_in(pr):
        out = dot_tn(a_a[...].reshape(length, width), dd[pr])
        for ff in range(8):
            st_i[pr, ff % 2, ff // 2] = out[ff * 64 : ff * 64 + 64].astype(BF)
        rs_y(3 + pr).start()

    attend_back(0, 0)
    grad_in(0)
    rs_x_start(0)
    rs_x_start(1)
    rs_z_start(2)
    attend_back(1, 0)
    rs_c_start(0)
    rs_c_start(1)
    rs_z_start(3)

    for j in range(2, 4):
        part_copy(j).wait_send()

    def grad_a(k):
        row0 = pl.multiple_of(k * rows, rows)
        total = None
        for pr in range(2):
            w = wi_a[:, :, pr * 384 : pr * 384 + 384].reshape(width, 384)
            p = dot_nt(dd[pr, pl.ds(row0, rows), :], w)
            total = p if total is None else total + p
        return total

    def da_copy(j):
        return rcopy(part.at[j], db_r.at[j - 2], ex_s.at[10 + j - 2], ex_r.at[10 + j - 2], dev_c)

    for j in range(2, 4):
        part[j] = grad_a((1 - c) + 2 * (j - 2))
        da_copy(j).start()
    grad_in(1)
    for j in range(2):
        part[j] = grad_a(c + 2 * j)
    rs_x_start(2)
    for j in range(2):
        k = c + 2 * j
        rcopy(part.at[j + 2], db_r.at[j], ex_s.at[10 + j], ex_r.at[10 + j], dev_c).wait_recv()
        grad = part[j] + db_r[j]
        hat, rstd = normalize(x_a[k].astype(F32))
        vec_g[0:1, :] += col_sum(grad * hat)
        vec_g[1:2, :] += col_sum(grad)
        stage[1, j] = (dh_own[j] + normalize_back(grad, vec[0:1, :], hat, rstd)).astype(BF)
    for cp in send_rows(1, stage, gt):
        cp.start()

    for r in range(4):
        tile = vec_g[:, r * 128 : r * 128 + 128]
        rolled = pltpu.roll(tile, 64, 1)
        for yy in range(2):
            st_s[yy, r, 0:8, :] = tile if yy == 0 else rolled
            st_s[yy, r, 8:16, :] = jnp.zeros((8, 128), F32)
            ff = 2 * r + yy
            st_s[yy, r, pl.ds(8 + c, 1), :] = eb_g[:, ff * 128 : ff * 128 + 128]
    rs_y(5).start()
    rs_z_start(4)
    rs_z_start(5)
    rs_x_start(3)
    rs_c_start(2)
    rs_c_start(3)
    for g in range(3):
        rs_finish(g)
    rs_x_start(4)
    rs_x_start(5)
    rs_c_start(4)
    rs_c_start(5)
    for g in range(3, 6):
        rs_finish(g)
    for n, out in ((0, lo), (1, gt)):
        far, near = send_rows(n, stage, out)
        near.wait()
        far.wait_send()
        rcopy(stage.at[n, 1 - x], out.at[1 - x], out_s.at[n, 0], out_r.at[n], dev_x).wait_recv()
    for g in range(5):
        ag_drain(g)
    swap_drain(0, tok, x_a)
    swap_drain(1, cot, e_a)
    for pr in range(2):
        o_copy(pr).wait_send()
    for j in range(2):
        b_copy(j).wait_send()
        dr_copy(j).wait_send()
        db_copy(j + 2).wait_send()
        da_copy(j + 2).wait_send()
    for g in range(6):
        rs_drain(g)


def fast_shards(
    tokens, placement_order, group_lengths, first_gain, first_shift, attention_in, query_bias,
    value_bias, attention_out, attention_bias, second_gain, second_shift, expand_weight,
    expand_bias, contract_weight, contract_bias, cotangent,
):
    batch, rows, width = tokens.shape
    lanes = first_gain.shape[0]
    vectors = (
        first_gain, first_shift, query_bias, value_bias, attention_bias, second_gain,
        second_shift, contract_bias,
    )
    stacked = jnp.pad(jnp.stack(vectors), ((0, 0), (0, 128 - lanes)))
    small = jnp.concatenate(
        [stacked, expand_bias.reshape(2, 128), jnp.zeros((6, 128), BF)], axis=0
    ).astype(F32)
    chunks = 4
    length = chunks * rows
    ff = expand_weight.shape[1] // 2
    vm = pl.BlockSpec(memory_space=pltpu.VMEM)
    sm = pl.BlockSpec(memory_space=pltpu.SMEM)
    hb = pl.BlockSpec(memory_space=pl.ANY)
    V = pltpu.VMEM

    def rs_scratch(lead, shape, pairs=None):
        pre = () if pairs is None else (pairs,)
        return V(pre + lead + shape, BF)

    pieces = (((128, width), None), ((64, ff), None), ((64, 256), None), ((64, 384), 2))

    def family(lead, dtype):
        out = []
        for shape, pairs in pieces:
            pre = () if pairs is None else (pairs,)
            out.append(V(pre + lead + shape, dtype))
        out.append(V(lead + (16, 128), F32))
        return out

    dma = pltpu.SemaphoreType.DMA
    scratch = [
        V((8, 64, 768), BF), V((8, 64, width), BF), V((8, 64, ff), BF), V((8, 128, width), BF),
        V((8, 16, 128), F32), V((8, width), F32), V((1, ff), F32), V((8, 128), F32),
        V((chunks, rows, width), BF), V((chunks, rows, width), BF), V((chunks, rows, width), BF),
        V((2, length, 384), BF), V((chunks, rows, length), F32),
        V((2, 2, rows, rows), BF), V((2, 2, rows, 2 * rows), BF), V((2, 2, rows, 3 * rows), BF),
        V((2, 2, rows, 4 * rows), BF),
        V((chunks, rows, width), BF), V((2, rows, width), F32), V((chunks, rows, width), BF),
        V((chunks, rows, ff), BF), V((chunks, rows, ff), BF),
        V((4, rows, width), F32), V((4, rows, width), F32), V((2, rows, width), F32),
        V((2, rows, width), F32), V((chunks, rows, width), BF), V((2, rows, width), F32),
        V((chunks, rows, 256), BF), V((2, length, 384), BF), V((length, 128), F32),
        V((length, 128), F32), V((2, 2, rows, width), BF), V((8, width), F32), V((1, ff), F32),
    ]
    scratch += family((2, 4), BF) + family((4,), BF) + family((4,), BF) + family((4,), BF)
    scratch += family((), BF) + family((), BF) + family((), F32) + family((), F32)
    scratch += [
        dma((5, 7)), dma((5, 8)), dma((2, 3)), dma((2, 3)), dma((2,)), dma((12,)), dma((12,)),
        dma((6, 6)), dma((6, 7)), dma((2, 2)), dma((2,)),
    ]
    outs = pl.pallas_call(
        layer_kernel,
        out_shape=(
            jax.ShapeDtypeStruct(tokens.shape, BF),
            jax.ShapeDtypeStruct(tokens.shape, BF),
            jax.ShapeDtypeStruct(attention_in.shape, F32),
            jax.ShapeDtypeStruct(attention_out.shape, F32),
            jax.ShapeDtypeStruct(expand_weight.shape, F32),
            jax.ShapeDtypeStruct(contract_weight.shape, F32),
            jax.ShapeDtypeStruct((16, 128), F32),
        ),
        in_specs=[sm, sm, hb, hb, vm, vm, vm, vm, vm],
        out_specs=[hb, hb, vm, vm, vm, vm, vm],
        scratch_shapes=scratch,
        compiler_params=pltpu.CompilerParams(
            collective_id=0, has_side_effects=True, vmem_limit_bytes=63 << 20
        ),
    )(
        placement_order, group_lengths, tokens, cotangent, attention_in, attention_out,
        expand_weight, contract_weight, small,
    )
    layer_out, grad_tokens, g_in, g_out, g_e, g_c, g_sm = outs
    rows_of = [g_sm[i, :lanes] for i in range(8)]
    return (
        layer_out, grad_tokens, rows_of[0], rows_of[1], g_in, rows_of[2], rows_of[3], g_out,
        rows_of[4], rows_of[5], rows_of[6], g_e, g_sm[8:10].reshape(-1), g_c, rows_of[7],
    )


def solution(mesh):
    in_specs = (
        P("fsdp", "seq", None),
        P("fsdp"),
        P(),
        P("fsdp"),
        P("fsdp"),
        P("fsdp", None),
        P("fsdp"),
        P("fsdp"),
        P("fsdp", None),
        P("fsdp"),
        P("fsdp"),
        P("fsdp"),
        P("fsdp", None),
        P("fsdp"),
        P("fsdp", None),
        P("fsdp"),
        P("fsdp", "seq", None),
    )
    out_specs = (
        P("fsdp", "seq", None),
        P("fsdp", "seq", None),
        P("fsdp"),
        P("fsdp"),
        P("fsdp", None),
        P("fsdp"),
        P("fsdp"),
        P("fsdp", None),
        P("fsdp"),
        P("fsdp"),
        P("fsdp"),
        P("fsdp", None),
        P("fsdp"),
        P("fsdp", None),
        P("fsdp"),
    )
    pick = fast_shards if (mesh.shape["fsdp"], mesh.shape["seq"]) == (8, 4) else shards
    return jax.shard_map(pick, mesh=mesh, in_specs=in_specs, out_specs=out_specs, check_vma=False)
```

```python
import math

import jax
import jax.numpy as jnp
from jax import lax
from jax.experimental import pallas as pl
from jax.experimental.pallas import tpu as pltpu
from jax.sharding import PartitionSpec as P

HD = 64


norm_eps = 1e-05


def layer_norm(values, gain, shift):
    mean = jnp.mean(values, axis=-1, keepdims=True)
    centred = values - mean
    variance = jnp.mean(centred * centred, axis=-1, keepdims=True)
    return centred * lax.rsqrt(variance + norm_eps) * gain + shift


def gelu_tanh(values):
    return jax.nn.gelu(values, approximate=True)


def masked_scores(query_blk, keys, start, segment, scale):
    count = query_blk.shape[0]
    scores = jnp.einsum("qhd,khd->hqk", query_blk, keys, preferred_element_type=jnp.float32) * scale
    query_pos = start + jnp.arange(count, dtype=jnp.int32)
    key_pos = jnp.arange(keys.shape[0], dtype=jnp.int32)
    query_seg = lax.dynamic_slice_in_dim(segment, start, count, 0)
    allowed = (key_pos[None, :] <= query_pos[:, None]) & (
        (segment[None, :] == query_seg[:, None]) | (segment[None, :] == 0)
    )
    return jnp.where(allowed[None], scores, -1e30)


def forward_heads(query, keys, values, segment, block, scale):
    starts = jnp.arange(query.shape[0] // block, dtype=jnp.int32) * block

    def forward_one_block(start):
        query_blk = lax.dynamic_slice_in_dim(query, start, block, 0)
        scores = masked_scores(query_blk, keys, start, segment, scale)
        top = jnp.max(scores, axis=-1, keepdims=True)
        raised = jnp.exp(scores - top)
        total = jnp.sum(raised, axis=-1, keepdims=True)
        weights = (raised / total).astype(jnp.bfloat16)
        mixed = jnp.einsum("hqk,khd->qhd", weights, values, preferred_element_type=jnp.float32)
        return (mixed.astype(jnp.bfloat16), (top + jnp.log(total))[..., 0])

    return lax.map(forward_one_block, starts)


def backward_heads(query, keys, values, segment, log_total, grad_out, block, scale):
    count = query.shape[0] // block
    starts = jnp.arange(count, dtype=jnp.int32) * block
    grad_blocks = grad_out.reshape((count, block) + grad_out.shape[1:])

    def backward_one_block(carry, inputs):
        grad_keys, grad_values = carry
        start, total_blk, grad_blk = inputs
        query_blk = lax.dynamic_slice_in_dim(query, start, block, 0)
        scores = masked_scores(query_blk, keys, start, segment, scale)
        probs = jnp.exp(scores - total_blk[:, :, None])
        grad_probs = jnp.einsum(
            "qhd,khd->hqk", grad_blk, values, preferred_element_type=jnp.float32
        )
        inner = jnp.sum(probs * grad_probs, axis=-1, keepdims=True)
        grad_scores = (probs * (grad_probs - inner)).astype(jnp.bfloat16)
        grad_query = (
            jnp.einsum("hqk,khd->qhd", grad_scores, keys, preferred_element_type=jnp.float32)
            * scale
        )
        grad_keys = (
            grad_keys
            + jnp.einsum("hqk,qhd->khd", grad_scores, query_blk, preferred_element_type=jnp.float32)
            * scale
        )
        grad_values = grad_values + jnp.einsum(
            "hqk,qhd->khd", probs.astype(jnp.bfloat16), grad_blk, preferred_element_type=jnp.float32
        )
        return ((grad_keys, grad_values), grad_query)

    zeros = jnp.zeros(keys.shape, jnp.float32)
    (grad_keys, grad_values), grad_query = lax.scan(
        backward_one_block, (zeros, zeros), (starts, log_total, grad_blocks)
    )
    return (grad_query.reshape(query.shape), grad_keys, grad_values)


def shards(
    tokens,
    placement_order,
    group_lengths,
    first_gain,
    first_shift,
    attention_in,
    query_bias,
    value_bias,
    attention_out,
    attention_bias,
    second_gain,
    second_shift,
    expand_weight,
    expand_bias,
    contract_weight,
    contract_bias,
    cotangent,
):
    batch, rows, width = tokens.shape
    seq_count = lax.axis_size("seq")
    seq_len = rows * seq_count
    block = min(512, seq_len)
    scale = 1.0 / math.sqrt(HD)
    gathered = (
        lax.all_gather(attention_in, "fsdp", axis=0, tiled=True),
        lax.all_gather(attention_out, "fsdp", axis=0, tiled=True),
        lax.all_gather(expand_weight, "fsdp", axis=0, tiled=True),
        lax.all_gather(contract_weight, "fsdp", axis=0, tiled=True),
        lax.all_gather(first_gain, "fsdp", axis=0, tiled=True),
        lax.all_gather(first_shift, "fsdp", axis=0, tiled=True),
        lax.all_gather(query_bias, "fsdp", axis=0, tiled=True),
        lax.all_gather(value_bias, "fsdp", axis=0, tiled=True),
        lax.all_gather(attention_bias, "fsdp", axis=0, tiled=True),
        lax.all_gather(second_gain, "fsdp", axis=0, tiled=True),
        lax.all_gather(second_shift, "fsdp", axis=0, tiled=True),
        lax.all_gather(expand_bias, "fsdp", axis=0, tiled=True),
        lax.all_gather(contract_bias, "fsdp", axis=0, tiled=True),
    )
    in_full, out_full, expand_full, contract_full = (
        gathered[0],
        gathered[1],
        gathered[2],
        gathered[3],
    )
    small = [item.astype(jnp.float32) for item in gathered[4:]]
    (
        gain_one,
        shift_one,
        bias_query,
        bias_value,
        bias_attention,
        gain_two,
        shift_two,
        bias_expand,
        bias_contract,
    ) = small
    groups = group_lengths.shape[0]
    picked = (placement_order[:, None] == jnp.arange(groups, dtype=jnp.int32)[None, :]).astype(
        jnp.int32
    )
    lengths = jnp.sum(picked[:, :, None] * group_lengths[None, :, :], axis=1)
    positions = jnp.arange(seq_len, dtype=jnp.int32)
    first_end = lengths[:, 0:1]
    second_end = first_end + lengths[:, 1:2]
    segment = (positions[None, :] >= first_end).astype(jnp.int32) + (
        positions[None, :] >= second_end
    ).astype(jnp.int32)
    tok_rows = tokens.reshape(batch * rows, width).astype(jnp.float32)
    normed, norm_one_pull = jax.vjp(layer_norm, tok_rows, gain_one, shift_one)
    normed_low = normed.astype(jnp.bfloat16)
    bias_in = jnp.concatenate([bias_query, jnp.zeros((width,), jnp.float32), bias_value])
    projected = (jnp.dot(normed_low, in_full, preferred_element_type=jnp.float32) + bias_in).astype(
        jnp.bfloat16
    )
    heads_in = lax.all_to_all(
        projected.reshape(batch, rows, 3, width), "seq", split_axis=3, concat_axis=1, tiled=True
    )
    head_cols = heads_in.shape[3]
    per_device = head_cols // HD
    mixed_list = []
    total_list = []
    for index in range(batch):
        query = heads_in[index, :, 0].reshape(seq_len, per_device, HD)
        keys = heads_in[index, :, 1].reshape(seq_len, per_device, HD)
        values = heads_in[index, :, 2].reshape(seq_len, per_device, HD)
        mixed_blocks, log_total = forward_heads(query, keys, values, segment[index], block, scale)
        mixed_list.append(mixed_blocks.reshape(seq_len, head_cols))
        total_list.append(log_total)
    mixed = lax.all_to_all(jnp.stack(mixed_list), "seq", split_axis=1, concat_axis=2, tiled=True)
    mixed_rows = mixed.reshape(batch * rows, width)
    hidden = (
        tok_rows
        + jnp.dot(mixed_rows, out_full, preferred_element_type=jnp.float32)
        + bias_attention
    )
    normed_two, norm_two_pull = jax.vjp(layer_norm, hidden, gain_two, shift_two)
    normed_two_low = normed_two.astype(jnp.bfloat16)
    expanded = (
        jnp.dot(normed_two_low, expand_full, preferred_element_type=jnp.float32) + bias_expand
    )
    activated, gelu_pull = jax.vjp(gelu_tanh, expanded)
    activated_low = activated.astype(jnp.bfloat16)
    result = (
        hidden
        + jnp.dot(activated_low, contract_full, preferred_element_type=jnp.float32)
        + bias_contract
    )
    layer_out = result.astype(jnp.bfloat16).reshape(batch, rows, width)
    grad_low = cotangent.reshape(batch * rows, width)
    grad_res = grad_low.astype(jnp.float32)
    grad_contract = jnp.dot(activated_low.T, grad_low, preferred_element_type=jnp.float32)
    grad_bias_contract = jnp.sum(grad_res, axis=0)
    (grad_expanded,) = gelu_pull(
        jnp.dot(grad_low, contract_full.T, preferred_element_type=jnp.float32)
    )
    grad_expanded_low = grad_expanded.astype(jnp.bfloat16)
    grad_expand = jnp.dot(normed_two_low.T, grad_expanded_low, preferred_element_type=jnp.float32)
    grad_bias_expand = jnp.sum(grad_expanded_low.astype(jnp.float32), axis=0)
    grad_hidden, grad_gain_two, grad_shift_two = norm_two_pull(
        jnp.dot(grad_expanded_low, expand_full.T, preferred_element_type=jnp.float32)
    )
    grad_hidden = grad_hidden + grad_res
    grad_branch_low = grad_hidden.astype(jnp.bfloat16)
    grad_out_proj = jnp.dot(mixed_rows.T, grad_branch_low, preferred_element_type=jnp.float32)
    grad_bias_attention = jnp.sum(grad_branch_low.astype(jnp.float32), axis=0)
    grad_mixed = jnp.dot(grad_branch_low, out_full.T, preferred_element_type=jnp.float32).astype(
        jnp.bfloat16
    )
    grad_heads = lax.all_to_all(
        grad_mixed.reshape(batch, rows, width), "seq", split_axis=2, concat_axis=1, tiled=True
    )
    grad_list = []
    for index in range(batch):
        query = heads_in[index, :, 0].reshape(seq_len, per_device, HD)
        keys = heads_in[index, :, 1].reshape(seq_len, per_device, HD)
        values = heads_in[index, :, 2].reshape(seq_len, per_device, HD)
        grad_out = grad_heads[index].reshape(seq_len, per_device, HD)
        grad_query, grad_keys, grad_values = backward_heads(
            query, keys, values, segment[index], total_list[index], grad_out, block, scale
        )
        stacked = jnp.stack(
            [
                grad_query.reshape(seq_len, head_cols),
                grad_keys.reshape(seq_len, head_cols),
                grad_values.reshape(seq_len, head_cols),
            ],
            axis=1,
        )
        grad_list.append(stacked.astype(jnp.bfloat16))
    grad_proj = lax.all_to_all(jnp.stack(grad_list), "seq", split_axis=1, concat_axis=3, tiled=True)
    grad_proj_rows = grad_proj.reshape(batch * rows, 3 * width)
    grad_in_proj = jnp.dot(normed_low.T, grad_proj_rows, preferred_element_type=jnp.float32)
    grad_proj_wide = grad_proj_rows.astype(jnp.float32)
    grad_bias_query = jnp.sum(grad_proj_wide[:, :width], axis=0)
    grad_bias_value = jnp.sum(grad_proj_wide[:, 2 * width :], axis=0)
    grad_tok, grad_gain_one, grad_shift_one = norm_one_pull(
        jnp.dot(grad_proj_rows, in_full.T, preferred_element_type=jnp.float32)
    )
    grad_tokens = (grad_tok + grad_hidden).astype(jnp.bfloat16).reshape(batch, rows, width)
    shares = (
        lax.psum_scatter(
            grad_in_proj.astype(jnp.bfloat16), "fsdp", scatter_dimension=0, tiled=True
        ).astype(jnp.float32),
        lax.psum_scatter(
            grad_out_proj.astype(jnp.bfloat16), "fsdp", scatter_dimension=0, tiled=True
        ).astype(jnp.float32),
        lax.psum_scatter(
            grad_expand.astype(jnp.bfloat16), "fsdp", scatter_dimension=0, tiled=True
        ).astype(jnp.float32),
        lax.psum_scatter(
            grad_contract.astype(jnp.bfloat16), "fsdp", scatter_dimension=0, tiled=True
        ).astype(jnp.float32),
        lax.psum_scatter(
            grad_gain_one.astype(jnp.bfloat16), "fsdp", scatter_dimension=0, tiled=True
        ).astype(jnp.float32),
        lax.psum_scatter(
            grad_shift_one.astype(jnp.bfloat16), "fsdp", scatter_dimension=0, tiled=True
        ).astype(jnp.float32),
        lax.psum_scatter(
            grad_bias_query.astype(jnp.bfloat16), "fsdp", scatter_dimension=0, tiled=True
        ).astype(jnp.float32),
        lax.psum_scatter(
            grad_bias_value.astype(jnp.bfloat16), "fsdp", scatter_dimension=0, tiled=True
        ).astype(jnp.float32),
        lax.psum_scatter(
            grad_bias_attention.astype(jnp.bfloat16), "fsdp", scatter_dimension=0, tiled=True
        ).astype(jnp.float32),
        lax.psum_scatter(
            grad_gain_two.astype(jnp.bfloat16), "fsdp", scatter_dimension=0, tiled=True
        ).astype(jnp.float32),
        lax.psum_scatter(
            grad_shift_two.astype(jnp.bfloat16), "fsdp", scatter_dimension=0, tiled=True
        ).astype(jnp.float32),
        lax.psum_scatter(
            grad_bias_expand.astype(jnp.bfloat16), "fsdp", scatter_dimension=0, tiled=True
        ).astype(jnp.float32),
        lax.psum_scatter(
            grad_bias_contract.astype(jnp.bfloat16), "fsdp", scatter_dimension=0, tiled=True
        ).astype(jnp.float32),
    )
    totals = (
        lax.psum(shares[0].astype(jnp.bfloat16), "seq").astype(jnp.float32),
        lax.psum(shares[1].astype(jnp.bfloat16), "seq").astype(jnp.float32),
        lax.psum(shares[2].astype(jnp.bfloat16), "seq").astype(jnp.float32),
        lax.psum(shares[3].astype(jnp.bfloat16), "seq").astype(jnp.float32),
        lax.psum(shares[4].astype(jnp.bfloat16), "seq").astype(jnp.float32),
        lax.psum(shares[5].astype(jnp.bfloat16), "seq").astype(jnp.float32),
        lax.psum(shares[6].astype(jnp.bfloat16), "seq").astype(jnp.float32),
        lax.psum(shares[7].astype(jnp.bfloat16), "seq").astype(jnp.float32),
        lax.psum(shares[8].astype(jnp.bfloat16), "seq").astype(jnp.float32),
        lax.psum(shares[9].astype(jnp.bfloat16), "seq").astype(jnp.float32),
        lax.psum(shares[10].astype(jnp.bfloat16), "seq").astype(jnp.float32),
        lax.psum(shares[11].astype(jnp.bfloat16), "seq").astype(jnp.float32),
        lax.psum(shares[12].astype(jnp.bfloat16), "seq").astype(jnp.float32),
    )
    return (
        layer_out,
        grad_tokens,
        totals[4],
        totals[5],
        totals[0],
        totals[6],
        totals[7],
        totals[1],
        totals[8],
        totals[9],
        totals[10],
        totals[2],
        totals[11],
        totals[3],
        totals[12],
    )


MESH = pl.DeviceIdType.MESH
BF = jnp.bfloat16
F32 = jnp.float32
NEG = -1e30
GELU_A = math.sqrt(2.0 / math.pi)
GELU_B = 0.044715
ORDER = (0, 1, 4, 5, 2, 3, 6, 7)


def dot_nn(a, b):
    return lax.dot_general(a, b, (((1,), (0,)), ((), ())), preferred_element_type=F32)


def dot_nt(a, b):
    return lax.dot_general(a, b, (((1,), (1,)), ((), ())), preferred_element_type=F32)


def dot_tn(a, b):
    return lax.dot_general(a, b, (((0,), (0,)), ((), ())), preferred_element_type=F32)


def normalize(v):
    mean = jnp.mean(v, axis=-1, keepdims=True)
    centred = v - mean
    var = jnp.mean(centred * centred, axis=-1, keepdims=True)
    rstd = lax.rsqrt(var + norm_eps)
    return centred * rstd, rstd


def normalize_back(grad, gain, hat, rstd):
    g = grad * gain
    return rstd * (
        g
        - jnp.mean(g, axis=-1, keepdims=True)
        - hat * jnp.mean(g * hat, axis=-1, keepdims=True)
    )


def col_sum(v):
    return jnp.sum(v, axis=0, keepdims=True)


def layer_kernel(
    po, gl, tok, cot, win, wout, wexp, wcon, small,
    lo, gt, g_in, g_out, g_e, g_c, g_sm,
    wi_a, wo_a, we_a, wc_a, sm_a, vec, ebv, lane_mask,
    x_a, e_a, a_a, qkv, bias, p0, p1, p2, p3, o_a, h_own, b_a, g_a, du_a,
    part, db, part_r, db_r, dr_a, dh_own, do_a, dd, acc_k, acc_v, stage,
    vec_g, eb_g,
    st_c, st_e, st_o, st_i, st_s,
    rh_c, ry_c, ry_e, ry_o, ry_i, ry_s,
    rz_c, rz_e, rz_o, rz_i, rz_s,
    xb_c, xb_e, xb_o, xb_i, xb_s,
    rx_c, rx_e, rx_o, rx_i, rx_s,
    fc_c, fc_e, fc_o, fc_i, fc_s,
    rc_c, rc_e, rc_o, rc_i, rc_s,
    ag_s, ag_r, ax_s, ax_r, tk_s, tk_r, loc, ex_s, ex_r, rs_s, rs_r, cx_s, cx_r, out_s, out_r,
):
    f = lax.axis_index("fsdp")
    s = lax.axis_index("seq")
    z = f // 2
    y = f % 2
    x = s // 2
    c = s % 2
    dev_y = (z * 2 + 1 - y, s)
    dev_x = (f, (1 - x) * 2 + c)
    dev_c = (f, x * 2 + 1 - c)
    chunks, rows, width = x_a.shape
    length = chunks * rows

    def dev_z(zo):
        return (zo * 2 + y, s)

    def rcopy(src, dst, ssem, rsem, dev):
        return pltpu.make_async_remote_copy(
            src_ref=src, dst_ref=dst, send_sem=ssem, recv_sem=rsem, device_id=dev, device_id_type=MESH
        )

    def slot(zz, yy):
        return (zz % 2) * 4 + (zz // 2) * 2 + yy

    barrier = pltpu.get_barrier_semaphore()
    for dev in (dev_z((z + 1) % 4), dev_z((z + 2) % 4), dev_z((z + 3) % 4), dev_y, dev_x, dev_c):
        pl.semaphore_signal(barrier, inc=1, device_id=dev, device_id_type=MESH)

    sm_a[f] = small[...]
    for pr in range(2):
        for part_i in range(3):
            col = pl.multiple_of(part_i * width + c * 256 + pr * 128, 128)
            wi_a[pr, f, :, part_i * 128 : part_i * 128 + 128] = win[:, pl.ds(col, 128)]
    wc_a[slot(z, y)] = wcon[pl.ds(pl.multiple_of(c * 128, 128), 128), :]
    for b, ff in enumerate(ORDER):
        col = pl.multiple_of(ff * 256 + c * 128, 128)
        dst = (b % 4) * 128
        we_a[b // 4, f, :, dst : dst + 128] = wexp[:, pl.ds(col, 128)]
    wo_a[f] = wout[...]
    pl.semaphore_wait(barrier, 6)
    step = [0]
    actions = {}

    def point():
        for name in SCHEDULE[step[0]]:
            key, _, rest = name.partition(":")
            actions[key](*[int(v) for v in rest.split(".") if v])
        step[0] += 1

    col_c = pl.multiple_of(c * 256, 256)

    def view(g, zz, yy, half):
        o = zz * 2 + yy
        if g == 0:
            return sm_a.at[o]
        if g in (1, 2):
            return wi_a.at[g - 1, o]
        if g == 3:
            return wc_a.at[slot(zz, yy), pl.ds(pl.multiple_of(half * 64, 64), 64), :]
        if g == 4:
            return we_a.at[0, o, pl.ds(pl.multiple_of(half * 32, 32), 32), :]
        if g == 5:
            return wo_a.at[o, :, pl.ds(col_c, 256)]
        return we_a.at[1, o]

    def ag_copy(g, zz, yy, sem, dev):
        ref = view(g, zz, yy, x)
        return rcopy(ref, ref, ag_s.at[g, sem], ag_r.at[g, zz * 2 + yy], dev)

    def ax_copy(g, zz, yy, sem, half):
        ref = view(g, zz, yy, half)
        return rcopy(ref, ref, ax_s.at[g - 3, sem], ax_r.at[g - 3, zz * 2 + yy], dev_x)

    def ag_start(g):
        for d in range(1, 4):
            ag_copy(g, z, y, d - 1, dev_z((z + d) % 4)).start()
        ag_copy(g, z, y, 3, dev_y).start()

    def ag_from_z(g, d):
        zo = (z + d) % 4
        cp = ag_copy(g, zo, y, 3 + d, dev_y)
        cp.wait_recv()
        cp.start()
        if g in (3, 4):
            ax_copy(g, zo, y, d - 1, x).start()

    def ag_from_y(g, zo):
        ag_copy(g, zo, 1 - y, 3, dev_y).wait_recv()
        ax_copy(g, zo, 1 - y, 3 + zo, x).start()

    def ag_finish(g):
        if g in (3, 4):
            for d in range(1, 4):
                ax_copy(g, (z + d) % 4, y, d - 1, 1 - x).wait_recv()
            for zo in range(4):
                ax_copy(g, zo, 1 - y, 3 + zo, 1 - x).wait_recv()
        else:
            for zo in range(4):
                ag_copy(g, zo, 1 - y, 3, dev_y).wait_recv()

    def ag_drain(g):
        for i in range(7):
            ag_copy(g, z, y, i, dev_y).wait_send()
            if g in (3, 4):
                ax_copy(g, z, y, i, x).wait_send()

    def swap_start(n, src, ref):
        rcopy(src.at[1 - x], ref.at[s], tk_s.at[n, 0], tk_r.at[n, 0], dev_x).start()
        rcopy(src.at[x], ref.at[s], tk_s.at[n, 1], tk_r.at[n, 1], dev_c).start()
        pltpu.make_async_copy(src.at[x], ref.at[s], loc.at[n]).start()

    def swap_forward(n, src, ref):
        k = (1 - x) * 2 + c
        rcopy(src.at[1 - x], ref.at[k], tk_s.at[n, 0], tk_r.at[n, 0], dev_x).wait_recv()
        rcopy(ref.at[k], ref.at[k], tk_s.at[n, 2], tk_r.at[n, 2], dev_c).start()

    def swap_finish(n, src, ref):
        rcopy(ref.at[s], ref.at[s], tk_s.at[n, 2], tk_r.at[n, 2], dev_c).wait_recv()

    def swap_near(n, src, ref):
        pltpu.make_async_copy(src.at[x], ref.at[s], loc.at[n]).wait()
        rcopy(src.at[x], ref.at[s], tk_s.at[n, 1], tk_r.at[n, 1], dev_c).wait_recv()

    def swap_drain(n, src, ref):
        rcopy(src.at[1 - x], ref.at[s], tk_s.at[n, 0], tk_r.at[n, 0], dev_x).wait_send()
        rcopy(src.at[x], ref.at[s], tk_s.at[n, 1], tk_r.at[n, 1], dev_c).wait_send()
        rcopy(ref.at[s], ref.at[s], tk_s.at[n, 2], tk_r.at[n, 2], dev_c).wait_send()

    swaps = ((tok, x_a), (cot, e_a))
    actions["start"] = ag_start
    actions["swap"] = lambda n: swap_start(n, *swaps[n])
    actions["share"] = lambda n: swap_forward(n, *swaps[n])
    actions["az"] = ag_from_z
    actions["ay"] = ag_from_y
    point()

    group = po[x]
    first_end = gl[group, 0]
    second_end = first_end + gl[group, 1]

    def mask_block(k, carry):
        qp = k * rows + lax.broadcasted_iota(jnp.int32, (rows, length), 0)
        kp = lax.broadcasted_iota(jnp.int32, (rows, length), 1)
        hidden_key = (kp >= first_end) & (kp < second_end) & (qp >= second_end)
        bad = (kp > qp) | hidden_key
        bias[k] = jnp.where(bad, NEG, 0.0).astype(F32)
        return carry

    lax.fori_loop(0, chunks, mask_block, 0)
    lanes = lax.broadcasted_iota(jnp.int32, (8, 128), 1)
    lane_row = lax.broadcasted_iota(jnp.int32, (8, 128), 0)
    lane_mask[...] = jnp.where((lanes < 64) == (lane_row < 1), 1.0, 0.0).astype(F32)
    vec_g[...] = jnp.zeros_like(vec_g)
    eb_g[...] = jnp.zeros_like(eb_g)

    point()
    ag_finish(0)
    for r in range(4):
        low_half = sm_a[2 * r, 0:8, :]
        high_half = pltpu.roll(sm_a[2 * r + 1, 0:8, :], 64, 1)
        vec[:, r * 128 : r * 128 + 128] = jnp.where(lanes < 64, low_half, high_half)
    for b, ff in enumerate(ORDER):
        ebv[:, b * 128 : b * 128 + 128] = sm_a[ff, pl.ds(8 + c, 1), :]
    swap_near(0, tok, x_a)
    point()
    swap_finish(0, tok, x_a)

    def norm_one(k, carry):
        hat, _ = normalize(x_a[k].astype(F32))
        a_a[k] = (hat * vec[0:1, :] + vec[1:2, :]).astype(BF)
        return carry

    lax.fori_loop(0, chunks, norm_one, 0)
    point()

    def project(pr):
        col = pl.multiple_of(c * 256 + pr * 128, 128)

        def block(k, carry):
            row0 = pl.multiple_of(k * rows, rows)
            out = dot_nn(a_a[k], wi_a[pr].reshape(width, 384))
            qkv[pr, pl.ds(row0, rows), 0:128] = (out[:, 0:128] + vec[2:3, pl.ds(col, 128)]).astype(BF)
            qkv[pr, pl.ds(row0, rows), 128:256] = out[:, 128:256].astype(BF)
            qkv[pr, pl.ds(row0, rows), 256:384] = (out[:, 256:384] + vec[3:4, pl.ds(col, 128)]).astype(BF)
            return carry

        lax.fori_loop(0, chunks, block, 0)

    probs = (p0, p1, p2, p3)
    masks = [lane_mask[i : i + 1, :] for i in range(2)]
    masks_low = [m.astype(BF) for m in masks]
    scaled_low = [(m * 0.125).astype(BF) for m in masks]

    def attend(pr, i):
        span = (i + 1) * rows
        q = qkv[pr, i * rows : i * rows + rows, 0:128]
        k = qkv[pr, 0:span, 128:256]
        v = qkv[pr, 0:span, 256:384]
        mixed = []
        for hh in range(2):
            sc = dot_nt(q * scaled_low[hh], k) + bias[i, :, 0:span]
            top = jnp.max(sc, axis=-1, keepdims=True)
            ex = jnp.exp(sc - top)
            tot = jnp.sum(ex, axis=-1, keepdims=True)
            pb = (ex * (1.0 / tot)).astype(BF)
            probs[i][pr, hh] = pb
            mixed.append(dot_nn(pb, v) * masks[hh])
        col = pl.multiple_of(c * 256 + pr * 128, 128)
        o_a[i, :, pl.ds(col, 128)] = (mixed[0] + mixed[1]).astype(BF)

    def o_copy(pr):
        col = pl.multiple_of(c * 256 + pr * 128, 128)
        ref = o_a.at[:, :, pl.ds(col, 128)]
        return rcopy(ref, ref, ex_s.at[pr], ex_r.at[pr], dev_c)

    def wo_copy():
        ref = wo_a.at[:, :, pl.ds(col_c, 256)]
        return rcopy(ref, ref, ex_s.at[12], ex_r.at[12], dev_c)

    def wo_start():
        ag_finish(5)
        wo_copy().start()

    actions["wo"] = wo_start
    ag_finish(1)
    project(0)
    point()
    for i in range(chunks):
        attend(0, i)
        point()
    o_copy(0).start()
    ag_finish(2)
    project(1)
    point()
    for i in range(chunks):
        attend(1, i)
        if i == chunks - 1:
            o_copy(1).start()
        point()
    for pr in range(2):
        o_copy(pr).wait_recv()
    ref = wo_a.at[:, :, pl.ds(pl.multiple_of((1 - c) * 256, 256), 256)]
    rcopy(ref, ref, ex_s.at[12], ex_r.at[12], dev_c).wait_recv()

    def b_copy(j):
        ref = b_a.at[c + 2 * j]
        return rcopy(ref, ref, ex_s.at[2 + j], ex_r.at[2 + j], dev_c)

    for j in range(2):
        k = c + 2 * j
        out = dot_nn(o_a[k], wo_a[...].reshape(width, width))
        h = x_a[k].astype(F32) + out + vec[4:5, :]
        h_own[j] = h
        hat, _ = normalize(h)
        b_a[k] = (hat * vec[5:6, :] + vec[6:7, :]).astype(BF)
        b_copy(j).start()
        point()
    swap_near(1, cot, e_a)
    swap_finish(1, cot, e_a)
    ag_finish(3)
    ag_finish(4)
    half = we_a.shape[3]

    def mlp_chunk(h, j, k):
        we = we_a[h].reshape(width, half)
        wc = wc_a[4 * h : 4 * h + 4].reshape(half, width)
        u = dot_nn(b_a[k], we) + ebv[:, h * half : h * half + half]
        u2 = u * u
        th = jnp.tanh(GELU_A * (u + GELU_B * (u2 * u)))
        hf = 0.5 * (1.0 + th)
        g = (u * hf).astype(BF)
        g_a[h, k] = g
        slope = hf + (0.5 * GELU_A) * u * (1.0 - th * th) * (1.0 + (3.0 * GELU_B) * u2)
        du = (slope * dot_nt(e_a[k], wc)).astype(BF)
        du_a[h, k] = du
        eb_g[:, h * half : h * half + half] += col_sum(du.astype(F32))
        new_part = dot_nn(g, wc)
        new_db = dot_nt(du, we)
        if h == 0:
            part[j] = new_part
            db[j] = new_db
        else:
            part[j] += new_part
            db[j] += new_db

    def part_copy(j):
        return rcopy(part.at[j], part_r.at[j - 2], ex_s.at[4 + j - 2], ex_r.at[4 + j - 2], dev_c)

    def db_copy(j):
        return rcopy(db.at[j], db_r.at[j - 2], ex_s.at[6 + j - 2], ex_r.at[6 + j - 2], dev_c)

    def rs_names(g):
        return (
            (st_c, ry_c, rz_c, xb_c, rx_c, fc_c, rc_c),
            tuple(r.at[0] for r in (st_e, ry_e, rz_e, xb_e, rx_e, fc_e, rc_e)),
            tuple(r.at[1] for r in (st_e, ry_e, rz_e, xb_e, rx_e, fc_e, rc_e)),
            (st_o, ry_o, rz_o, xb_o, rx_o, fc_o, rc_o),
            tuple(r.at[0] for r in (st_i, ry_i, rz_i, xb_i, rx_i, fc_i, rc_i)),
            tuple(r.at[1] for r in (st_i, ry_i, rz_i, xb_i, rx_i, fc_i, rc_i)),
            (st_s, ry_s, rz_s, xb_s, rx_s, fc_s, rc_s),
        )[g]

    mine = pl.ds(pl.multiple_of(x * 64, 64), 64)
    theirs = pl.ds(pl.multiple_of((1 - x) * 64, 64), 64)

    def con_x(zt):
        return rcopy(st_c.at[:, zt, theirs], rh_c.at[zt], cx_s.at[zt], cx_r.at[zt], dev_x)

    def con_y(zt):
        return rcopy(st_c.at[1 - y, zt, mine], ry_c.at[zt], rs_s.at[0, zt], rs_r.at[0, zt], dev_y)

    def con_z(zt):
        return rcopy(st_c.at[y, zt, mine], rz_c.at[z], rs_s.at[0, 4 + zt], rs_r.at[0, 4 + z], dev_z(zt))

    def con_y_start(zt):
        con_x(zt).wait_recv()
        for yy in range(2):
            st_c[yy, zt, mine] = (st_c[yy, zt, mine].astype(F32) + rh_c[zt, yy].astype(F32)).astype(BF)
        con_y(zt).start()

    def con_z_start(zt):
        con_y(zt).wait_recv()
        st_c[y, zt, mine] = (st_c[y, zt, mine].astype(F32) + ry_c[zt].astype(F32)).astype(BF)

        @pl.when(z != zt)
        def _():
            con_z(zt).start()

    def rs_y(g, zo):
        st, ry = rs_names(g)[:2]
        return rcopy(st.at[1 - y, zo], ry.at[zo], rs_s.at[g, zo], rs_r.at[g, zo], dev_y)

    def rs_z(g, zo):
        st, _, rz = rs_names(g)[:3]
        return rcopy(st.at[y, zo], rz.at[z], rs_s.at[g, 4 + zo], rs_r.at[g, 4 + z], dev_z(zo))

    def rs_x(g):
        xb, rx = rs_names(g)[3:5]
        return rcopy(xb, rx, rs_s.at[g, 8], rs_r.at[g, 8], dev_x)

    def rs_c(g):
        fc, rc = rs_names(g)[5:7]
        return rcopy(fc, rc, rs_s.at[g, 9], rs_r.at[g, 9], dev_c)

    def rs_y_start(g):
        for d in (1, 2, 3, 0):
            rs_y(g, (z + d) % 4).start()

    def rs_z_start(g, d):
        zo = (z + d) % 4
        st, ry = rs_names(g)[:2]
        rs_y(g, zo).wait_recv()
        st[y, zo] = (st[y, zo].astype(F32) + ry[zo].astype(F32)).astype(st.dtype)
        rs_z(g, zo).start()

    def rs_x_start(g):
        st, ry, rz, xb = rs_names(g)[:4]
        if g == 0:
            total = st_c[y, z, mine].astype(F32)
        else:
            rs_y(g, z).wait_recv()
            total = st[y, z].astype(F32) + ry[z].astype(F32)
        for d in range(1, 4):
            zo = (z + d) % 4
            if g == 0:
                cp = rcopy(st_c.at[y, zo, mine], rz.at[zo], rs_s.at[g, 4 + zo], rs_r.at[g, 4 + zo], dev_z(zo))
            else:
                cp = rcopy(st.at[y, zo], rz.at[zo], rs_s.at[g, 4 + zo], rs_r.at[g, 4 + zo], dev_z(zo))
            cp.wait_recv()
            total = total + rz[zo].astype(F32)
        xb[...] = total.astype(xb.dtype)
        rs_x(g).start()

    def write_out(g, side, value):
        if g == 0:
            g_c[pl.ds(pl.multiple_of(side * 128, 128), 128), :] = value
        elif g in (1, 2):
            for b in range(4):
                col = pl.multiple_of(ORDER[(g - 1) * 4 + b] * 256 + side * 128, 128)
                g_e[:, pl.ds(col, 128)] = value[:, b * 128 : b * 128 + 128]
        elif g == 3:
            g_out[:, pl.ds(pl.multiple_of(side * 256, 256), 256)] = value
        else:
            for part_i in range(3):
                col = pl.multiple_of(part_i * width + side * 256 + (g - 4) * 128, 128)
                g_in[:, pl.ds(col, 128)] = value[:, part_i * 128 : part_i * 128 + 128]

    def rs_c_start(g):
        xb, rx, fc = rs_names(g)[3:6]
        rs_x(g).wait_recv()
        if g == 0:
            fc[mine] = xb[...].astype(F32)
            fc[theirs] = rx[...].astype(F32)
        else:
            fc[...] = xb[...].astype(F32) + rx[...].astype(F32)
        rs_c(g).start()
        if g < 6:
            write_out(g, c, fc[...])

    def rs_finish(g):
        fc, rc = rs_names(g)[5:7]
        rs_c(g).wait_recv()
        if g < 6:
            write_out(g, 1 - c, rc[...])
        else:
            g_sm[...] = fc[...] + rc[...]

    def rs_drain(g):
        for zo in range(4):
            if g == 0:
                con_x(zo).wait_send()
                con_y(zo).wait_send()
            else:
                rs_y(g, zo).wait_send()

            @pl.when(z != zo)
            def _():
                if g == 0:
                    con_z(zo).wait_send()
                else:
                    rs_z(g, zo).wait_send()

        rs_x(g).wait_send()
        rs_c(g).wait_send()

    def grad_con(zt):
        col = (zt // 2) * 256
        out = dot_tn(
            g_a[zt % 2, :, :, col : col + 256].reshape(length, 256), e_a[...].reshape(length, width)
        )
        st_c[0, zt] = out[0:128].astype(BF)
        st_c[1, zt] = out[128:256].astype(BF)
        con_x(zt).start()

    def grad_exp(h):
        out = dot_tn(b_a[...].reshape(length, width), du_a[h].reshape(length, half))
        for ff in range(8):
            st_e[h, ff % 2, ff // 2] = out[ff * 64 : ff * 64 + 64].astype(BF)
        rs_y_start(1 + h)

    actions["cy"] = con_y_start
    actions["cz"] = con_z_start
    actions["rz"] = rs_z_start
    actions["rx"] = rs_x_start
    actions["rc"] = rs_c_start
    actions["rf"] = rs_finish
    for j in (0, 1, 2, 3):
        if j >= 2:
            ref = b_a.at[1 - c + 2 * (j - 2)]
            rcopy(ref, ref, ex_s.at[j], ex_r.at[j], dev_c).wait_recv()
        mlp_chunk(0, j, (c + 2 * j) if j < 2 else (1 - c) + 2 * (j - 2))
        point()
    grad_con(0)
    point()
    grad_con(2)
    point()
    grad_exp(0)
    point()
    ag_finish(6)
    for j in (2, 3, 0, 1):
        mlp_chunk(1, j, (c + 2 * j) if j < 2 else (1 - c) + 2 * (j - 2))
        if j >= 2:
            part_copy(j).start()
            db_copy(j).start()
        point()
    grad_con(1)
    point()
    grad_con(3)
    point()
    grad_exp(1)
    point()

    def send_rows(n, ref, out):
        far = rcopy(stage.at[n, 1 - x], out.at[x], out_s.at[n, 0], out_r.at[n], dev_x)
        near = pltpu.make_async_copy(stage.at[n, x], out.at[x], out_s.at[n, 1])
        return far, near

    def dr_copy(j):
        ref = dr_a.at[c + 2 * j]
        return rcopy(ref, ref, ex_s.at[8 + j], ex_r.at[8 + j], dev_c)

    for j in range(2):
        k = c + 2 * j
        h = h_own[j]
        e = e_a[k].astype(F32)
        rcopy(db.at[j + 2], db_r.at[j], ex_s.at[6 + j], ex_r.at[6 + j], dev_c).wait_recv()
        grad_b = db[j] + db_r[j]
        hat, rstd = normalize(h)
        dh = e + normalize_back(grad_b, vec[5:6, :], hat, rstd)
        dh_own[j] = dh
        dr = dh.astype(BF)
        dr_a[k] = dr
        dr_copy(j).start()
        vec_g[4:5, :] += col_sum(dr.astype(F32))
        vec_g[5:6, :] += col_sum(grad_b * hat)
        vec_g[6:7, :] += col_sum(grad_b)
        vec_g[7:8, :] += col_sum(e)
        rcopy(part.at[j + 2], part_r.at[j], ex_s.at[4 + j], ex_r.at[4 + j], dev_c).wait_recv()
        stage[0, j] = (h + part[j] + part_r[j] + vec[7:8, :]).astype(BF)
        point()
    for cp in send_rows(0, stage, lo):
        cp.start()

    head_row = pl.multiple_of(c * 4, 4)

    def grad_mixed(k):
        w = wo_a[pl.ds(head_row, 4)].reshape(256, width)
        do_a[k] = dot_nt(dr_a[k], w).astype(BF)

    for j in range(2):
        grad_mixed(c + 2 * j)
    point()
    for j in range(2):
        ref = dr_a.at[1 - c + 2 * j]
        rcopy(ref, ref, ex_s.at[8 + j], ex_r.at[8 + j], dev_c).wait_recv()
        grad_mixed(1 - c + 2 * j)
    point()
    out = dot_tn(o_a[...].reshape(length, width), dr_a[:, :, pl.ds(col_c, 256)].reshape(length, 256))
    for ff in range(8):
        st_o[ff % 2, ff // 2] = out[ff * 64 : ff * 64 + 64].astype(BF)
    rs_y_start(3)
    point()

    def attend_back(pr, i):
        span = (i + 1) * rows
        q = qkv[pr, i * rows : i * rows + rows, 0:128]
        k = qkv[pr, 0:span, 128:256]
        v = qkv[pr, 0:span, 256:384]
        do = do_a[i, :, pr * 128 : pr * 128 + 128]
        grad_q = None
        for hh in range(2):
            dom = do * masks_low[hh]
            pb = probs[i][pr, hh]
            pf = pb.astype(F32)
            t = pf * dot_nt(dom, v)
            inner = jnp.sum(t, axis=-1, keepdims=True)
            ds = (t - pf * inner).astype(BF)
            acc_v[0:span] += dot_tn(pb, dom)
            acc_k[0:span] += dot_tn(ds, q * scaled_low[hh])
            gq = dot_nn(ds, k * scaled_low[hh])
            grad_q = gq if grad_q is None else grad_q + gq
        dd[pr, i * rows : i * rows + rows, 0:128] = grad_q.astype(BF)

    def back_start():
        acc_k[...] = jnp.zeros_like(acc_k)
        acc_v[...] = jnp.zeros_like(acc_v)

    def back_end(pr):
        dd[pr, :, 128:256] = acc_k[...].astype(BF)
        dd[pr, :, 256:384] = acc_v[...].astype(BF)
        col = pl.multiple_of(c * 256 + pr * 128, 128)
        vec_g[2:3, pl.ds(col, 128)] = col_sum(dd[pr, :, 0:128].astype(F32))
        vec_g[3:4, pl.ds(col, 128)] = col_sum(dd[pr, :, 256:384].astype(F32))

    def grad_in(pr):
        out = dot_tn(a_a[...].reshape(length, width), dd[pr])
        for ff in range(8):
            st_i[pr, ff % 2, ff // 2] = out[ff * 64 : ff * 64 + 64].astype(BF)
        rs_y_start(4 + pr)

    for pr in range(2):
        back_start()
        for i in range(chunks):
            attend_back(pr, i)
            if i < chunks - 1:
                point()
        back_end(pr)
        grad_in(pr)
        point()

    for j in range(2, 4):
        part_copy(j).wait_send()

    def grad_a(k):
        row0 = pl.multiple_of(k * rows, rows)
        total = None
        for pr in range(2):
            p = dot_nt(dd[pr, pl.ds(row0, rows), :], wi_a[pr].reshape(width, 384))
            total = p if total is None else total + p
        return total

    def da_copy(j):
        return rcopy(part.at[j], db_r.at[j - 2], ex_s.at[10 + j - 2], ex_r.at[10 + j - 2], dev_c)

    for j in range(2, 4):
        part[j] = grad_a((1 - c) + 2 * (j - 2))
        da_copy(j).start()
        point()
    for j in range(2):
        part[j] = grad_a(c + 2 * j)
        point()
    for j in range(2):
        k = c + 2 * j
        rcopy(part.at[j + 2], db_r.at[j], ex_s.at[10 + j], ex_r.at[10 + j], dev_c).wait_recv()
        grad = part[j] + db_r[j]
        hat, rstd = normalize(x_a[k].astype(F32))
        vec_g[0:1, :] += col_sum(grad * hat)
        vec_g[1:2, :] += col_sum(grad)
        stage[1, j] = (dh_own[j] + normalize_back(grad, vec[0:1, :], hat, rstd)).astype(BF)
        point()
    for cp in send_rows(1, stage, gt):
        cp.start()

    for r in range(4):
        tile = vec_g[:, r * 128 : r * 128 + 128]
        rolled = pltpu.roll(tile, 64, 1)
        for yy in range(2):
            st_s[yy, r, 0:8, :] = tile if yy == 0 else rolled
            st_s[yy, r, 8:16, :] = jnp.zeros((8, 128), F32)
            b = ORDER.index(2 * r + yy)
            st_s[yy, r, pl.ds(8 + c, 1), :] = eb_g[:, b * 128 : b * 128 + 128]
    rs_y_start(6)
    point()
    for n, out in ((0, lo), (1, gt)):
        far, near = send_rows(n, stage, out)
        near.wait()
        far.wait_send()
        rcopy(stage.at[n, 1 - x], out.at[1 - x], out_s.at[n, 0], out_r.at[n], dev_x).wait_recv()
    for g in range(7):
        ag_drain(g)
    swap_drain(0, tok, x_a)
    swap_drain(1, cot, e_a)
    wo_copy().wait_send()
    for pr in range(2):
        o_copy(pr).wait_send()
    for j in range(2):
        b_copy(j).wait_send()
        dr_copy(j).wait_send()
        db_copy(j + 2).wait_send()
        da_copy(j + 2).wait_send()
    for g in range(7):
        rs_drain(g)


SCHEDULE = (
    ("start:1", "start:0", "start:3", "swap:0", "swap:1", "start:2", "start:4", "az:1.1", "az:1.3", "az:0.1",),
    ("az:0.3", "az:0.2", "az:1.2", "az:3.3", "az:3.2", "az:3.1", "start:5",),
    ("share:0",),
    (),
    ("az:2.3", "az:2.2",),
    ("ay:3.0", "ay:3.3", "az:2.1",),
    (),
    ("start:6", "ay:3.1",),
    ("az:4.2", "ay:3.2", "az:4.3", "az:4.1",),
    ("share:1",),
    ("az:5.1", "az:5.2",),
    ("az:5.3", "ay:4.3", "ay:4.1",),
    ("ay:4.0", "ay:4.2",),
    ("wo", "az:6.3",),
    ("az:6.2",),
    ("az:6.1",),
    (),
    (),
    (),
    (),
    (),
    (),
    (),
    (),
    (),
    (),
    (),
    (),
    ("rz:1.1", "cy:0",),
    (),
    ("rz:1.3",),
    (),
    ("cy:2",),
    ("rz:1.2",),
    (),
    (),
    ("rz:2.1",),
    ("cy:3", "cy:1", "rz:2.2", "rz:2.3",),
    ("cz:0", "rz:3.1", "rz:3.2",),
    ("cz:2", "rx:1",),
    ("rz:3.3", "cz:3",),
    ("rc:1", "cz:1", "rx:2", "rz:4.1",),
    ("rz:4.3",),
    ("rz:4.2", "rc:2",),
    (),
    ("rf:2", "rx:0",),
    ("rz:5.1", "rx:3",),
    ("rf:1",),
    ("rz:5.2", "rx:4", "rz:5.3",),
    ("rz:6.2", "rz:6.3", "rz:6.1", "rc:4", "rx:5", "rx:6", "rc:3", "rc:0", "rf:3", "rc:5", "rc:6", "rf:6", "rf:4", "rf:0", "rf:5",),
)


def finish_kernel(*refs):
    gs = refs[6]
    outs = refs[7:]
    for i in range(6):
        outs[i][...] = refs[i][...]
    for i in range(8):
        outs[6 + i][...] = gs[i : i + 1, 0 : outs[6 + i].shape[1]]
    outs[14][:, 0:128] = gs[8:9, :]
    outs[14][:, 128:256] = gs[9:10, :]


def fast_shards(
    tokens, placement_order, group_lengths, first_gain, first_shift, attention_in, query_bias,
    value_bias, attention_out, attention_bias, second_gain, second_shift, expand_weight,
    expand_bias, contract_weight, contract_bias, cotangent,
):
    batch, rows, width = tokens.shape
    lanes = first_gain.shape[0]
    vectors = (
        first_gain, first_shift, query_bias, value_bias, attention_bias, second_gain,
        second_shift, contract_bias,
    )
    stacked = jnp.pad(jnp.stack(vectors), ((0, 0), (0, 128 - lanes)))
    small = jnp.concatenate(
        [stacked, expand_bias.reshape(2, 128), jnp.zeros((6, 128), BF)], axis=0
    ).astype(F32)
    chunks = 4
    length = chunks * rows
    half = expand_weight.shape[1] // 4
    vm = pl.BlockSpec(memory_space=pltpu.VMEM)
    sm = pl.BlockSpec(memory_space=pltpu.SMEM)
    hb = pl.BlockSpec(memory_space=pl.ANY)
    V = pltpu.VMEM
    pieces = (((128, width), None), ((64, half), 2), ((64, 256), None), ((64, 384), 2))

    def family(lead, dtype, con=128):
        out = []
        for n, (shape, pairs) in enumerate(pieces):
            if n == 0:
                shape = (con, width)
            pre = () if pairs is None else (pairs,)
            out.append(V(pre + lead + shape, dtype))
        out.append(V(lead + (16, 128), F32))
        return out

    dma = pltpu.SemaphoreType.DMA
    scratch = [
        V((2, 8, 64, 384), BF), V((8, 64, width), BF), V((2, 8, 64, half), BF), V((8, 128, width), BF),
        V((8, 16, 128), F32), V((8, width), F32), V((1, 2 * half), F32), V((8, 128), F32),
        V((chunks, rows, width), BF), V((chunks, rows, width), BF), V((chunks, rows, width), BF),
        V((2, length, 384), BF), V((chunks, rows, length), F32),
        V((2, 2, rows, rows), BF), V((2, 2, rows, 2 * rows), BF), V((2, 2, rows, 3 * rows), BF),
        V((2, 2, rows, 4 * rows), BF),
        V((chunks, rows, width), BF), V((2, rows, width), F32), V((chunks, rows, width), BF),
        V((2, chunks, rows, half), BF), V((2, chunks, rows, half), BF),
        V((4, rows, width), F32), V((4, rows, width), F32), V((2, rows, width), F32),
        V((2, rows, width), F32), V((chunks, rows, width), BF), V((2, rows, width), F32),
        V((chunks, rows, 256), BF), V((2, length, 384), BF), V((length, 128), F32),
        V((length, 128), F32), V((2, 2, rows, width), BF), V((8, width), F32), V((1, 2 * half), F32),
    ]
    scratch += family((2, 4), BF) + [V((4, 2, 64, width), BF)] + family((4,), BF, 64)
    scratch += family((4,), BF, 64) + family((), BF, 64) + family((), BF, 64)
    scratch += family((), F32) + family((), F32)
    scratch += [
        dma((7, 7)), dma((7, 8)), dma((2, 7)), dma((2, 8)), dma((2, 3)), dma((2, 3)), dma((2,)),
        dma((13,)), dma((13,)), dma((7, 10)), dma((7, 10)), dma((4,)), dma((4,)), dma((2, 2)), dma((2,)),
    ]
    grads = (
        jax.ShapeDtypeStruct(tokens.shape, BF),
        jax.ShapeDtypeStruct(tokens.shape, BF),
        jax.ShapeDtypeStruct(attention_in.shape, F32),
        jax.ShapeDtypeStruct(attention_out.shape, F32),
        jax.ShapeDtypeStruct(expand_weight.shape, F32),
        jax.ShapeDtypeStruct(contract_weight.shape, F32),
    )
    outs = pl.pallas_call(
        layer_kernel,
        out_shape=grads + (jax.ShapeDtypeStruct((16, 128), F32),),
        in_specs=[sm, sm, hb, hb, vm, vm, vm, vm, vm],
        out_specs=[hb, hb, vm, vm, vm, vm, vm],
        scratch_shapes=scratch,
        compiler_params=pltpu.CompilerParams(
            collective_id=0, has_side_effects=True, vmem_limit_bytes=63 << 20
        ),
    )(
        placement_order, group_lengths, tokens, cotangent, attention_in, attention_out,
        expand_weight, contract_weight, small,
    )
    outs = pl.pallas_call(
        finish_kernel,
        out_shape=grads
        + tuple(jax.ShapeDtypeStruct((1, lanes), F32) for _ in range(8))
        + (jax.ShapeDtypeStruct((1, 256), F32),),
        in_specs=[vm] * 7,
        out_specs=[vm] * 15,
    )(*outs)
    layer_out, grad_tokens, g_in, g_out, g_e, g_c = outs[:6]
    v = [item.reshape(-1) for item in outs[6:]]
    return (
        layer_out, grad_tokens, v[0], v[1], g_in, v[2], v[3], g_out,
        v[4], v[5], v[6], g_e, v[8], g_c, v[7],
    )


def solution(mesh):
    in_specs = (
        P("fsdp", "seq", None),
        P("fsdp"),
        P(),
        P("fsdp"),
        P("fsdp"),
        P("fsdp", None),
        P("fsdp"),
        P("fsdp"),
        P("fsdp", None),
        P("fsdp"),
        P("fsdp"),
        P("fsdp"),
        P("fsdp", None),
        P("fsdp"),
        P("fsdp", None),
        P("fsdp"),
        P("fsdp", "seq", None),
    )
    out_specs = (
        P("fsdp", "seq", None),
        P("fsdp", "seq", None),
        P("fsdp"),
        P("fsdp"),
        P("fsdp", None),
        P("fsdp"),
        P("fsdp"),
        P("fsdp", None),
        P("fsdp"),
        P("fsdp"),
        P("fsdp"),
        P("fsdp", None),
        P("fsdp"),
        P("fsdp", None),
        P("fsdp"),
    )
    pick = fast_shards if (mesh.shape["fsdp"], mesh.shape["seq"]) == (8, 4) else shards
    return jax.shard_map(pick, mesh=mesh, in_specs=in_specs, out_specs=out_specs, check_vma=False)
```

```python
import math

import jax
import jax.numpy as jnp
from jax import lax
from jax.experimental import pallas as pl
from jax.experimental.pallas import tpu as pltpu
from jax.sharding import PartitionSpec as P

HD = 64


norm_eps = 1e-05


def layer_norm(values, gain, shift):
    mean = jnp.mean(values, axis=-1, keepdims=True)
    centred = values - mean
    variance = jnp.mean(centred * centred, axis=-1, keepdims=True)
    return centred * lax.rsqrt(variance + norm_eps) * gain + shift


def gelu_tanh(values):
    return jax.nn.gelu(values, approximate=True)


def masked_scores(query_blk, keys, start, segment, scale):
    count = query_blk.shape[0]
    scores = jnp.einsum("qhd,khd->hqk", query_blk, keys, preferred_element_type=jnp.float32) * scale
    query_pos = start + jnp.arange(count, dtype=jnp.int32)
    key_pos = jnp.arange(keys.shape[0], dtype=jnp.int32)
    query_seg = lax.dynamic_slice_in_dim(segment, start, count, 0)
    allowed = (key_pos[None, :] <= query_pos[:, None]) & (
        (segment[None, :] == query_seg[:, None]) | (segment[None, :] == 0)
    )
    return jnp.where(allowed[None], scores, -1e30)


def forward_heads(query, keys, values, segment, block, scale):
    starts = jnp.arange(query.shape[0] // block, dtype=jnp.int32) * block

    def forward_one_block(start):
        query_blk = lax.dynamic_slice_in_dim(query, start, block, 0)
        scores = masked_scores(query_blk, keys, start, segment, scale)
        top = jnp.max(scores, axis=-1, keepdims=True)
        raised = jnp.exp(scores - top)
        total = jnp.sum(raised, axis=-1, keepdims=True)
        weights = (raised / total).astype(jnp.bfloat16)
        mixed = jnp.einsum("hqk,khd->qhd", weights, values, preferred_element_type=jnp.float32)
        return (mixed.astype(jnp.bfloat16), (top + jnp.log(total))[..., 0])

    return lax.map(forward_one_block, starts)


def backward_heads(query, keys, values, segment, log_total, grad_out, block, scale):
    count = query.shape[0] // block
    starts = jnp.arange(count, dtype=jnp.int32) * block
    grad_blocks = grad_out.reshape((count, block) + grad_out.shape[1:])

    def backward_one_block(carry, inputs):
        grad_keys, grad_values = carry
        start, total_blk, grad_blk = inputs
        query_blk = lax.dynamic_slice_in_dim(query, start, block, 0)
        scores = masked_scores(query_blk, keys, start, segment, scale)
        probs = jnp.exp(scores - total_blk[:, :, None])
        grad_probs = jnp.einsum(
            "qhd,khd->hqk", grad_blk, values, preferred_element_type=jnp.float32
        )
        inner = jnp.sum(probs * grad_probs, axis=-1, keepdims=True)
        grad_scores = (probs * (grad_probs - inner)).astype(jnp.bfloat16)
        grad_query = (
            jnp.einsum("hqk,khd->qhd", grad_scores, keys, preferred_element_type=jnp.float32)
            * scale
        )
        grad_keys = (
            grad_keys
            + jnp.einsum("hqk,qhd->khd", grad_scores, query_blk, preferred_element_type=jnp.float32)
            * scale
        )
        grad_values = grad_values + jnp.einsum(
            "hqk,qhd->khd", probs.astype(jnp.bfloat16), grad_blk, preferred_element_type=jnp.float32
        )
        return ((grad_keys, grad_values), grad_query)

    zeros = jnp.zeros(keys.shape, jnp.float32)
    (grad_keys, grad_values), grad_query = lax.scan(
        backward_one_block, (zeros, zeros), (starts, log_total, grad_blocks)
    )
    return (grad_query.reshape(query.shape), grad_keys, grad_values)


def shards(
    tokens,
    placement_order,
    group_lengths,
    first_gain,
    first_shift,
    attention_in,
    query_bias,
    value_bias,
    attention_out,
    attention_bias,
    second_gain,
    second_shift,
    expand_weight,
    expand_bias,
    contract_weight,
    contract_bias,
    cotangent,
):
    batch, rows, width = tokens.shape
    seq_count = lax.axis_size("seq")
    seq_len = rows * seq_count
    block = min(512, seq_len)
    scale = 1.0 / math.sqrt(HD)
    gathered = (
        lax.all_gather(attention_in, "fsdp", axis=0, tiled=True),
        lax.all_gather(attention_out, "fsdp", axis=0, tiled=True),
        lax.all_gather(expand_weight, "fsdp", axis=0, tiled=True),
        lax.all_gather(contract_weight, "fsdp", axis=0, tiled=True),
        lax.all_gather(first_gain, "fsdp", axis=0, tiled=True),
        lax.all_gather(first_shift, "fsdp", axis=0, tiled=True),
        lax.all_gather(query_bias, "fsdp", axis=0, tiled=True),
        lax.all_gather(value_bias, "fsdp", axis=0, tiled=True),
        lax.all_gather(attention_bias, "fsdp", axis=0, tiled=True),
        lax.all_gather(second_gain, "fsdp", axis=0, tiled=True),
        lax.all_gather(second_shift, "fsdp", axis=0, tiled=True),
        lax.all_gather(expand_bias, "fsdp", axis=0, tiled=True),
        lax.all_gather(contract_bias, "fsdp", axis=0, tiled=True),
    )
    in_full, out_full, expand_full, contract_full = (
        gathered[0],
        gathered[1],
        gathered[2],
        gathered[3],
    )
    small = [item.astype(jnp.float32) for item in gathered[4:]]
    (
        gain_one,
        shift_one,
        bias_query,
        bias_value,
        bias_attention,
        gain_two,
        shift_two,
        bias_expand,
        bias_contract,
    ) = small
    groups = group_lengths.shape[0]
    picked = (placement_order[:, None] == jnp.arange(groups, dtype=jnp.int32)[None, :]).astype(
        jnp.int32
    )
    lengths = jnp.sum(picked[:, :, None] * group_lengths[None, :, :], axis=1)
    positions = jnp.arange(seq_len, dtype=jnp.int32)
    first_end = lengths[:, 0:1]
    second_end = first_end + lengths[:, 1:2]
    segment = (positions[None, :] >= first_end).astype(jnp.int32) + (
        positions[None, :] >= second_end
    ).astype(jnp.int32)
    tok_rows = tokens.reshape(batch * rows, width).astype(jnp.float32)
    normed, norm_one_pull = jax.vjp(layer_norm, tok_rows, gain_one, shift_one)
    normed_low = normed.astype(jnp.bfloat16)
    bias_in = jnp.concatenate([bias_query, jnp.zeros((width,), jnp.float32), bias_value])
    projected = (jnp.dot(normed_low, in_full, preferred_element_type=jnp.float32) + bias_in).astype(
        jnp.bfloat16
    )
    heads_in = lax.all_to_all(
        projected.reshape(batch, rows, 3, width), "seq", split_axis=3, concat_axis=1, tiled=True
    )
    head_cols = heads_in.shape[3]
    per_device = head_cols // HD
    mixed_list = []
    total_list = []
    for index in range(batch):
        query = heads_in[index, :, 0].reshape(seq_len, per_device, HD)
        keys = heads_in[index, :, 1].reshape(seq_len, per_device, HD)
        values = heads_in[index, :, 2].reshape(seq_len, per_device, HD)
        mixed_blocks, log_total = forward_heads(query, keys, values, segment[index], block, scale)
        mixed_list.append(mixed_blocks.reshape(seq_len, head_cols))
        total_list.append(log_total)
    mixed = lax.all_to_all(jnp.stack(mixed_list), "seq", split_axis=1, concat_axis=2, tiled=True)
    mixed_rows = mixed.reshape(batch * rows, width)
    hidden = (
        tok_rows
        + jnp.dot(mixed_rows, out_full, preferred_element_type=jnp.float32)
        + bias_attention
    )
    normed_two, norm_two_pull = jax.vjp(layer_norm, hidden, gain_two, shift_two)
    normed_two_low = normed_two.astype(jnp.bfloat16)
    expanded = (
        jnp.dot(normed_two_low, expand_full, preferred_element_type=jnp.float32) + bias_expand
    )
    activated, gelu_pull = jax.vjp(gelu_tanh, expanded)
    activated_low = activated.astype(jnp.bfloat16)
    result = (
        hidden
        + jnp.dot(activated_low, contract_full, preferred_element_type=jnp.float32)
        + bias_contract
    )
    layer_out = result.astype(jnp.bfloat16).reshape(batch, rows, width)
    grad_low = cotangent.reshape(batch * rows, width)
    grad_res = grad_low.astype(jnp.float32)
    grad_contract = jnp.dot(activated_low.T, grad_low, preferred_element_type=jnp.float32)
    grad_bias_contract = jnp.sum(grad_res, axis=0)
    (grad_expanded,) = gelu_pull(
        jnp.dot(grad_low, contract_full.T, preferred_element_type=jnp.float32)
    )
    grad_expanded_low = grad_expanded.astype(jnp.bfloat16)
    grad_expand = jnp.dot(normed_two_low.T, grad_expanded_low, preferred_element_type=jnp.float32)
    grad_bias_expand = jnp.sum(grad_expanded_low.astype(jnp.float32), axis=0)
    grad_hidden, grad_gain_two, grad_shift_two = norm_two_pull(
        jnp.dot(grad_expanded_low, expand_full.T, preferred_element_type=jnp.float32)
    )
    grad_hidden = grad_hidden + grad_res
    grad_branch_low = grad_hidden.astype(jnp.bfloat16)
    grad_out_proj = jnp.dot(mixed_rows.T, grad_branch_low, preferred_element_type=jnp.float32)
    grad_bias_attention = jnp.sum(grad_branch_low.astype(jnp.float32), axis=0)
    grad_mixed = jnp.dot(grad_branch_low, out_full.T, preferred_element_type=jnp.float32).astype(
        jnp.bfloat16
    )
    grad_heads = lax.all_to_all(
        grad_mixed.reshape(batch, rows, width), "seq", split_axis=2, concat_axis=1, tiled=True
    )
    grad_list = []
    for index in range(batch):
        query = heads_in[index, :, 0].reshape(seq_len, per_device, HD)
        keys = heads_in[index, :, 1].reshape(seq_len, per_device, HD)
        values = heads_in[index, :, 2].reshape(seq_len, per_device, HD)
        grad_out = grad_heads[index].reshape(seq_len, per_device, HD)
        grad_query, grad_keys, grad_values = backward_heads(
            query, keys, values, segment[index], total_list[index], grad_out, block, scale
        )
        stacked = jnp.stack(
            [
                grad_query.reshape(seq_len, head_cols),
                grad_keys.reshape(seq_len, head_cols),
                grad_values.reshape(seq_len, head_cols),
            ],
            axis=1,
        )
        grad_list.append(stacked.astype(jnp.bfloat16))
    grad_proj = lax.all_to_all(jnp.stack(grad_list), "seq", split_axis=1, concat_axis=3, tiled=True)
    grad_proj_rows = grad_proj.reshape(batch * rows, 3 * width)
    grad_in_proj = jnp.dot(normed_low.T, grad_proj_rows, preferred_element_type=jnp.float32)
    grad_proj_wide = grad_proj_rows.astype(jnp.float32)
    grad_bias_query = jnp.sum(grad_proj_wide[:, :width], axis=0)
    grad_bias_value = jnp.sum(grad_proj_wide[:, 2 * width :], axis=0)
    grad_tok, grad_gain_one, grad_shift_one = norm_one_pull(
        jnp.dot(grad_proj_rows, in_full.T, preferred_element_type=jnp.float32)
    )
    grad_tokens = (grad_tok + grad_hidden).astype(jnp.bfloat16).reshape(batch, rows, width)
    shares = (
        lax.psum_scatter(
            grad_in_proj.astype(jnp.bfloat16), "fsdp", scatter_dimension=0, tiled=True
        ).astype(jnp.float32),
        lax.psum_scatter(
            grad_out_proj.astype(jnp.bfloat16), "fsdp", scatter_dimension=0, tiled=True
        ).astype(jnp.float32),
        lax.psum_scatter(
            grad_expand.astype(jnp.bfloat16), "fsdp", scatter_dimension=0, tiled=True
        ).astype(jnp.float32),
        lax.psum_scatter(
            grad_contract.astype(jnp.bfloat16), "fsdp", scatter_dimension=0, tiled=True
        ).astype(jnp.float32),
        lax.psum_scatter(
            grad_gain_one.astype(jnp.bfloat16), "fsdp", scatter_dimension=0, tiled=True
        ).astype(jnp.float32),
        lax.psum_scatter(
            grad_shift_one.astype(jnp.bfloat16), "fsdp", scatter_dimension=0, tiled=True
        ).astype(jnp.float32),
        lax.psum_scatter(
            grad_bias_query.astype(jnp.bfloat16), "fsdp", scatter_dimension=0, tiled=True
        ).astype(jnp.float32),
        lax.psum_scatter(
            grad_bias_value.astype(jnp.bfloat16), "fsdp", scatter_dimension=0, tiled=True
        ).astype(jnp.float32),
        lax.psum_scatter(
            grad_bias_attention.astype(jnp.bfloat16), "fsdp", scatter_dimension=0, tiled=True
        ).astype(jnp.float32),
        lax.psum_scatter(
            grad_gain_two.astype(jnp.bfloat16), "fsdp", scatter_dimension=0, tiled=True
        ).astype(jnp.float32),
        lax.psum_scatter(
            grad_shift_two.astype(jnp.bfloat16), "fsdp", scatter_dimension=0, tiled=True
        ).astype(jnp.float32),
        lax.psum_scatter(
            grad_bias_expand.astype(jnp.bfloat16), "fsdp", scatter_dimension=0, tiled=True
        ).astype(jnp.float32),
        lax.psum_scatter(
            grad_bias_contract.astype(jnp.bfloat16), "fsdp", scatter_dimension=0, tiled=True
        ).astype(jnp.float32),
    )
    totals = (
        lax.psum(shares[0].astype(jnp.bfloat16), "seq").astype(jnp.float32),
        lax.psum(shares[1].astype(jnp.bfloat16), "seq").astype(jnp.float32),
        lax.psum(shares[2].astype(jnp.bfloat16), "seq").astype(jnp.float32),
        lax.psum(shares[3].astype(jnp.bfloat16), "seq").astype(jnp.float32),
        lax.psum(shares[4].astype(jnp.bfloat16), "seq").astype(jnp.float32),
        lax.psum(shares[5].astype(jnp.bfloat16), "seq").astype(jnp.float32),
        lax.psum(shares[6].astype(jnp.bfloat16), "seq").astype(jnp.float32),
        lax.psum(shares[7].astype(jnp.bfloat16), "seq").astype(jnp.float32),
        lax.psum(shares[8].astype(jnp.bfloat16), "seq").astype(jnp.float32),
        lax.psum(shares[9].astype(jnp.bfloat16), "seq").astype(jnp.float32),
        lax.psum(shares[10].astype(jnp.bfloat16), "seq").astype(jnp.float32),
        lax.psum(shares[11].astype(jnp.bfloat16), "seq").astype(jnp.float32),
        lax.psum(shares[12].astype(jnp.bfloat16), "seq").astype(jnp.float32),
    )
    return (
        layer_out,
        grad_tokens,
        totals[4],
        totals[5],
        totals[0],
        totals[6],
        totals[7],
        totals[1],
        totals[8],
        totals[9],
        totals[10],
        totals[2],
        totals[11],
        totals[3],
        totals[12],
    )


MESH = pl.DeviceIdType.MESH
BF = jnp.bfloat16
F32 = jnp.float32
NEG = -1e30
GELU_A = math.sqrt(2.0 / math.pi)
GELU_B = 0.044715


def dot_nn(a, b):
    return lax.dot_general(a, b, (((1,), (0,)), ((), ())), preferred_element_type=F32)


def dot_nt(a, b):
    return lax.dot_general(a, b, (((1,), (1,)), ((), ())), preferred_element_type=F32)


def dot_tn(a, b):
    return lax.dot_general(a, b, (((0,), (0,)), ((), ())), preferred_element_type=F32)


def normalize(v):
    mean = jnp.mean(v, axis=-1, keepdims=True)
    centred = v - mean
    var = jnp.mean(centred * centred, axis=-1, keepdims=True)
    rstd = lax.rsqrt(var + norm_eps)
    return centred * rstd, rstd


def normalize_back(grad, gain, hat, rstd):
    g = grad * gain
    return rstd * (
        g
        - jnp.mean(g, axis=-1, keepdims=True)
        - hat * jnp.mean(g * hat, axis=-1, keepdims=True)
    )


def col_sum(v):
    return jnp.sum(v, axis=0, keepdims=True)


def layer_kernel(
    po, gl, tok, cot, win, wout, wexp, wcon, v0, v1, v2, v3, v4, v5, v6, v7, v8,
    lo, gt, h_in, h_out, h_e, h_c, g_sm,
    g_in, g_out, g_e, g_c,
    wi_a, wo_a, we_a, wc_a, sm_a, vec, ebv, lane_mask,
    x_a, e_a, a_a, qkv, bias, p0, p1, p2, p3, o_a, h_own, b_a, g_a, du_a,
    part, db, part_r, db_r, dr_a, dh_own, do_a, dd, acc_k, acc_v, stage,
    vec_g, eb_g,
    gi_acc,
    st_c, st_e, st_o, st_i, rh_c, ry_c, ry_e, ry_o, ry_i,
    rz_c, rz_e, rz_o, rz_i, xb_c, xb_e, xb_o, xb_i,
    rx_c, rx_e, rx_o, rx_i, fc_c, fc_e, fc_o, fc_i, rc_c, rc_e, rc_o, rc_i,
    st_s, rz_s, rx_s, sv_s, sv_r, sw_s, sw_r, su_s, su_r,
    in_s, gr_s, ag_s, ag_r, ax_s, ax_r, tk_s, tk_r, loc, ex_s, ex_r, rs_s, rs_r, cx_s, cx_r, out_s, out_r,
):
    f = lax.axis_index("fsdp")
    s = lax.axis_index("seq")
    z = f // 2
    y = f % 2
    x = s // 2
    c = s % 2
    dev_y = (z * 2 + 1 - y, s)
    dev_x = (f, (1 - x) * 2 + c)
    dev_c = (f, x * 2 + 1 - c)
    chunks, rows, width = x_a.shape
    length = chunks * rows

    def dev_z(zo):
        return (zo * 2 + y, s)

    def rcopy(src, dst, ssem, rsem, dev):
        return pltpu.make_async_remote_copy(
            src_ref=src, dst_ref=dst, send_sem=ssem, recv_sem=rsem, device_id=dev, device_id_type=MESH
        )

    def slot(zz, yy, at=z):
        return ((zz + at) % 2) * 4 + (zz // 2) * 2 + yy

    def owner(b):
        return 2 * ((z + b // 4) % 2 + 2 * ((b % 4) // 2)) + b % 2

    def flip(v, d):
        for bit in (1, 2, 4):
            if d & bit:
                v = v + bit - 2 * bit * ((v // bit) % 2)
        return v

    barrier = pltpu.get_barrier_semaphore()
    for d in range(1, 8):
        pl.semaphore_signal(barrier, inc=1, device_id=(flip(f, d), s), device_id_type=MESH)
    for d in range(1, 4):
        pl.semaphore_signal(barrier, inc=1, device_id=(f, flip(s, d)), device_id_type=MESH)

    def at_col(ref, col):
        return ref.at[:, pl.ds(pl.multiple_of(col, 128), 128)]

    loads = []
    for pr in range(2):
        for part_i in range(3):
            dst = wi_a.at[pr, f, :, part_i * 128 : part_i * 128 + 128]
            loads.append((at_col(win, part_i * width + c * 256 + pr * 128), dst))
    loads.append((wcon.at[pl.ds(pl.multiple_of(c * 128, 128), 128), :], wc_a.at[slot(z, y)]))
    for b in range(8):
        dst = we_a.at[b // 4, f, :, (b % 4) * 128 : (b % 4) * 128 + 128]
        loads.append((at_col(wexp, owner(b) * 256 + c * 128), dst))
    loads.append((wout, wo_a.at[f]))
    loads = [pltpu.make_async_copy(src, dst, in_s.at[i]) for i, (src, dst) in enumerate(loads)]
    for cp in loads:
        cp.start()
    sm_a[f] = jnp.zeros((16, 128), F32)
    for i, ref in enumerate((v0, v1, v2, v3, v4, v5, v6, v7)):
        sm_a[f, i : i + 1, 0:64] = ref[...].astype(F32).reshape(1, 64)
    eb = v8[...].astype(F32)
    sm_a[f, 8:9, :] = eb[0:128].reshape(1, 128)
    sm_a[f, 9:10, :] = eb[128:256].reshape(1, 128)
    for cp in loads:
        cp.wait()
    pl.semaphore_wait(barrier, 10)
    step = [0]
    actions = {}

    def point():
        for name in SCHEDULE[step[0]]:
            key, _, rest = name.partition(":")
            actions[key](*[int(v) for v in rest.split(".") if v])
        step[0] += 1

    col_c = pl.multiple_of(c * 256, 256)

    def view(g, zz, yy, half, at=z):
        o = zz * 2 + yy
        if g in (1, 2):
            return wi_a.at[g - 1, o]
        if g == 3:
            return wc_a.at[slot(zz, yy, at), pl.ds(pl.multiple_of(half * 64, 64), 64), :]
        if g == 5:
            return wo_a.at[o, :, pl.ds(col_c, 256)]
        return we_a.at[g // 6, o]

    def ag_copy(g, zz, yy, sem, dev, at=z):
        src = view(g, zz, yy, x)
        if g in (4, 6) and at is not z:
            src = we_a.at[(g // 6 + z + at) % 2, zz * 2 + yy]
        return rcopy(src, view(g, zz, yy, x, at), ag_s.at[g, sem], ag_r.at[g, zz * 2 + yy], dev)

    def ax_copy(zz, yy, sem, half):
        ref = view(3, zz, yy, half)
        return rcopy(ref, ref, ax_s.at[sem], ax_r.at[zz * 2 + yy], dev_x)

    def small_first(d):
        return rcopy(sm_a.at[f], sm_a.at[f], su_s.at[d], su_r.at[f], (flip(f, d), s))

    def ag_start(g):
        if g == 0:
            for d in range(1, 8):
                small_first(d).start()
            return
        for d in (2,) if g == 3 else (1, 3) if g == 7 else (1, 2, 3):
            zo = (z + d) % 4
            ag_copy(3 if g == 7 else g, z, y, d - 1, dev_z(zo), zo).start()
        if g != 7:
            ag_copy(g, z, y, 3, dev_y).start()

    def ag_from_z(g, d):
        zo = (z + d) % 4
        cp = ag_copy(g, zo, y, 3 + d, dev_y)
        cp.wait_recv()
        cp.start()
        if g == 3:
            ax_copy(zo, y, d - 1, x).start()

    def ag_from_y(d):
        zo = (z + d) % 4
        ag_copy(3, zo, 1 - y, 3, dev_y).wait_recv()
        ax_copy(zo, 1 - y, 3 + d, x).start()

    def ag_finish(g):
        if g in (3, 7):
            for d in (0, 2) if g == 3 else (1, 3):
                zo = (z + d) % 4
                if d:
                    ax_copy(zo, y, d - 1, 1 - x).wait_recv()
                ax_copy(zo, 1 - y, 3 + d, 1 - x).wait_recv()
        else:
            for zo in range(4):
                ag_copy(g, zo, 1 - y, 3, dev_y).wait_recv()

    def ag_drain(g):
        for i in range(7):
            ag_copy(g, z, y, i, dev_y).wait_send()
            if g == 3:
                ax_copy(z, y, i, x).wait_send()

    def swap_start(n, src, ref):
        rcopy(src.at[1 - x], ref.at[s], tk_s.at[n, 0], tk_r.at[n, 0], dev_x).start()
        rcopy(src.at[x], ref.at[s], tk_s.at[n, 1], tk_r.at[n, 1], dev_c).start()
        pltpu.make_async_copy(src.at[x], ref.at[s], loc.at[n]).start()

    def swap_forward(n, src, ref):
        k = (1 - x) * 2 + c
        rcopy(src.at[1 - x], ref.at[k], tk_s.at[n, 0], tk_r.at[n, 0], dev_x).wait_recv()
        rcopy(ref.at[k], ref.at[k], tk_s.at[n, 2], tk_r.at[n, 2], dev_c).start()

    def swap_finish(n, src, ref):
        rcopy(ref.at[s], ref.at[s], tk_s.at[n, 2], tk_r.at[n, 2], dev_c).wait_recv()

    def swap_near(n, src, ref):
        pltpu.make_async_copy(src.at[x], ref.at[s], loc.at[n]).wait()
        rcopy(src.at[x], ref.at[s], tk_s.at[n, 1], tk_r.at[n, 1], dev_c).wait_recv()

    def swap_drain(n, src, ref):
        rcopy(src.at[1 - x], ref.at[s], tk_s.at[n, 0], tk_r.at[n, 0], dev_x).wait_send()
        rcopy(src.at[x], ref.at[s], tk_s.at[n, 1], tk_r.at[n, 1], dev_c).wait_send()
        rcopy(ref.at[s], ref.at[s], tk_s.at[n, 2], tk_r.at[n, 2], dev_c).wait_send()

    swaps = ((tok, x_a), (cot, e_a))
    actions["start"] = ag_start
    actions["swap"] = lambda n: swap_start(n, *swaps[n])
    actions["share"] = lambda n: swap_forward(n, *swaps[n])
    actions["az"] = ag_from_z
    actions["ay"] = ag_from_y
    point()

    picked = lax.broadcasted_iota(jnp.int32, gl.shape, 1) == po[x]
    lengths = jnp.sum(jnp.where(picked, gl[...], 0), axis=1, keepdims=True)
    first_end = lengths[0:1, :]
    second_end = first_end + lengths[1:2, :]

    def mask_block(k, carry):
        qp = k * rows + lax.broadcasted_iota(jnp.int32, (rows, length), 0)
        kp = lax.broadcasted_iota(jnp.int32, (rows, length), 1)
        hidden_key = (kp >= first_end) & (kp < second_end) & (qp >= second_end)
        bad = (kp > qp) | hidden_key
        bias[k] = jnp.where(bad, NEG, 0.0).astype(F32)
        return carry

    lax.fori_loop(0, chunks, mask_block, 0)
    lanes = lax.broadcasted_iota(jnp.int32, (8, 128), 1)
    lane_row = lax.broadcasted_iota(jnp.int32, (8, 128), 0)
    lane_mask[...] = jnp.where((lanes < 64) == (lane_row < 1), 1.0, 0.0).astype(F32)
    vec_g[...] = jnp.zeros_like(vec_g)
    eb_g[...] = jnp.zeros_like(eb_g)

    point()
    for d in range(1, 8):
        ff = flip(f, d)
        rcopy(sm_a.at[ff], sm_a.at[ff], su_s.at[d], su_r.at[ff], (ff, s)).wait_recv()
    for r in range(4):
        low_half = sm_a[2 * r, 0:8, :]
        high_half = pltpu.roll(sm_a[2 * r + 1, 0:8, :], 64, 1)
        vec[:, r * 128 : r * 128 + 128] = jnp.where(lanes < 64, low_half, high_half)
    for b in range(8):
        ebv[:, b * 128 : b * 128 + 128] = sm_a[owner(b), pl.ds(8 + c, 1), :]
    swap_near(0, tok, x_a)
    point()
    swap_finish(0, tok, x_a)

    def norm_one(k, carry):
        hat, _ = normalize(x_a[k].astype(F32))
        a_a[k] = (hat * vec[0:1, :] + vec[1:2, :]).astype(BF)
        return carry

    lax.fori_loop(0, chunks, norm_one, 0)
    point()

    def project(pr):
        col = pl.multiple_of(c * 256 + pr * 128, 128)
        w = wi_a[pr].reshape(width, 384)
        for k in range(chunks):
            block = pl.ds(k * rows, rows)
            out = dot_nn(a_a[k], w)
            qkv[pr, block, 0:128] = (out[:, 0:128] + vec[2:3, pl.ds(col, 128)]).astype(BF)
            qkv[pr, block, 128:256] = out[:, 128:256].astype(BF)
            qkv[pr, block, 256:384] = (out[:, 256:384] + vec[3:4, pl.ds(col, 128)]).astype(BF)

    probs = (p0, p1, p2, p3)
    masks = [lane_mask[i : i + 1, :] for i in range(2)]
    masks_low = [m.astype(BF) for m in masks]
    scaled_low = [(m * 0.125).astype(BF) for m in masks]

    def split(v, kinds):
        return [v * m for m in kinds]

    def scores(pr, i):
        span = (i + 1) * rows
        q = qkv[pr, i * rows : i * rows + rows, 0:128]
        k = qkv[pr, 0:span, 128:256]
        return [dot_nt(qm, k) + bias[i, :, 0:span] for qm in split(q, scaled_low)]

    def attend(pr, i, sc):
        span = (i + 1) * rows
        v = qkv[pr, 0:span, 256:384]
        weights = []
        for hh in range(2):
            top = jnp.max(sc[hh], axis=-1, keepdims=True)
            ex = jnp.exp(sc[hh] - top)
            tot = jnp.sum(ex, axis=-1, keepdims=True)
            weights.append((ex * (1.0 / tot)).astype(BF))
            probs[i][pr, hh] = weights[hh]
        out = dot_nn(jnp.concatenate(weights, axis=1), jnp.concatenate(split(v, masks_low), axis=0))
        col = pl.multiple_of(c * 256 + pr * 128, 128)
        o_a[i, :, pl.ds(col, 128)] = out.astype(BF)

    def o_copy(pr):
        col = pl.multiple_of(c * 256 + pr * 128, 128)
        ref = o_a.at[:, :, pl.ds(col, 128)]
        return rcopy(ref, ref, ex_s.at[pr], ex_r.at[pr], dev_c)

    def wo_copy():
        ref = wo_a.at[:, :, pl.ds(col_c, 256)]
        return rcopy(ref, ref, ex_s.at[12], ex_r.at[12], dev_c)

    def wo_start():
        ag_finish(5)
        wo_copy().start()

    actions["wo"] = wo_start
    ag_finish(1)
    project(0)
    point()
    sc = scores(0, 0)
    for i in range(chunks):
        if i < chunks - 1:
            ahead = scores(0, i + 1)
        else:
            ag_finish(2)
            project(1)
            ahead = scores(1, 0)
        attend(0, i, sc)
        sc = ahead
        if i == chunks - 1:
            o_copy(0).start()
        point()
    for i in range(chunks):
        ahead = scores(1, i + 1) if i < chunks - 1 else None
        attend(1, i, sc)
        sc = ahead
        if i == chunks - 1:
            o_copy(1).start()
        point()
    for pr in range(2):
        o_copy(pr).wait_recv()
    ref = wo_a.at[:, :, pl.ds(pl.multiple_of((1 - c) * 256, 256), 256)]
    rcopy(ref, ref, ex_s.at[12], ex_r.at[12], dev_c).wait_recv()

    def b_copy(j):
        ref = b_a.at[c + 2 * j]
        return rcopy(ref, ref, ex_s.at[2 + j], ex_r.at[2 + j], dev_c)

    for j in range(2):
        k = c + 2 * j
        out = dot_nn(o_a[k], wo_a[...].reshape(width, width))
        h = x_a[k].astype(F32) + out + vec[4:5, :]
        h_own[j] = h
        hat, _ = normalize(h)
        b_a[k] = (hat * vec[5:6, :] + vec[6:7, :]).astype(BF)
        b_copy(j).start()
        point()
    swap_near(1, cot, e_a)
    swap_finish(1, cot, e_a)
    ag_finish(3)
    ag_finish(4)
    half = we_a.shape[3]

    def mlp_chunk(h, j, k):
        we = we_a[h].reshape(width, half)
        wc = wc_a[4 * h : 4 * h + 4].reshape(half, width)
        u = dot_nn(b_a[k], we) + ebv[:, h * half : h * half + half]
        u2 = u * u
        th = jnp.tanh(u * (GELU_A + (GELU_A * GELU_B) * u2))
        hf = 0.5 * th + 0.5
        gf = u * hf
        g = gf.astype(BF)
        g_a[h, k] = g
        slope = hf + (gf - gf * hf) * ((2.0 * GELU_A) + (6.0 * GELU_A * GELU_B) * u2)
        du = (slope * dot_nt(e_a[k], wc)).astype(BF)
        du_a[h, k] = du
        eb_g[:, h * half : h * half + half] += col_sum(du.astype(F32))
        new_part = dot_nn(g, wc)
        new_db = dot_nt(du, we)
        if h == 0:
            part[j] = new_part
            db[j] = new_db
        else:
            part[j] += new_part
            db[j] += new_db

    def part_copy(j):
        return rcopy(part.at[j], part_r.at[j - 2], ex_s.at[4 + j - 2], ex_r.at[4 + j - 2], dev_c)

    def db_copy(j):
        return rcopy(db.at[j], db_r.at[j - 2], ex_s.at[6 + j - 2], ex_r.at[6 + j - 2], dev_c)

    def rs_names(g):
        return (
            (st_c, ry_c, rz_c, xb_c, rx_c, fc_c, rc_c),
            tuple(r.at[0] for r in (st_e, ry_e, rz_e, xb_e, rx_e, fc_e, rc_e)),
            tuple(r.at[1] for r in (st_e, ry_e, rz_e, xb_e, rx_e, fc_e, rc_e)),
            (st_o, ry_o, rz_o, xb_o, rx_o, fc_o, rc_o),
            tuple(r.at[0] for r in (st_i, ry_i, rz_i, xb_i, rx_i, fc_i, rc_i)),
            tuple(r.at[1] for r in (st_i, ry_i, rz_i, xb_i, rx_i, fc_i, rc_i)),
        )[g]

    mine = pl.ds(pl.multiple_of(x * 64, 64), 64)
    theirs = pl.ds(pl.multiple_of((1 - x) * 64, 64), 64)

    def con_x(zt):
        return rcopy(st_c.at[:, zt, theirs], rh_c.at[zt], cx_s.at[zt], cx_r.at[zt], dev_x)

    def con_y(zt):
        return rcopy(st_c.at[1 - y, zt, mine], ry_c.at[zt], rs_s.at[0, zt], rs_r.at[0, zt], dev_y)

    def con_z(zt):
        return rcopy(st_c.at[y, zt, mine], rz_c.at[z], rs_s.at[0, 4 + zt], rs_r.at[0, 4 + z], dev_z(zt))

    def con_y_start(d):
        zt = (z + d) % 4
        con_x(zt).wait_recv()
        for yy in range(2):
            st_c[yy, zt, mine] = (st_c[yy, zt, mine].astype(F32) + rh_c[zt, yy].astype(F32)).astype(BF)
        con_y(zt).start()

    def con_z_start(d):
        zt = (z + d) % 4
        con_y(zt).wait_recv()
        st_c[y, zt, mine] = (st_c[y, zt, mine].astype(F32) + ry_c[zt].astype(F32)).astype(BF)
        if d:
            con_z(zt).start()

    def rs_y(g, zo):
        st, ry = rs_names(g)[:2]
        return rcopy(st.at[1 - y, zo], ry.at[zo], rs_s.at[g, zo], rs_r.at[g, zo], dev_y)

    def rs_z(g, zo):
        st, _, rz = rs_names(g)[:3]
        to = g
        if g in (1, 2):
            h = (g - 1 + z + zo) % 2
            rz, to = rz_e.at[h], 1 + h
        return rcopy(st.at[y, zo], rz.at[z], rs_s.at[g, 4 + zo], rs_r.at[to, 4 + z], dev_z(zo))

    def rs_x(g):
        xb, rx = rs_names(g)[3:5]
        return rcopy(xb, rx, rs_s.at[g, 8], rs_r.at[g, 8], dev_x)

    def rs_c(g):
        fc, rc = rs_names(g)[5:7]
        return rcopy(fc, rc, rs_s.at[g, 9], rs_r.at[g, 9], dev_c)

    def rs_y_start(g):
        for d in (1, 2, 3, 0):
            rs_y(g, (z + d) % 4).start()

    def rs_z_start(g, d):
        zo = (z + d) % 4
        st, ry = rs_names(g)[:2]
        rs_y(g, zo).wait_recv()
        st[y, zo] = (st[y, zo].astype(F32) + ry[zo].astype(F32)).astype(st.dtype)
        rs_z(g, zo).start()

    def rs_x_start(g):
        st, ry, rz, xb = rs_names(g)[:4]
        if g == 0:
            total = st_c[y, z, mine].astype(F32)
        else:
            rs_y(g, z).wait_recv()
            total = st[y, z].astype(F32) + ry[z].astype(F32)
        for d in range(1, 4):
            zo = (z + d) % 4
            if g == 0:
                cp = rcopy(st_c.at[y, zo, mine], rz.at[zo], rs_s.at[g, 4 + zo], rs_r.at[g, 4 + zo], dev_z(zo))
            else:
                cp = rcopy(st.at[y, zo], rz.at[zo], rs_s.at[g, 4 + zo], rs_r.at[g, 4 + zo], dev_z(zo))
            cp.wait_recv()
            total = total + rz[zo].astype(F32)
        xb[...] = total.astype(xb.dtype)
        rs_x(g).start()

    def write_out(g, side, value):
        if g == 0:
            g_c[pl.ds(pl.multiple_of(side * 128, 128), 128), :] = value
        elif g in (1, 2):
            for b in range(4):
                col = pl.multiple_of(owner((g - 1) * 4 + b) * 256 + side * 128, 128)
                g_e[:, pl.ds(col, 128)] = value[:, b * 128 : b * 128 + 128]
        elif g == 3:
            g_out[:, pl.ds(pl.multiple_of(side * 256, 256), 256)] = value
        else:
            for part_i in range(3):
                col = pl.multiple_of(part_i * width + side * 256 + (g - 4) * 128, 128)
                g_in[:, pl.ds(col, 128)] = value[:, part_i * 128 : part_i * 128 + 128]

    def rs_c_start(g):
        xb, rx, fc = rs_names(g)[3:6]
        rs_x(g).wait_recv()
        if g == 0:
            fc[mine] = xb[...].astype(F32)
            fc[theirs] = rx[...].astype(F32)
        else:
            fc[...] = xb[...].astype(F32) + rx[...].astype(F32)
        rs_c(g).start()
        write_out(g, c, fc[...])

    def rs_finish(g):
        fc, rc = rs_names(g)[5:7]
        rs_c(g).wait_recv()
        write_out(g, 1 - c, rc[...])
        written.append(g)
        if g not in pairs or pairs[g] in written:
            grad_copy(g).start()

    written = []
    pairs = {1: 2, 2: 1, 4: 5, 5: 4}

    def grad_copy(g):
        src, dst = ((g_c, h_c), (g_e, h_e), (g_e, h_e), (g_out, h_out), (g_in, h_in), (g_in, h_in))[g]
        return pltpu.make_async_copy(src, dst, gr_s.at[(0, 1, 1, 2, 3, 3)[g]])

    def rs_drain(g):
        for d in range(4):
            zo = (z + d) % 4
            if g == 0:
                con_x(zo).wait_send()
                con_y(zo).wait_send()
            else:
                rs_y(g, zo).wait_send()
            if d:
                (con_z(zo) if g == 0 else rs_z(g, zo)).wait_send()
        rs_x(g).wait_send()
        rs_c(g).wait_send()

    def grad_con(d):
        zt = (z + d) % 4
        col = pl.ds(pl.multiple_of((zt // 2) * 256, 256), 256)
        out = dot_tn(g_a[d % 2, :, :, col].reshape(length, 256), e_a[...].reshape(length, width))
        st_c[0, zt] = out[0:128].astype(BF)
        st_c[1, zt] = out[128:256].astype(BF)
        con_x(zt).start()

    def grad_exp(h):
        out = dot_tn(b_a[...].reshape(length, width), du_a[h].reshape(length, half))
        for ff in range(8):
            st_e[h, ff % 2, ff // 2] = out[ff * 64 : ff * 64 + 64].astype(BF)
        rs_y_start(1 + h)

    actions["cy"] = con_y_start
    actions["cz"] = con_z_start
    actions["rz"] = rs_z_start
    actions["rx"] = rs_x_start
    actions["rc"] = rs_c_start
    actions["rf"] = rs_finish
    for j in (0, 1, 2, 3):
        if j >= 2:
            ref = b_a.at[1 - c + 2 * (j - 2)]
            rcopy(ref, ref, ex_s.at[j], ex_r.at[j], dev_c).wait_recv()
        mlp_chunk(0, j, (c + 2 * j) if j < 2 else (1 - c) + 2 * (j - 2))
        point()
    grad_con(2)
    point()
    grad_con(0)
    point()
    grad_exp(0)
    point()
    ag_finish(7)
    ag_finish(6)
    for j in (2, 3, 0, 1):
        mlp_chunk(1, j, (c + 2 * j) if j < 2 else (1 - c) + 2 * (j - 2))
        if j >= 2:
            part_copy(j).start()
            db_copy(j).start()
        point()
    grad_con(1)
    point()
    grad_con(3)
    point()
    grad_exp(1)
    point()

    def send_rows(n, ref, out):
        far = rcopy(stage.at[n, 1 - x], out.at[x], out_s.at[n, 0], out_r.at[n], dev_x)
        near = pltpu.make_async_copy(stage.at[n, x], out.at[x], out_s.at[n, 1])
        return far, near

    def dr_copy(j):
        ref = dr_a.at[c + 2 * j]
        return rcopy(ref, ref, ex_s.at[8 + j], ex_r.at[8 + j], dev_c)

    for j in range(2):
        k = c + 2 * j
        h = h_own[j]
        e = e_a[k].astype(F32)
        rcopy(db.at[j + 2], db_r.at[j], ex_s.at[6 + j], ex_r.at[6 + j], dev_c).wait_recv()
        grad_b = db[j] + db_r[j]
        hat, rstd = normalize(h)
        dh = e + normalize_back(grad_b, vec[5:6, :], hat, rstd)
        dh_own[j] = dh
        dr = dh.astype(BF)
        dr_a[k] = dr
        dr_copy(j).start()
        vec_g[4:5, :] += col_sum(dr.astype(F32))
        vec_g[5:6, :] += col_sum(grad_b * hat)
        vec_g[6:7, :] += col_sum(grad_b)
        vec_g[7:8, :] += col_sum(e)
        rcopy(part.at[j + 2], part_r.at[j], ex_s.at[4 + j], ex_r.at[4 + j], dev_c).wait_recv()
        stage[0, j] = (h + part[j] + part_r[j] + vec[7:8, :]).astype(BF)
        point()
    for cp in send_rows(0, stage, lo):
        cp.start()

    head_row = pl.multiple_of(c * 4, 4)

    def grad_mixed(k):
        w = wo_a[pl.ds(head_row, 4)].reshape(256, width)
        do_a[k] = dot_nt(dr_a[k], w).astype(BF)

    for j in range(2):
        grad_mixed(c + 2 * j)
    point()
    for j in range(2):
        ref = dr_a.at[1 - c + 2 * j]
        rcopy(ref, ref, ex_s.at[8 + j], ex_r.at[8 + j], dev_c).wait_recv()
        grad_mixed(1 - c + 2 * j)
    point()
    out = dot_tn(o_a[...].reshape(length, width), dr_a[:, :, pl.ds(col_c, 256)].reshape(length, 256))
    for ff in range(8):
        st_o[ff % 2, ff // 2] = out[ff * 64 : ff * 64 + 64].astype(BF)
    rs_y_start(3)
    point()

    def grad_probs(pr, i):
        v = qkv[pr, 0 : (i + 1) * rows, 256:384]
        do = do_a[i, :, pr * 128 : pr * 128 + 128]
        return [dot_nt(dom, v) for dom in split(do, masks_low)]

    def attend_back(pr, i, gp):
        span = (i + 1) * rows
        block = pl.ds(i * rows, rows)
        q = qkv[pr, block, 0:128]
        k = qkv[pr, 0:span, 128:256]
        do = do_a[i, :, pr * 128 : pr * 128 + 128]
        ds = []
        for hh in range(2):
            pf = probs[i][pr, hh].astype(F32)
            t = pf * gp[hh]
            inner = jnp.sum(t, axis=-1, keepdims=True)
            ds.append((t - pf * inner).astype(BF))
        both = jnp.concatenate([probs[i][pr, 0], probs[i][pr, 1]], axis=0)
        grad_v = dot_tn(both, jnp.concatenate(split(do, masks_low), axis=0))
        grad_k = dot_tn(jnp.concatenate(ds, axis=0), jnp.concatenate(split(q, scaled_low), axis=0))
        if i == chunks - 1:
            acc_v[...] = grad_v
            acc_k[...] = grad_k
        else:
            acc_v[0:span] += grad_v
            acc_k[0:span] += grad_k
        grad_q = dot_nn(
            jnp.concatenate(ds, axis=1), jnp.concatenate(split(k, scaled_low), axis=0)
        ).astype(BF)
        grad_k = acc_k[block].astype(BF)
        grad_v = acc_v[block].astype(BF)
        dd[pr, block, 0:128] = grad_q
        dd[pr, block, 128:256] = grad_k
        dd[pr, block, 256:384] = grad_v
        col = pl.multiple_of(c * 256 + pr * 128, 128)
        vec_g[2:3, pl.ds(col, 128)] += col_sum(grad_q.astype(F32))
        vec_g[3:4, pl.ds(col, 128)] += col_sum(grad_v.astype(F32))

    def grad_in(pr, out):
        for ff in range(8):
            st_i[pr, ff % 2, ff // 2] = out[ff * 64 : ff * 64 + 64].astype(BF)
        rs_y_start(4 + pr)

    def da_copy(j):
        return rcopy(part.at[j], db_r.at[j - 2], ex_s.at[10 + j - 2], ex_r.at[10 + j - 2], dev_c)

    def grad_a(i):
        total = None
        for pr in range(2):
            p = dot_nt(dd[pr, i * rows : i * rows + rows, :], wi_a[pr].reshape(width, 384))
            total = p if total is None else total + p
        other = (i + c) % 2
        part[i // 2 + 2 * other] = total

        @pl.when(other == 1)
        def _():
            da_copy(2 + i // 2).start()

    def norm_one_back(j):
        k = c + 2 * j
        rcopy(part.at[j + 2], db_r.at[j], ex_s.at[10 + j], ex_r.at[10 + j], dev_c).wait_recv()
        grad = part[j] + db_r[j]
        hat, rstd = normalize(x_a[k].astype(F32))
        vec_g[0:1, :] += col_sum(grad * hat)
        vec_g[1:2, :] += col_sum(grad)
        stage[1, j] = (dh_own[j] + normalize_back(grad, vec[0:1, :], hat, rstd)).astype(BF)

    order = [(pr, i) for pr in range(2) for i in range(chunks - 1, -1, -1)]
    gp = grad_probs(*order[0])
    for n, (pr, i) in enumerate(order):
        ahead = grad_probs(*order[n + 1]) if n < 7 else None
        attend_back(pr, i, gp)
        gp = ahead
        if pr == 0 and i == 0:
            grad_in(0, dot_tn(a_a[...].reshape(length, width), dd[0]))
            for j in range(2, 4):
                part_copy(j).wait_send()
        if pr == 1:
            block = dot_tn(a_a[i], dd[1, i * rows : i * rows + rows, :])
            if i == chunks - 1:
                gi_acc[...] = block
            elif i > 0:
                gi_acc[...] += block
            else:
                grad_in(1, gi_acc[...] + block)
                point()
            grad_a(i)
            if i < 2:
                norm_one_back(i)
        point()
    for cp in send_rows(1, stage, gt):
        cp.start()

    for r in range(4):
        tile = vec_g[:, r * 128 : r * 128 + 128]
        rolled = pltpu.roll(tile, 64, 1)
        for yy in range(2):
            ff = 2 * r + yy
            st_s[ff, 0:8, :] = tile if yy == 0 else rolled
            st_s[ff, 8:16, :] = jnp.zeros((8, 128), F32)
            lane = pl.multiple_of(slot(r, yy) * 128, 128)
            st_s[ff, pl.ds(8 + c, 1), :] = eb_g[:, pl.ds(lane, 128)]

    def small_copy(d):
        ff = flip(f, d)
        return rcopy(st_s.at[ff], rz_s.at[f], sv_s.at[d], sv_r.at[f], (ff, s))

    def small_last(d):
        ss = flip(s, d)
        return rcopy(rx_s.at[s], rx_s.at[s], sw_s.at[d], sw_r.at[s], (f, ss))

    for d in range(1, 8):
        small_copy(d).start()

    def small_sum():
        rz_s[f] = st_s[f]
        for d in range(1, 8):
            ff = flip(f, d)
            rcopy(st_s.at[ff], rz_s.at[ff], sv_s.at[d], sv_r.at[ff], (ff, s)).wait_recv()
        total = rz_s[0]
        for ff in range(1, 8):
            total = total + rz_s[ff]
        rx_s[s] = total
        for d in range(1, 4):
            small_last(d).start()

    def small_end():
        for d in range(1, 4):
            ss = flip(s, d)
            rcopy(rx_s.at[ss], rx_s.at[ss], sw_s.at[d], sw_r.at[ss], (f, ss)).wait_recv()
        g_sm[...] = (rx_s[0] + rx_s[1]) + (rx_s[2] + rx_s[3])

    actions["sb"] = small_sum
    actions["sc"] = small_end
    point()
    for n, out in ((0, lo), (1, gt)):
        far, near = send_rows(n, stage, out)
        near.wait()
        far.wait_send()
        rcopy(stage.at[n, 1 - x], out.at[1 - x], out_s.at[n, 0], out_r.at[n], dev_x).wait_recv()
    for g in (0, 1, 3, 4):
        grad_copy(g).wait()
    for g in range(1, 7):
        ag_drain(g)
    swap_drain(0, tok, x_a)
    swap_drain(1, cot, e_a)
    wo_copy().wait_send()
    for pr in range(2):
        o_copy(pr).wait_send()
    for j in range(2):
        b_copy(j).wait_send()
        dr_copy(j).wait_send()
        db_copy(j + 2).wait_send()
        da_copy(j + 2).wait_send()
    for g in range(6):
        rs_drain(g)
    for d in range(1, 8):
        small_copy(d).wait_send()
        small_first(d).wait_send()
    for d in range(1, 4):
        small_last(d).wait_send()


SCHEDULE = (
    (),
    ("start:1", "start:2", "swap:0", "start:0", "start:3", "start:5", "az:1.3", "az:1.1", "az:1.2", "start:4", "az:2.2", "az:2.3", "start:7", "share:0",),
    ("az:2.1",),
    (),
    ("swap:1", "az:3.2", "start:6", "ay:0",),
    (),
    ("az:5.3", "az:5.2", "az:5.1",),
    (),
    ("az:4.1",),
    (),
    ("az:4.3",),
    (),
    ("share:1", "ay:2", "wo", "az:4.2", "az:3.1", "az:3.3",),
    (),
    (),
    (),
    ("az:6.1", "ay:1", "az:6.3",),
    (),
    ("ay:3", "az:6.2",),
    (),
    (),
    (),
    (),
    ("rz:1.1",),
    (),
    ("cy:2", "rz:1.2",),
    (),
    ("rz:1.3",),
    (),
    (),
    (),
    ("cz:2",),
    (),
    (),
    ("rz:2.2",),
    (),
    ("rz:2.1",),
    ("rz:2.3", "rz:3.2", "cy:3", "rz:3.3",),
    ("cy:1", "rz:3.1",),
    ("rz:4.2", "rx:2", "rz:4.1", "cy:0", "rx:1",),
    ("rz:4.3", "cz:3",),
    (),
    ("cz:1", "rx:3", "rc:1",),
    ("rx:4", "rz:5.1", "rz:5.3", "rz:5.2", "sb", "cz:0", "rx:0", "rx:5", "rc:4", "rc:2", "rf:1", "rc:0", "rc:3", "rf:3", "rf:2", "rc:5", "rf:0", "rf:5", "sc", "rf:4",),
)


def finish_kernel(*refs):
    gs = refs[6]
    outs = refs[7:]
    for i in range(6):
        outs[i][...] = refs[i][...]
    for i in range(8):
        outs[6 + i][...] = gs[i : i + 1, 0 : outs[6 + i].shape[1]]
    outs[14][:, 0:128] = gs[8:9, :]
    outs[14][:, 128:256] = gs[9:10, :]


def fast_shards(
    tokens, placement_order, group_lengths, first_gain, first_shift, attention_in, query_bias,
    value_bias, attention_out, attention_bias, second_gain, second_shift, expand_weight,
    expand_bias, contract_weight, contract_bias, cotangent,
):
    batch, rows, width = tokens.shape
    lanes = first_gain.shape[0]
    chunks = 4
    length = chunks * rows
    half = expand_weight.shape[1] // 4
    vm = pl.BlockSpec(memory_space=pltpu.VMEM)
    sm = pl.BlockSpec(memory_space=pltpu.SMEM)
    hb = pl.BlockSpec(memory_space=pl.ANY)
    V = pltpu.VMEM
    pieces = (((128, width), None), ((64, half), 2), ((64, 256), None), ((64, 384), 2))

    def family(lead, dtype, con=128):
        out = []
        for n, (shape, pairs) in enumerate(pieces):
            if n == 0:
                shape = (con, width)
            pre = () if pairs is None else (pairs,)
            out.append(V(pre + lead + shape, dtype))
        return out

    dma = pltpu.SemaphoreType.DMA
    scratch = [
        V(attention_in.shape, F32), V(attention_out.shape, F32), V(expand_weight.shape, F32),
        V(contract_weight.shape, F32),
        V((2, 8, 64, 384), BF), V((8, 64, width), BF), V((2, 8, 64, half), BF), V((8, 128, width), BF),
        V((8, 16, 128), F32), V((8, width), F32), V((1, 2 * half), F32), V((8, 128), F32),
        V((chunks, rows, width), BF), V((chunks, rows, width), BF), V((chunks, rows, width), BF),
        V((2, length, 384), BF), V((chunks, rows, length), F32),
        V((2, 2, rows, rows), BF), V((2, 2, rows, 2 * rows), BF), V((2, 2, rows, 3 * rows), BF),
        V((2, 2, rows, 4 * rows), BF),
        V((chunks, rows, width), BF), V((2, rows, width), F32), V((chunks, rows, width), BF),
        V((2, chunks, rows, half), BF), V((2, chunks, rows, half), BF),
        V((4, rows, width), F32), V((4, rows, width), F32), V((2, rows, width), F32),
        V((2, rows, width), F32), V((chunks, rows, width), BF), V((2, rows, width), F32),
        V((chunks, rows, 256), BF), V((2, length, 384), BF), V((length, 128), F32),
        V((length, 128), F32), V((2, 2, rows, width), BF), V((8, width), F32), V((1, 2 * half), F32),
    ]
    scratch += [V((width, 384), F32)]
    scratch += family((2, 4), BF) + [V((4, 2, 64, width), BF)] + family((4,), BF, 64)
    scratch += family((4,), BF, 64) + family((), BF, 64) + family((), BF, 64)
    scratch += family((), F32) + family((), F32)
    scratch += [V((8, 16, 128), F32), V((8, 16, 128), F32), V((4, 16, 128), F32)]
    scratch += [dma((8,)), dma((8,)), dma((4,)), dma((4,)), dma((8,)), dma((8,))]
    scratch += [
        dma((16,)), dma((6,)), dma((7, 7)), dma((7, 8)), dma((7,)), dma((8,)), dma((2, 3)), dma((2, 3)), dma((2,)),
        dma((13,)), dma((13,)), dma((7, 10)), dma((7, 10)), dma((4,)), dma((4,)), dma((2, 2)), dma((2,)),
    ]
    grads = (
        jax.ShapeDtypeStruct(tokens.shape, BF),
        jax.ShapeDtypeStruct(tokens.shape, BF),
        jax.ShapeDtypeStruct(attention_in.shape, F32),
        jax.ShapeDtypeStruct(attention_out.shape, F32),
        jax.ShapeDtypeStruct(expand_weight.shape, F32),
        jax.ShapeDtypeStruct(contract_weight.shape, F32),
    )
    outs = pl.pallas_call(
        layer_kernel,
        out_shape=grads + (jax.ShapeDtypeStruct((16, 128), F32),),
        in_specs=[sm, vm] + [hb] * 6 + [vm] * 9,
        out_specs=[hb] * 6 + [vm],
        scratch_shapes=scratch,
        compiler_params=pltpu.CompilerParams(
            collective_id=0, has_side_effects=True, vmem_limit_bytes=63 << 20
        ),
    )(
        placement_order, group_lengths.T, tokens, cotangent, attention_in, attention_out,
        expand_weight, contract_weight, first_gain, first_shift, query_bias, value_bias,
        attention_bias, second_gain, second_shift, contract_bias, expand_bias,
    )
    outs = pl.pallas_call(
        finish_kernel,
        out_shape=grads
        + tuple(jax.ShapeDtypeStruct((1, lanes), F32) for _ in range(8))
        + (jax.ShapeDtypeStruct((1, 256), F32),),
        in_specs=[vm] * 7,
        out_specs=[vm] * 15,
    )(*outs)
    layer_out, grad_tokens, g_in, g_out, g_e, g_c = outs[:6]
    v = [item.reshape(-1) for item in outs[6:]]
    return (
        layer_out, grad_tokens, v[0], v[1], g_in, v[2], v[3], g_out,
        v[4], v[5], v[6], g_e, v[8], g_c, v[7],
    )


def solution(mesh):
    in_specs = (
        P("fsdp", "seq", None),
        P("fsdp"),
        P(),
        P("fsdp"),
        P("fsdp"),
        P("fsdp", None),
        P("fsdp"),
        P("fsdp"),
        P("fsdp", None),
        P("fsdp"),
        P("fsdp"),
        P("fsdp"),
        P("fsdp", None),
        P("fsdp"),
        P("fsdp", None),
        P("fsdp"),
        P("fsdp", "seq", None),
    )
    out_specs = (
        P("fsdp", "seq", None),
        P("fsdp", "seq", None),
        P("fsdp"),
        P("fsdp"),
        P("fsdp", None),
        P("fsdp"),
        P("fsdp"),
        P("fsdp", None),
        P("fsdp"),
        P("fsdp"),
        P("fsdp"),
        P("fsdp", None),
        P("fsdp"),
        P("fsdp", None),
        P("fsdp"),
    )
    pick = fast_shards if (mesh.shape["fsdp"], mesh.shape["seq"]) == (8, 4) else shards
    return jax.shard_map(pick, mesh=mesh, in_specs=in_specs, out_specs=out_specs, check_vma=False)
```

```python
import math

import jax
import jax.numpy as jnp
from jax import lax
from jax.experimental import pallas as pl
from jax.experimental.pallas import tpu as pltpu
from jax.sharding import PartitionSpec as P

HD = 64


norm_eps = 1e-05


def layer_norm(values, gain, shift):
    mean = jnp.mean(values, axis=-1, keepdims=True)
    centred = values - mean
    variance = jnp.mean(centred * centred, axis=-1, keepdims=True)
    return centred * lax.rsqrt(variance + norm_eps) * gain + shift


def gelu_tanh(values):
    return jax.nn.gelu(values, approximate=True)


def masked_scores(query_blk, keys, start, segment, scale):
    count = query_blk.shape[0]
    scores = jnp.einsum("qhd,khd->hqk", query_blk, keys, preferred_element_type=jnp.float32) * scale
    query_pos = start + jnp.arange(count, dtype=jnp.int32)
    key_pos = jnp.arange(keys.shape[0], dtype=jnp.int32)
    query_seg = lax.dynamic_slice_in_dim(segment, start, count, 0)
    allowed = (key_pos[None, :] <= query_pos[:, None]) & (
        (segment[None, :] == query_seg[:, None]) | (segment[None, :] == 0)
    )
    return jnp.where(allowed[None], scores, -1e30)


def forward_heads(query, keys, values, segment, block, scale):
    starts = jnp.arange(query.shape[0] // block, dtype=jnp.int32) * block

    def forward_one_block(start):
        query_blk = lax.dynamic_slice_in_dim(query, start, block, 0)
        scores = masked_scores(query_blk, keys, start, segment, scale)
        top = jnp.max(scores, axis=-1, keepdims=True)
        raised = jnp.exp(scores - top)
        total = jnp.sum(raised, axis=-1, keepdims=True)
        weights = (raised / total).astype(jnp.bfloat16)
        mixed = jnp.einsum("hqk,khd->qhd", weights, values, preferred_element_type=jnp.float32)
        return (mixed.astype(jnp.bfloat16), (top + jnp.log(total))[..., 0])

    return lax.map(forward_one_block, starts)


def backward_heads(query, keys, values, segment, log_total, grad_out, block, scale):
    count = query.shape[0] // block
    starts = jnp.arange(count, dtype=jnp.int32) * block
    grad_blocks = grad_out.reshape((count, block) + grad_out.shape[1:])

    def backward_one_block(carry, inputs):
        grad_keys, grad_values = carry
        start, total_blk, grad_blk = inputs
        query_blk = lax.dynamic_slice_in_dim(query, start, block, 0)
        scores = masked_scores(query_blk, keys, start, segment, scale)
        probs = jnp.exp(scores - total_blk[:, :, None])
        grad_probs = jnp.einsum(
            "qhd,khd->hqk", grad_blk, values, preferred_element_type=jnp.float32
        )
        inner = jnp.sum(probs * grad_probs, axis=-1, keepdims=True)
        grad_scores = (probs * (grad_probs - inner)).astype(jnp.bfloat16)
        grad_query = (
            jnp.einsum("hqk,khd->qhd", grad_scores, keys, preferred_element_type=jnp.float32)
            * scale
        )
        grad_keys = (
            grad_keys
            + jnp.einsum("hqk,qhd->khd", grad_scores, query_blk, preferred_element_type=jnp.float32)
            * scale
        )
        grad_values = grad_values + jnp.einsum(
            "hqk,qhd->khd", probs.astype(jnp.bfloat16), grad_blk, preferred_element_type=jnp.float32
        )
        return ((grad_keys, grad_values), grad_query)

    zeros = jnp.zeros(keys.shape, jnp.float32)
    (grad_keys, grad_values), grad_query = lax.scan(
        backward_one_block, (zeros, zeros), (starts, log_total, grad_blocks)
    )
    return (grad_query.reshape(query.shape), grad_keys, grad_values)


def shards(
    tokens,
    placement_order,
    group_lengths,
    first_gain,
    first_shift,
    attention_in,
    query_bias,
    value_bias,
    attention_out,
    attention_bias,
    second_gain,
    second_shift,
    expand_weight,
    expand_bias,
    contract_weight,
    contract_bias,
    cotangent,
):
    batch, rows, width = tokens.shape
    seq_count = lax.axis_size("seq")
    seq_len = rows * seq_count
    block = min(512, seq_len)
    scale = 1.0 / math.sqrt(HD)
    gathered = (
        lax.all_gather(attention_in, "fsdp", axis=0, tiled=True),
        lax.all_gather(attention_out, "fsdp", axis=0, tiled=True),
        lax.all_gather(expand_weight, "fsdp", axis=0, tiled=True),
        lax.all_gather(contract_weight, "fsdp", axis=0, tiled=True),
        lax.all_gather(first_gain, "fsdp", axis=0, tiled=True),
        lax.all_gather(first_shift, "fsdp", axis=0, tiled=True),
        lax.all_gather(query_bias, "fsdp", axis=0, tiled=True),
        lax.all_gather(value_bias, "fsdp", axis=0, tiled=True),
        lax.all_gather(attention_bias, "fsdp", axis=0, tiled=True),
        lax.all_gather(second_gain, "fsdp", axis=0, tiled=True),
        lax.all_gather(second_shift, "fsdp", axis=0, tiled=True),
        lax.all_gather(expand_bias, "fsdp", axis=0, tiled=True),
        lax.all_gather(contract_bias, "fsdp", axis=0, tiled=True),
    )
    in_full, out_full, expand_full, contract_full = (
        gathered[0],
        gathered[1],
        gathered[2],
        gathered[3],
    )
    small = [item.astype(jnp.float32) for item in gathered[4:]]
    (
        gain_one,
        shift_one,
        bias_query,
        bias_value,
        bias_attention,
        gain_two,
        shift_two,
        bias_expand,
        bias_contract,
    ) = small
    groups = group_lengths.shape[0]
    picked = (placement_order[:, None] == jnp.arange(groups, dtype=jnp.int32)[None, :]).astype(
        jnp.int32
    )
    lengths = jnp.sum(picked[:, :, None] * group_lengths[None, :, :], axis=1)
    positions = jnp.arange(seq_len, dtype=jnp.int32)
    first_end = lengths[:, 0:1]
    second_end = first_end + lengths[:, 1:2]
    segment = (positions[None, :] >= first_end).astype(jnp.int32) + (
        positions[None, :] >= second_end
    ).astype(jnp.int32)
    tok_rows = tokens.reshape(batch * rows, width).astype(jnp.float32)
    normed, norm_one_pull = jax.vjp(layer_norm, tok_rows, gain_one, shift_one)
    normed_low = normed.astype(jnp.bfloat16)
    bias_in = jnp.concatenate([bias_query, jnp.zeros((width,), jnp.float32), bias_value])
    projected = (jnp.dot(normed_low, in_full, preferred_element_type=jnp.float32) + bias_in).astype(
        jnp.bfloat16
    )
    heads_in = lax.all_to_all(
        projected.reshape(batch, rows, 3, width), "seq", split_axis=3, concat_axis=1, tiled=True
    )
    head_cols = heads_in.shape[3]
    per_device = head_cols // HD
    mixed_list = []
    total_list = []
    for index in range(batch):
        query = heads_in[index, :, 0].reshape(seq_len, per_device, HD)
        keys = heads_in[index, :, 1].reshape(seq_len, per_device, HD)
        values = heads_in[index, :, 2].reshape(seq_len, per_device, HD)
        mixed_blocks, log_total = forward_heads(query, keys, values, segment[index], block, scale)
        mixed_list.append(mixed_blocks.reshape(seq_len, head_cols))
        total_list.append(log_total)
    mixed = lax.all_to_all(jnp.stack(mixed_list), "seq", split_axis=1, concat_axis=2, tiled=True)
    mixed_rows = mixed.reshape(batch * rows, width)
    hidden = (
        tok_rows
        + jnp.dot(mixed_rows, out_full, preferred_element_type=jnp.float32)
        + bias_attention
    )
    normed_two, norm_two_pull = jax.vjp(layer_norm, hidden, gain_two, shift_two)
    normed_two_low = normed_two.astype(jnp.bfloat16)
    expanded = (
        jnp.dot(normed_two_low, expand_full, preferred_element_type=jnp.float32) + bias_expand
    )
    activated, gelu_pull = jax.vjp(gelu_tanh, expanded)
    activated_low = activated.astype(jnp.bfloat16)
    result = (
        hidden
        + jnp.dot(activated_low, contract_full, preferred_element_type=jnp.float32)
        + bias_contract
    )
    layer_out = result.astype(jnp.bfloat16).reshape(batch, rows, width)
    grad_low = cotangent.reshape(batch * rows, width)
    grad_res = grad_low.astype(jnp.float32)
    grad_contract = jnp.dot(activated_low.T, grad_low, preferred_element_type=jnp.float32)
    grad_bias_contract = jnp.sum(grad_res, axis=0)
    (grad_expanded,) = gelu_pull(
        jnp.dot(grad_low, contract_full.T, preferred_element_type=jnp.float32)
    )
    grad_expanded_low = grad_expanded.astype(jnp.bfloat16)
    grad_expand = jnp.dot(normed_two_low.T, grad_expanded_low, preferred_element_type=jnp.float32)
    grad_bias_expand = jnp.sum(grad_expanded_low.astype(jnp.float32), axis=0)
    grad_hidden, grad_gain_two, grad_shift_two = norm_two_pull(
        jnp.dot(grad_expanded_low, expand_full.T, preferred_element_type=jnp.float32)
    )
    grad_hidden = grad_hidden + grad_res
    grad_branch_low = grad_hidden.astype(jnp.bfloat16)
    grad_out_proj = jnp.dot(mixed_rows.T, grad_branch_low, preferred_element_type=jnp.float32)
    grad_bias_attention = jnp.sum(grad_branch_low.astype(jnp.float32), axis=0)
    grad_mixed = jnp.dot(grad_branch_low, out_full.T, preferred_element_type=jnp.float32).astype(
        jnp.bfloat16
    )
    grad_heads = lax.all_to_all(
        grad_mixed.reshape(batch, rows, width), "seq", split_axis=2, concat_axis=1, tiled=True
    )
    grad_list = []
    for index in range(batch):
        query = heads_in[index, :, 0].reshape(seq_len, per_device, HD)
        keys = heads_in[index, :, 1].reshape(seq_len, per_device, HD)
        values = heads_in[index, :, 2].reshape(seq_len, per_device, HD)
        grad_out = grad_heads[index].reshape(seq_len, per_device, HD)
        grad_query, grad_keys, grad_values = backward_heads(
            query, keys, values, segment[index], total_list[index], grad_out, block, scale
        )
        stacked = jnp.stack(
            [
                grad_query.reshape(seq_len, head_cols),
                grad_keys.reshape(seq_len, head_cols),
                grad_values.reshape(seq_len, head_cols),
            ],
            axis=1,
        )
        grad_list.append(stacked.astype(jnp.bfloat16))
    grad_proj = lax.all_to_all(jnp.stack(grad_list), "seq", split_axis=1, concat_axis=3, tiled=True)
    grad_proj_rows = grad_proj.reshape(batch * rows, 3 * width)
    grad_in_proj = jnp.dot(normed_low.T, grad_proj_rows, preferred_element_type=jnp.float32)
    grad_proj_wide = grad_proj_rows.astype(jnp.float32)
    grad_bias_query = jnp.sum(grad_proj_wide[:, :width], axis=0)
    grad_bias_value = jnp.sum(grad_proj_wide[:, 2 * width :], axis=0)
    grad_tok, grad_gain_one, grad_shift_one = norm_one_pull(
        jnp.dot(grad_proj_rows, in_full.T, preferred_element_type=jnp.float32)
    )
    grad_tokens = (grad_tok + grad_hidden).astype(jnp.bfloat16).reshape(batch, rows, width)
    shares = (
        lax.psum_scatter(
            grad_in_proj.astype(jnp.bfloat16), "fsdp", scatter_dimension=0, tiled=True
        ).astype(jnp.float32),
        lax.psum_scatter(
            grad_out_proj.astype(jnp.bfloat16), "fsdp", scatter_dimension=0, tiled=True
        ).astype(jnp.float32),
        lax.psum_scatter(
            grad_expand.astype(jnp.bfloat16), "fsdp", scatter_dimension=0, tiled=True
        ).astype(jnp.float32),
        lax.psum_scatter(
            grad_contract.astype(jnp.bfloat16), "fsdp", scatter_dimension=0, tiled=True
        ).astype(jnp.float32),
        lax.psum_scatter(
            grad_gain_one.astype(jnp.bfloat16), "fsdp", scatter_dimension=0, tiled=True
        ).astype(jnp.float32),
        lax.psum_scatter(
            grad_shift_one.astype(jnp.bfloat16), "fsdp", scatter_dimension=0, tiled=True
        ).astype(jnp.float32),
        lax.psum_scatter(
            grad_bias_query.astype(jnp.bfloat16), "fsdp", scatter_dimension=0, tiled=True
        ).astype(jnp.float32),
        lax.psum_scatter(
            grad_bias_value.astype(jnp.bfloat16), "fsdp", scatter_dimension=0, tiled=True
        ).astype(jnp.float32),
        lax.psum_scatter(
            grad_bias_attention.astype(jnp.bfloat16), "fsdp", scatter_dimension=0, tiled=True
        ).astype(jnp.float32),
        lax.psum_scatter(
            grad_gain_two.astype(jnp.bfloat16), "fsdp", scatter_dimension=0, tiled=True
        ).astype(jnp.float32),
        lax.psum_scatter(
            grad_shift_two.astype(jnp.bfloat16), "fsdp", scatter_dimension=0, tiled=True
        ).astype(jnp.float32),
        lax.psum_scatter(
            grad_bias_expand.astype(jnp.bfloat16), "fsdp", scatter_dimension=0, tiled=True
        ).astype(jnp.float32),
        lax.psum_scatter(
            grad_bias_contract.astype(jnp.bfloat16), "fsdp", scatter_dimension=0, tiled=True
        ).astype(jnp.float32),
    )
    totals = (
        lax.psum(shares[0].astype(jnp.bfloat16), "seq").astype(jnp.float32),
        lax.psum(shares[1].astype(jnp.bfloat16), "seq").astype(jnp.float32),
        lax.psum(shares[2].astype(jnp.bfloat16), "seq").astype(jnp.float32),
        lax.psum(shares[3].astype(jnp.bfloat16), "seq").astype(jnp.float32),
        lax.psum(shares[4].astype(jnp.bfloat16), "seq").astype(jnp.float32),
        lax.psum(shares[5].astype(jnp.bfloat16), "seq").astype(jnp.float32),
        lax.psum(shares[6].astype(jnp.bfloat16), "seq").astype(jnp.float32),
        lax.psum(shares[7].astype(jnp.bfloat16), "seq").astype(jnp.float32),
        lax.psum(shares[8].astype(jnp.bfloat16), "seq").astype(jnp.float32),
        lax.psum(shares[9].astype(jnp.bfloat16), "seq").astype(jnp.float32),
        lax.psum(shares[10].astype(jnp.bfloat16), "seq").astype(jnp.float32),
        lax.psum(shares[11].astype(jnp.bfloat16), "seq").astype(jnp.float32),
        lax.psum(shares[12].astype(jnp.bfloat16), "seq").astype(jnp.float32),
    )
    return (
        layer_out,
        grad_tokens,
        totals[4],
        totals[5],
        totals[0],
        totals[6],
        totals[7],
        totals[1],
        totals[8],
        totals[9],
        totals[10],
        totals[2],
        totals[11],
        totals[3],
        totals[12],
    )


MESH = pl.DeviceIdType.MESH
BF = jnp.bfloat16
F32 = jnp.float32
NEG = -1e30
GELU_A = math.sqrt(2.0 / math.pi)
GELU_B = 0.044715


def dot_nn(a, b):
    return lax.dot_general(a, b, (((1,), (0,)), ((), ())), preferred_element_type=F32)


def dot_nt(a, b):
    return lax.dot_general(a, b, (((1,), (1,)), ((), ())), preferred_element_type=F32)


def dot_tn(a, b):
    return lax.dot_general(a, b, (((0,), (0,)), ((), ())), preferred_element_type=F32)


def normalize(v):
    mean = jnp.mean(v, axis=-1, keepdims=True)
    centred = v - mean
    var = jnp.mean(centred * centred, axis=-1, keepdims=True)
    rstd = lax.rsqrt(var + norm_eps)
    return centred * rstd, rstd


def normalize_back(grad, gain, hat, rstd):
    g = grad * gain
    return rstd * (
        g
        - jnp.mean(g, axis=-1, keepdims=True)
        - hat * jnp.mean(g * hat, axis=-1, keepdims=True)
    )


def col_sum(v):
    return jnp.sum(v, axis=0, keepdims=True)


def layer_kernel(
    po, gl, tok, cot, win, wout, wexp, wcon, v0, v1, v2, v3, v4, v5, v6, v7, v8,
    lo, gt, h_in, h_out, h_e, h_c, g_sm,
    g_in, g_out, g_e, g_c,
    wi_a, wo_a, we_a, wc_a, sm_a, vec, ebv, lane_mask,
    x_a, e_a, a_a, qkv, bias, p0, p1, p2, p3, o_a, h_own, b_a, g_a, du_a,
    part, db, part_r, db_r, dr_a, dh_own, do_a, dd, acc_k, acc_v, stage,
    vec_g, eb_g,
    gi_acc,
    st_c, st_e, st_o, st_i, rh_c, ry_c, ry_e, ry_o, ry_i,
    rz_c, rz_e, rz_o, rz_i, xb_c, xb_e, xb_o, xb_i,
    rx_c, rx_e, rx_o, rx_i, fc_c, fc_e, fc_o, fc_i, rc_c, rc_e, rc_o, rc_i,
    st_s, rz_s, rx_s, sv_s, sv_r, sw_s, sw_r, su_s, su_r,
    in_s, gr_s, ag_s, ag_r, ax_s, ax_r, tk_s, tk_r, loc, ex_s, ex_r, rs_s, rs_r, cx_s, cx_r, out_s, out_r,
):
    f = lax.axis_index("fsdp")
    s = lax.axis_index("seq")
    z = f // 2
    y = f % 2
    x = s // 2
    c = s % 2
    dev_y = (z * 2 + 1 - y, s)
    dev_x = (f, (1 - x) * 2 + c)
    dev_c = (f, x * 2 + 1 - c)
    chunks, rows, width = x_a.shape
    length = chunks * rows

    def dev_z(zo):
        return (zo * 2 + y, s)

    def rcopy(src, dst, ssem, rsem, dev):
        return pltpu.make_async_remote_copy(
            src_ref=src, dst_ref=dst, send_sem=ssem, recv_sem=rsem, device_id=dev, device_id_type=MESH
        )

    def slot(zz, yy, at=z):
        return ((zz + at) % 2) * 4 + (zz // 2) * 2 + yy

    def owner(b):
        return 2 * ((z + b // 4) % 2 + 2 * ((b % 4) // 2)) + b % 2

    def flip(v, d):
        for bit in (1, 2, 4):
            if d & bit:
                v = v + bit - 2 * bit * ((v // bit) % 2)
        return v

    barrier = pltpu.get_barrier_semaphore()
    for d in range(1, 8):
        pl.semaphore_signal(barrier, inc=1, device_id=(flip(f, d), s), device_id_type=MESH)
    for d in range(1, 4):
        pl.semaphore_signal(barrier, inc=1, device_id=(f, flip(s, d)), device_id_type=MESH)

    def at_col(ref, col):
        return ref.at[:, pl.ds(pl.multiple_of(col, 128), 128)]

    loads = []
    for pr in range(2):
        for part_i in range(3):
            dst = wi_a.at[pr, f, :, part_i * 128 : part_i * 128 + 128]
            loads.append((at_col(win, part_i * width + c * 256 + pr * 128), dst))
    loads.append((wcon.at[pl.ds(pl.multiple_of(c * 128, 128), 128), :], wc_a.at[slot(z, y)]))
    for b in range(8):
        dst = we_a.at[b // 4, f, :, (b % 4) * 128 : (b % 4) * 128 + 128]
        loads.append((at_col(wexp, owner(b) * 256 + c * 128), dst))
    loads.append((wout, wo_a.at[f]))
    loads = [pltpu.make_async_copy(src, dst, in_s.at[i]) for i, (src, dst) in enumerate(loads)]
    for cp in loads:
        cp.start()
    sm_a[f] = jnp.zeros((16, 128), F32)
    for i, ref in enumerate((v0, v1, v2, v3, v4, v5, v6, v7)):
        sm_a[f, i : i + 1, 0:64] = ref[...].astype(F32).reshape(1, 64)
    eb = v8[...].astype(F32)
    sm_a[f, 8:9, :] = eb[0:128].reshape(1, 128)
    sm_a[f, 9:10, :] = eb[128:256].reshape(1, 128)
    for cp in loads:
        cp.wait()
    pl.semaphore_wait(barrier, 10)
    step = [0]
    actions = {}

    def point():
        for name in SCHEDULE[step[0]]:
            key, _, rest = name.partition(":")
            actions[key](*[int(v) for v in rest.split(".") if v])
        step[0] += 1

    col_c = pl.multiple_of(c * 256, 256)

    def view(g, zz, yy, half, at=z):
        o = zz * 2 + yy
        if g in (1, 2):
            return wi_a.at[g - 1, o]
        if g == 3:
            return wc_a.at[slot(zz, yy, at), pl.ds(pl.multiple_of(half * 64, 64), 64), :]
        if g == 5:
            return wo_a.at[o, :, pl.ds(col_c, 256)]
        if g == 4:
            return we_a.at[0, o]
        return we_a.at[1, o, pl.ds(pl.multiple_of(half * 32, 32), 32), :]

    def ag_copy(g, zz, yy, sem, dev, at=z):
        src = view(g, zz, yy, x)
        if g == 4 and at is not z:
            src = we_a.at[(z + at) % 2, zz * 2 + yy]
        if g == 6 and at is not z:
            src = we_a.at[(1 + z + at) % 2, zz * 2 + yy, pl.ds(pl.multiple_of(x * 32, 32), 32), :]
        return rcopy(src, view(g, zz, yy, x, at), ag_s.at[g, sem], ag_r.at[g, zz * 2 + yy], dev)

    def ax_copy(g, zz, yy, sem, half):
        ref = view(g, zz, yy, half)
        return rcopy(ref, ref, ax_s.at[g // 6, sem], ax_r.at[g // 6, zz * 2 + yy], dev_x)

    def small_first(d):
        return rcopy(sm_a.at[f], sm_a.at[f], su_s.at[d], su_r.at[f], (flip(f, d), s))

    def ag_start(g):
        if g == 0:
            for d in range(1, 8):
                small_first(d).start()
            return
        for d in (2,) if g == 3 else (1, 3) if g == 7 else (1, 2, 3):
            zo = (z + d) % 4
            ag_copy(3 if g == 7 else g, z, y, d - 1, dev_z(zo), zo).start()
        if g != 7:
            ag_copy(g, z, y, 3, dev_y).start()

    def ag_from_z(g, d):
        zo = (z + d) % 4
        cp = ag_copy(g, zo, y, 3 + d, dev_y)
        cp.wait_recv()
        cp.start()
        if g in (3, 6):
            ax_copy(g, zo, y, d - 1, x).start()

    def ag_from_y(g, d):
        zo = (z + d) % 4
        ag_copy(g, zo, 1 - y, 3, dev_y).wait_recv()
        ax_copy(g, zo, 1 - y, 3 + d, x).start()

    def ag_finish(g):
        if g in (3, 6, 7):
            for d in {3: (0, 2), 6: (0, 1, 2, 3), 7: (1, 3)}[g]:
                zo = (z + d) % 4
                o = 3 if g == 7 else g
                if d:
                    ax_copy(o, zo, y, d - 1, 1 - x).wait_recv()
                ax_copy(o, zo, 1 - y, 3 + d, 1 - x).wait_recv()
        else:
            for zo in range(4):
                ag_copy(g, zo, 1 - y, 3, dev_y).wait_recv()

    def ag_drain(g):
        for i in range(7):
            ag_copy(g, z, y, i, dev_y).wait_send()
            if g in (3, 6):
                ax_copy(g, z, y, i, x).wait_send()

    def swap_start(n, src, ref):
        rcopy(src.at[1 - x], ref.at[s], tk_s.at[n, 0], tk_r.at[n, 0], dev_x).start()
        rcopy(src.at[x], ref.at[s], tk_s.at[n, 1], tk_r.at[n, 1], dev_c).start()
        pltpu.make_async_copy(src.at[x], ref.at[s], loc.at[n]).start()

    def swap_forward(n, src, ref):
        k = (1 - x) * 2 + c
        rcopy(src.at[1 - x], ref.at[k], tk_s.at[n, 0], tk_r.at[n, 0], dev_x).wait_recv()
        rcopy(ref.at[k], ref.at[k], tk_s.at[n, 2], tk_r.at[n, 2], dev_c).start()

    def swap_finish(n, src, ref):
        rcopy(ref.at[s], ref.at[s], tk_s.at[n, 2], tk_r.at[n, 2], dev_c).wait_recv()

    def swap_near(n, src, ref):
        pltpu.make_async_copy(src.at[x], ref.at[s], loc.at[n]).wait()
        rcopy(src.at[x], ref.at[s], tk_s.at[n, 1], tk_r.at[n, 1], dev_c).wait_recv()

    def swap_drain(n, src, ref):
        rcopy(src.at[1 - x], ref.at[s], tk_s.at[n, 0], tk_r.at[n, 0], dev_x).wait_send()
        rcopy(src.at[x], ref.at[s], tk_s.at[n, 1], tk_r.at[n, 1], dev_c).wait_send()
        rcopy(ref.at[s], ref.at[s], tk_s.at[n, 2], tk_r.at[n, 2], dev_c).wait_send()

    swaps = ((tok, x_a), (cot, e_a))
    actions["start"] = ag_start
    actions["swap"] = lambda n: swap_start(n, *swaps[n])
    actions["share"] = lambda n: swap_forward(n, *swaps[n])
    actions["az"] = ag_from_z
    actions["ay"] = ag_from_y
    point()

    picked = lax.broadcasted_iota(jnp.int32, gl.shape, 1) == po[x]
    lengths = jnp.sum(jnp.where(picked, gl[...], 0), axis=1, keepdims=True)
    first_end = lengths[0:1, :]
    second_end = first_end + lengths[1:2, :]

    def mask_block(k, carry):
        qp = k * rows + lax.broadcasted_iota(jnp.int32, (rows, length), 0)
        kp = lax.broadcasted_iota(jnp.int32, (rows, length), 1)
        hidden_key = (kp >= first_end) & (kp < second_end) & (qp >= second_end)
        bad = (kp > qp) | hidden_key
        bias[k] = jnp.where(bad, NEG, 0.0).astype(F32)
        return carry

    lax.fori_loop(0, chunks, mask_block, 0)
    lanes = lax.broadcasted_iota(jnp.int32, (8, 128), 1)
    lane_row = lax.broadcasted_iota(jnp.int32, (8, 128), 0)
    lane_mask[...] = jnp.where((lanes < 64) == (lane_row < 1), 1.0, 0.0).astype(F32)
    vec_g[...] = jnp.zeros_like(vec_g)
    eb_g[...] = jnp.zeros_like(eb_g)

    point()
    for d in range(1, 8):
        ff = flip(f, d)
        rcopy(sm_a.at[ff], sm_a.at[ff], su_s.at[d], su_r.at[ff], (ff, s)).wait_recv()
    for r in range(4):
        low_half = sm_a[2 * r, 0:8, :]
        high_half = pltpu.roll(sm_a[2 * r + 1, 0:8, :], 64, 1)
        vec[:, r * 128 : r * 128 + 128] = jnp.where(lanes < 64, low_half, high_half)
    for b in range(8):
        ebv[:, b * 128 : b * 128 + 128] = sm_a[owner(b), pl.ds(8 + c, 1), :]
    swap_near(0, tok, x_a)
    point()
    swap_finish(0, tok, x_a)

    def norm_one(k, carry):
        hat, _ = normalize(x_a[k].astype(F32))
        a_a[k] = (hat * vec[0:1, :] + vec[1:2, :]).astype(BF)
        return carry

    lax.fori_loop(0, chunks, norm_one, 0)
    point()

    def project(pr):
        col = pl.multiple_of(c * 256 + pr * 128, 128)
        w = wi_a[pr].reshape(width, 384)
        for k in range(chunks):
            block = pl.ds(k * rows, rows)
            out = dot_nn(a_a[k], w)
            qkv[pr, block, 0:128] = (out[:, 0:128] + vec[2:3, pl.ds(col, 128)]).astype(BF)
            qkv[pr, block, 128:256] = out[:, 128:256].astype(BF)
            qkv[pr, block, 256:384] = (out[:, 256:384] + vec[3:4, pl.ds(col, 128)]).astype(BF)

    probs = (p0, p1, p2, p3)
    masks = [lane_mask[i : i + 1, :] for i in range(2)]
    masks_low = [m.astype(BF) for m in masks]
    scaled_low = [(m * 0.125).astype(BF) for m in masks]

    def split(v, kinds):
        return [v * m for m in kinds]

    def scores(pr, i):
        span = (i + 1) * rows
        q = qkv[pr, i * rows : i * rows + rows, 0:128]
        k = qkv[pr, 0:span, 128:256]
        return [dot_nt(qm, k) + bias[i, :, 0:span] for qm in split(q, scaled_low)]

    def attend(pr, i, sc):
        span = (i + 1) * rows
        v = qkv[pr, 0:span, 256:384]
        weights = []
        for hh in range(2):
            top = jnp.max(sc[hh], axis=-1, keepdims=True)
            ex = jnp.exp(sc[hh] - top)
            tot = jnp.sum(ex, axis=-1, keepdims=True)
            weights.append((ex * (1.0 / tot)).astype(BF))
            probs[i][pr, hh] = weights[hh]
        out = dot_nn(jnp.concatenate(weights, axis=1), jnp.concatenate(split(v, masks_low), axis=0))
        col = pl.multiple_of(c * 256 + pr * 128, 128)
        o_a[i, :, pl.ds(col, 128)] = out.astype(BF)

    def o_copy(pr):
        col = pl.multiple_of(c * 256 + pr * 128, 128)
        ref = o_a.at[:, :, pl.ds(col, 128)]
        return rcopy(ref, ref, ex_s.at[pr], ex_r.at[pr], dev_c)

    def wo_copy():
        ref = wo_a.at[:, :, pl.ds(col_c, 256)]
        return rcopy(ref, ref, ex_s.at[12], ex_r.at[12], dev_c)

    def wo_start():
        ag_finish(5)
        wo_copy().start()

    actions["wo"] = wo_start
    ag_finish(1)
    project(0)
    point()
    sc = scores(0, 0)
    for i in range(chunks):
        if i < chunks - 1:
            ahead = scores(0, i + 1)
        else:
            ag_finish(2)
            project(1)
            ahead = scores(1, 0)
        attend(0, i, sc)
        sc = ahead
        if i == chunks - 1:
            o_copy(0).start()
        point()
    for i in range(chunks):
        ahead = scores(1, i + 1) if i < chunks - 1 else None
        attend(1, i, sc)
        sc = ahead
        if i == chunks - 1:
            o_copy(1).start()
        point()
    for pr in range(2):
        o_copy(pr).wait_recv()
    ref = wo_a.at[:, :, pl.ds(pl.multiple_of((1 - c) * 256, 256), 256)]
    rcopy(ref, ref, ex_s.at[12], ex_r.at[12], dev_c).wait_recv()

    def b_copy(j):
        ref = b_a.at[c + 2 * j]
        return rcopy(ref, ref, ex_s.at[2 + j], ex_r.at[2 + j], dev_c)

    for j in range(2):
        k = c + 2 * j
        out = dot_nn(o_a[k], wo_a[...].reshape(width, width))
        h = x_a[k].astype(F32) + out + vec[4:5, :]
        h_own[j] = h
        hat, _ = normalize(h)
        b_a[k] = (hat * vec[5:6, :] + vec[6:7, :]).astype(BF)
        b_copy(j).start()
        point()
    swap_near(1, cot, e_a)
    swap_finish(1, cot, e_a)
    ag_finish(3)
    ag_finish(4)
    half = we_a.shape[3]

    def hidden(d):
        zi = ((z + d) % 4) // 2
        return d % 2, zi, pl.ds(pl.multiple_of(zi * 256, 256), 256)

    def mlp_chunk(d, j, first):
        k = (c + 2 * j) if j < 2 else (1 - c) + 2 * (j - 2)
        h, zi, cols = hidden(d)
        bias_cols = pl.ds(pl.multiple_of(h * half + zi * 256, 256), 256)
        we = we_a[h, :, :, cols].reshape(width, 256)
        wc = wc_a[pl.ds(4 * h + 2 * zi, 2)].reshape(256, width)
        u = dot_nn(b_a[k], we) + ebv[:, bias_cols]
        u2 = u * u
        th = jnp.tanh(u * (GELU_A + (GELU_A * GELU_B) * u2))
        hf = 0.5 * th + 0.5
        gf = u * hf
        g = gf.astype(BF)
        g_a[h, k, :, cols] = g
        slope = hf + (gf - gf * hf) * ((2.0 * GELU_A) + (6.0 * GELU_A * GELU_B) * u2)
        du = (slope * dot_nt(e_a[k], wc)).astype(BF)
        du_a[h, k, :, cols] = du
        eb_g[:, bias_cols] += col_sum(du.astype(F32))
        new_part = dot_nn(g, wc)
        new_db = dot_nt(du, we)
        if first:
            part[j] = new_part
            db[j] = new_db
        else:
            part[j] += new_part
            db[j] += new_db

    def part_copy(j):
        return rcopy(part.at[j], part_r.at[j - 2], ex_s.at[4 + j - 2], ex_r.at[4 + j - 2], dev_c)

    def db_copy(j):
        return rcopy(db.at[j], db_r.at[j - 2], ex_s.at[6 + j - 2], ex_r.at[6 + j - 2], dev_c)

    def rs_names(g):
        if g == 0:
            return (st_c, ry_c, rz_c, xb_c, rx_c, fc_c, rc_c)
        if g < 5:
            return tuple(r.at[g - 1] for r in (st_e, ry_e, rz_e, xb_e, rx_e, fc_e, rc_e))
        if g == 5:
            return (st_o, ry_o, rz_o, xb_o, rx_o, fc_o, rc_o)
        return tuple(r.at[g - 6] for r in (st_i, ry_i, rz_i, xb_i, rx_i, fc_i, rc_i))

    mine = pl.ds(pl.multiple_of(x * 64, 64), 64)
    theirs = pl.ds(pl.multiple_of((1 - x) * 64, 64), 64)

    def con_x(zt):
        return rcopy(st_c.at[:, zt, theirs], rh_c.at[zt], cx_s.at[zt], cx_r.at[zt], dev_x)

    def con_y(zt):
        return rcopy(st_c.at[1 - y, zt, mine], ry_c.at[zt], rs_s.at[0, zt], rs_r.at[0, zt], dev_y)

    def con_z(zt):
        return rcopy(st_c.at[y, zt, mine], rz_c.at[z], rs_s.at[0, 4 + zt], rs_r.at[0, 4 + z], dev_z(zt))

    def con_y_start(d):
        zt = (z + d) % 4
        con_x(zt).wait_recv()
        for yy in range(2):
            st_c[yy, zt, mine] = (st_c[yy, zt, mine].astype(F32) + rh_c[zt, yy].astype(F32)).astype(BF)
        con_y(zt).start()

    def con_z_start(d):
        zt = (z + d) % 4
        con_y(zt).wait_recv()
        st_c[y, zt, mine] = (st_c[y, zt, mine].astype(F32) + ry_c[zt].astype(F32)).astype(BF)
        if d:
            con_z(zt).start()

    def rs_y(g, zo):
        st, ry = rs_names(g)[:2]
        return rcopy(st.at[1 - y, zo], ry.at[zo], rs_s.at[g, zo], rs_r.at[g, zo], dev_y)

    def rs_z(g, zo):
        st, _, rz = rs_names(g)[:3]
        to = g
        if 0 < g < 5:
            at = (g + 3 + z - zo) % 4
            rz, to = rz_e.at[at], 1 + at
        return rcopy(st.at[y, zo], rz.at[z], rs_s.at[g, 4 + zo], rs_r.at[to, 4 + z], dev_z(zo))

    def rs_x(g):
        xb, rx = rs_names(g)[3:5]
        return rcopy(xb, rx, rs_s.at[g, 8], rs_r.at[g, 8], dev_x)

    def rs_c(g):
        fc, rc = rs_names(g)[5:7]
        return rcopy(fc, rc, rs_s.at[g, 9], rs_r.at[g, 9], dev_c)

    def rs_y_start(g):
        for d in (1, 2, 3, 0):
            rs_y(g, (z + d) % 4).start()

    def rs_z_start(g, d):
        zo = (z + d) % 4
        st, ry = rs_names(g)[:2]
        rs_y(g, zo).wait_recv()
        st[y, zo] = (st[y, zo].astype(F32) + ry[zo].astype(F32)).astype(st.dtype)
        rs_z(g, zo).start()

    def rs_x_start(g):
        st, ry, rz, xb = rs_names(g)[:4]
        if g == 0:
            total = st_c[y, z, mine].astype(F32)
        else:
            rs_y(g, z).wait_recv()
            total = st[y, z].astype(F32) + ry[z].astype(F32)
        for d in range(1, 4):
            zo = (z + d) % 4
            if g == 0:
                cp = rcopy(st_c.at[y, zo, mine], rz.at[zo], rs_s.at[g, 4 + zo], rs_r.at[g, 4 + zo], dev_z(zo))
            else:
                cp = rcopy(st.at[y, zo], rz.at[zo], rs_s.at[g, 4 + zo], rs_r.at[g, 4 + zo], dev_z(zo))
            cp.wait_recv()
            total = total + rz[zo].astype(F32)
        xb[...] = total.astype(xb.dtype)
        rs_x(g).start()

    def write_out(g, side, value):
        if g == 0:
            g_c[pl.ds(pl.multiple_of(side * 128, 128), 128), :] = value
        elif g < 5:
            for yy in range(2):
                ff = 2 * ((z + g - 1) % 4) + yy
                col = pl.multiple_of(ff * 256 + side * 128, 128)
                g_e[:, pl.ds(col, 128)] = value[:, yy * 128 : yy * 128 + 128]
        elif g == 5:
            g_out[:, pl.ds(pl.multiple_of(side * 256, 256), 256)] = value
        else:
            for part_i in range(3):
                col = pl.multiple_of(part_i * width + side * 256 + (g - 6) * 128, 128)
                g_in[:, pl.ds(col, 128)] = value[:, part_i * 128 : part_i * 128 + 128]

    def rs_c_start(g):
        xb, rx, fc = rs_names(g)[3:6]
        rs_x(g).wait_recv()
        if g == 0:
            fc[mine] = xb[...].astype(F32)
            fc[theirs] = rx[...].astype(F32)
        else:
            fc[...] = xb[...].astype(F32) + rx[...].astype(F32)
        rs_c(g).start()
        write_out(g, c, fc[...])

    def rs_finish(g):
        fc, rc = rs_names(g)[5:7]
        rs_c(g).wait_recv()
        write_out(g, 1 - c, rc[...])
        written.append(g)
        for members, src, dst, sem in copies:
            if g in members and all(m in written for m in members):
                pltpu.make_async_copy(src, dst, gr_s.at[sem]).start()

    written = []
    copies = (
        ((0,), g_c, h_c, 0),
        ((1, 2, 3, 4), g_e, h_e, 1),
        ((5,), g_out, h_out, 2),
        ((6, 7), g_in, h_in, 3),
    )

    def rs_drain(g):
        for d in range(4):
            zo = (z + d) % 4
            if g == 0:
                con_x(zo).wait_send()
                con_y(zo).wait_send()
            else:
                rs_y(g, zo).wait_send()
            if d:
                (con_z(zo) if g == 0 else rs_z(g, zo)).wait_send()
        rs_x(g).wait_send()
        rs_c(g).wait_send()

    def grad_con(d):
        zt = (z + d) % 4
        h, _, cols = hidden(d)
        out = dot_tn(g_a[h, :, :, cols].reshape(length, 256), e_a[...].reshape(length, width))
        st_c[0, zt] = out[0:128].astype(BF)
        st_c[1, zt] = out[128:256].astype(BF)
        con_x(zt).start()

    def grad_exp(d):
        h, _, cols = hidden(d)
        out = dot_tn(b_a[...].reshape(length, width), du_a[h, :, :, cols].reshape(length, 256))
        for ff in range(8):
            st_e[d, ff % 2, ff // 2] = out[ff * 64 : ff * 64 + 64].astype(BF)
        rs_y_start(1 + d)

    actions["cy"] = con_y_start
    actions["cz"] = con_z_start
    actions["rz"] = rs_z_start
    actions["rx"] = rs_x_start
    actions["rc"] = rs_c_start
    actions["rf"] = rs_finish
    for d in (2, 0, 1, 3):
        if d == 1:
            ag_finish(7)
            ag_finish(6)
        for n, j in enumerate((0, 1, 2, 3) if d == 2 else (2, 3, 0, 1)):
            if d == 2 and j >= 2:
                ref = b_a.at[1 - c + 2 * (j - 2)]
                rcopy(ref, ref, ex_s.at[j], ex_r.at[j], dev_c).wait_recv()
            mlp_chunk(d, j, d == 2)
            if d == 3 and j >= 2:
                part_copy(j).start()
                db_copy(j).start()
            if n % 2:
                point()
        grad_con(d)
        point()
        grad_exp(d)
        point()

    def send_rows(n, ref, out):
        far = rcopy(stage.at[n, 1 - x], out.at[x], out_s.at[n, 0], out_r.at[n], dev_x)
        near = pltpu.make_async_copy(stage.at[n, x], out.at[x], out_s.at[n, 1])
        return far, near

    def dr_copy(j):
        ref = dr_a.at[c + 2 * j]
        return rcopy(ref, ref, ex_s.at[8 + j], ex_r.at[8 + j], dev_c)

    for j in range(2):
        k = c + 2 * j
        h = h_own[j]
        e = e_a[k].astype(F32)
        rcopy(db.at[j + 2], db_r.at[j], ex_s.at[6 + j], ex_r.at[6 + j], dev_c).wait_recv()
        grad_b = db[j] + db_r[j]
        hat, rstd = normalize(h)
        dh = e + normalize_back(grad_b, vec[5:6, :], hat, rstd)
        dh_own[j] = dh
        dr = dh.astype(BF)
        dr_a[k] = dr
        dr_copy(j).start()
        vec_g[4:5, :] += col_sum(dr.astype(F32))
        vec_g[5:6, :] += col_sum(grad_b * hat)
        vec_g[6:7, :] += col_sum(grad_b)
        vec_g[7:8, :] += col_sum(e)
        rcopy(part.at[j + 2], part_r.at[j], ex_s.at[4 + j], ex_r.at[4 + j], dev_c).wait_recv()
        stage[0, j] = (h + part[j] + part_r[j] + vec[7:8, :]).astype(BF)
        point()
    for cp in send_rows(0, stage, lo):
        cp.start()

    head_row = pl.multiple_of(c * 4, 4)

    def grad_mixed(k):
        w = wo_a[pl.ds(head_row, 4)].reshape(256, width)
        do_a[k] = dot_nt(dr_a[k], w).astype(BF)

    for j in range(2):
        grad_mixed(c + 2 * j)
    point()
    for j in range(2):
        ref = dr_a.at[1 - c + 2 * j]
        rcopy(ref, ref, ex_s.at[8 + j], ex_r.at[8 + j], dev_c).wait_recv()
        grad_mixed(1 - c + 2 * j)
    point()
    out = dot_tn(o_a[...].reshape(length, width), dr_a[:, :, pl.ds(col_c, 256)].reshape(length, 256))
    for ff in range(8):
        st_o[ff % 2, ff // 2] = out[ff * 64 : ff * 64 + 64].astype(BF)
    rs_y_start(5)
    point()

    def grad_probs(pr, i):
        v = qkv[pr, 0 : (i + 1) * rows, 256:384]
        do = do_a[i, :, pr * 128 : pr * 128 + 128]
        return [dot_nt(dom, v) for dom in split(do, masks_low)]

    def attend_back(pr, i, gp):
        span = (i + 1) * rows
        block = pl.ds(i * rows, rows)
        q = qkv[pr, block, 0:128]
        k = qkv[pr, 0:span, 128:256]
        do = do_a[i, :, pr * 128 : pr * 128 + 128]
        ds = []
        for hh in range(2):
            pf = probs[i][pr, hh].astype(F32)
            t = pf * gp[hh]
            inner = jnp.sum(t, axis=-1, keepdims=True)
            ds.append((t - pf * inner).astype(BF))
        both = jnp.concatenate([probs[i][pr, 0], probs[i][pr, 1]], axis=0)
        grad_v = dot_tn(both, jnp.concatenate(split(do, masks_low), axis=0))
        grad_k = dot_tn(jnp.concatenate(ds, axis=0), jnp.concatenate(split(q, scaled_low), axis=0))
        if i == chunks - 1:
            acc_v[...] = grad_v
            acc_k[...] = grad_k
        else:
            acc_v[0:span] += grad_v
            acc_k[0:span] += grad_k
        grad_q = dot_nn(
            jnp.concatenate(ds, axis=1), jnp.concatenate(split(k, scaled_low), axis=0)
        ).astype(BF)
        grad_k = acc_k[block].astype(BF)
        grad_v = acc_v[block].astype(BF)
        dd[pr, block, 0:128] = grad_q
        dd[pr, block, 128:256] = grad_k
        dd[pr, block, 256:384] = grad_v
        col = pl.multiple_of(c * 256 + pr * 128, 128)
        vec_g[2:3, pl.ds(col, 128)] += col_sum(grad_q.astype(F32))
        vec_g[3:4, pl.ds(col, 128)] += col_sum(grad_v.astype(F32))

    def grad_in(pr, out):
        for ff in range(8):
            st_i[pr, ff % 2, ff // 2] = out[ff * 64 : ff * 64 + 64].astype(BF)
        rs_y_start(6 + pr)

    def da_copy(j):
        return rcopy(part.at[j], db_r.at[j - 2], ex_s.at[10 + j - 2], ex_r.at[10 + j - 2], dev_c)

    def grad_a(i):
        total = None
        for pr in range(2):
            p = dot_nt(dd[pr, i * rows : i * rows + rows, :], wi_a[pr].reshape(width, 384))
            total = p if total is None else total + p
        other = (i + c) % 2
        part[i // 2 + 2 * other] = total

        @pl.when(other == 1)
        def _():
            da_copy(2 + i // 2).start()

    def norm_one_back(j):
        k = c + 2 * j
        rcopy(part.at[j + 2], db_r.at[j], ex_s.at[10 + j], ex_r.at[10 + j], dev_c).wait_recv()
        grad = part[j] + db_r[j]
        hat, rstd = normalize(x_a[k].astype(F32))
        vec_g[0:1, :] += col_sum(grad * hat)
        vec_g[1:2, :] += col_sum(grad)
        stage[1, j] = (dh_own[j] + normalize_back(grad, vec[0:1, :], hat, rstd)).astype(BF)

    order = [(pr, i) for pr in range(2) for i in range(chunks - 1, -1, -1)]
    gp = grad_probs(*order[0])
    for n, (pr, i) in enumerate(order):
        ahead = grad_probs(*order[n + 1]) if n < 7 else None
        attend_back(pr, i, gp)
        gp = ahead
        if pr == 0 and i == 0:
            grad_in(0, dot_tn(a_a[...].reshape(length, width), dd[0]))
            for j in range(2, 4):
                part_copy(j).wait_send()
        if pr == 1:
            block = dot_tn(a_a[i], dd[1, i * rows : i * rows + rows, :])
            if i == chunks - 1:
                gi_acc[...] = block
            elif i > 0:
                gi_acc[...] += block
            else:
                grad_in(1, gi_acc[...] + block)
                point()
            grad_a(i)
            if i < 2:
                norm_one_back(i)
        point()
    for cp in send_rows(1, stage, gt):
        cp.start()

    for r in range(4):
        tile = vec_g[:, r * 128 : r * 128 + 128]
        rolled = pltpu.roll(tile, 64, 1)
        for yy in range(2):
            ff = 2 * r + yy
            st_s[ff, 0:8, :] = tile if yy == 0 else rolled
            st_s[ff, 8:16, :] = jnp.zeros((8, 128), F32)
            lane = pl.multiple_of(slot(r, yy) * 128, 128)
            st_s[ff, pl.ds(8 + c, 1), :] = eb_g[:, pl.ds(lane, 128)]

    def small_copy(d):
        ff = flip(f, d)
        return rcopy(st_s.at[ff], rz_s.at[f], sv_s.at[d], sv_r.at[f], (ff, s))

    def small_last(d):
        ss = flip(s, d)
        return rcopy(rx_s.at[s], rx_s.at[s], sw_s.at[d], sw_r.at[s], (f, ss))

    for d in range(1, 8):
        small_copy(d).start()

    def small_sum():
        rz_s[f] = st_s[f]
        for d in range(1, 8):
            ff = flip(f, d)
            rcopy(st_s.at[ff], rz_s.at[ff], sv_s.at[d], sv_r.at[ff], (ff, s)).wait_recv()
        total = rz_s[0]
        for ff in range(1, 8):
            total = total + rz_s[ff]
        rx_s[s] = total
        for d in range(1, 4):
            small_last(d).start()

    def small_end():
        for d in range(1, 4):
            ss = flip(s, d)
            rcopy(rx_s.at[ss], rx_s.at[ss], sw_s.at[d], sw_r.at[ss], (f, ss)).wait_recv()
        g_sm[...] = (rx_s[0] + rx_s[1]) + (rx_s[2] + rx_s[3])

    actions["sb"] = small_sum
    actions["sc"] = small_end
    point()
    for n, out in ((0, lo), (1, gt)):
        far, near = send_rows(n, stage, out)
        near.wait()
        far.wait_send()
        rcopy(stage.at[n, 1 - x], out.at[1 - x], out_s.at[n, 0], out_r.at[n], dev_x).wait_recv()
    for _, src, dst, sem in copies:
        pltpu.make_async_copy(src, dst, gr_s.at[sem]).wait()
    for g in range(1, 7):
        ag_drain(g)
    swap_drain(0, tok, x_a)
    swap_drain(1, cot, e_a)
    wo_copy().wait_send()
    for pr in range(2):
        o_copy(pr).wait_send()
    for j in range(2):
        b_copy(j).wait_send()
        dr_copy(j).wait_send()
        db_copy(j + 2).wait_send()
        da_copy(j + 2).wait_send()
    for g in range(8):
        rs_drain(g)
    for d in range(1, 8):
        small_copy(d).wait_send()
        small_first(d).wait_send()
    for d in range(1, 4):
        small_last(d).wait_send()


SCHEDULE = (
    ("start:3", "start:1", "start:0", "swap:0", "start:2", "start:5", "start:4", "az:3.2", "start:6", "swap:1", "az:1.2",),
    ("az:1.1", "az:1.3", "share:0", "ay:3.2", "share:1",),
    ("az:2.1", "az:2.3", "az:2.2",),
    ("ay:3.0",),
    ("start:7", "az:5.3", "az:5.2", "az:5.1",),
    ("az:4.3",),
    (),
    ("ay:6.0", "az:4.2",),
    ("az:6.1", "az:4.1",),
    (),
    ("az:6.2", "az:6.3",),
    (),
    ("ay:6.1", "wo", "az:3.3", "az:3.1", "ay:6.2",),
    (),
    (),
    ("ay:6.3", "ay:3.3",),
    ("ay:3.1",),
    (),
    (),
    (),
    (),
    (),
    (),
    ("rz:3.1", "rz:3.2", "rz:3.3",),
    (),
    (),
    (),
    ("rz:1.2", "rz:1.1",),
    (),
    (),
    (),
    ("rz:1.3", "rz:2.2", "rz:2.1", "rz:2.3",),
    (),
    ("cy:2",),
    ("cy:1", "rz:4.2", "rz:4.3", "rz:4.1", "cy:3",),
    ("cy:0", "cz:2",),
    (),
    ("cz:1", "rx:4",),
    ("cz:3",),
    ("rz:5.2", "rx:1", "rz:5.1",),
    ("rc:4", "rz:5.3", "rx:2", "cz:0",),
    ("rz:6.1", "rx:0", "rz:6.2",),
    (),
    ("rz:6.3", "rc:2", "rx:5",),
    ("rx:3",),
    ("rz:7.1", "rc:0", "rz:7.2", "rz:7.3", "rc:1", "rc:5", "rx:6", "rf:4", "rx:7", "rf:1", "rf:2", "sb", "rf:0", "rf:5", "rc:3", "rc:7", "rc:6", "sc", "rf:7", "rf:3", "rf:6",),
)


def finish_kernel(*refs):
    gs = refs[6]
    outs = refs[7:]
    for i in range(6):
        outs[i][...] = refs[i][...]
    for i in range(8):
        outs[6 + i][...] = gs[i : i + 1, 0 : outs[6 + i].shape[1]]
    outs[14][:, 0:128] = gs[8:9, :]
    outs[14][:, 128:256] = gs[9:10, :]


def fast_shards(
    tokens, placement_order, group_lengths, first_gain, first_shift, attention_in, query_bias,
    value_bias, attention_out, attention_bias, second_gain, second_shift, expand_weight,
    expand_bias, contract_weight, contract_bias, cotangent,
):
    batch, rows, width = tokens.shape
    lanes = first_gain.shape[0]
    chunks = 4
    length = chunks * rows
    half = expand_weight.shape[1] // 4
    vm = pl.BlockSpec(memory_space=pltpu.VMEM)
    sm = pl.BlockSpec(memory_space=pltpu.SMEM)
    hb = pl.BlockSpec(memory_space=pl.ANY)
    V = pltpu.VMEM
    pieces = (((128, width), None), ((64, 256), 4), ((64, 256), None), ((64, 384), 2))

    def family(lead, dtype, con=128):
        out = []
        for n, (shape, pairs) in enumerate(pieces):
            if n == 0:
                shape = (con, width)
            pre = () if pairs is None else (pairs,)
            out.append(V(pre + lead + shape, dtype))
        return out

    dma = pltpu.SemaphoreType.DMA
    scratch = [
        V(attention_in.shape, F32), V(attention_out.shape, F32), V(expand_weight.shape, F32),
        V(contract_weight.shape, F32),
        V((2, 8, 64, 384), BF), V((8, 64, width), BF), V((2, 8, 64, half), BF), V((8, 128, width), BF),
        V((8, 16, 128), F32), V((8, width), F32), V((1, 2 * half), F32), V((8, 128), F32),
        V((chunks, rows, width), BF), V((chunks, rows, width), BF), V((chunks, rows, width), BF),
        V((2, length, 384), BF), V((chunks, rows, length), F32),
        V((2, 2, rows, rows), BF), V((2, 2, rows, 2 * rows), BF), V((2, 2, rows, 3 * rows), BF),
        V((2, 2, rows, 4 * rows), BF),
        V((chunks, rows, width), BF), V((2, rows, width), F32), V((chunks, rows, width), BF),
        V((2, chunks, rows, half), BF), V((2, chunks, rows, half), BF),
        V((4, rows, width), F32), V((4, rows, width), F32), V((2, rows, width), F32),
        V((2, rows, width), F32), V((chunks, rows, width), BF), V((2, rows, width), F32),
        V((chunks, rows, 256), BF), V((2, length, 384), BF), V((length, 128), F32),
        V((length, 128), F32), V((2, 2, rows, width), BF), V((8, width), F32), V((1, 2 * half), F32),
    ]
    scratch += [V((width, 384), F32)]
    scratch += family((2, 4), BF) + [V((4, 2, 64, width), BF)] + family((4,), BF, 64)
    scratch += family((4,), BF, 64) + family((), BF, 64) + family((), BF, 64)
    scratch += family((), F32) + family((), F32)
    scratch += [V((8, 16, 128), F32), V((8, 16, 128), F32), V((4, 16, 128), F32)]
    scratch += [dma((8,)), dma((8,)), dma((4,)), dma((4,)), dma((8,)), dma((8,))]
    scratch += [
        dma((16,)), dma((6,)), dma((7, 7)), dma((7, 8)), dma((2, 7)), dma((2, 8)), dma((2, 3)), dma((2, 3)), dma((2,)),
        dma((13,)), dma((13,)), dma((8, 10)), dma((8, 10)), dma((4,)), dma((4,)), dma((2, 2)), dma((2,)),
    ]
    grads = (
        jax.ShapeDtypeStruct(tokens.shape, BF),
        jax.ShapeDtypeStruct(tokens.shape, BF),
        jax.ShapeDtypeStruct(attention_in.shape, F32),
        jax.ShapeDtypeStruct(attention_out.shape, F32),
        jax.ShapeDtypeStruct(expand_weight.shape, F32),
        jax.ShapeDtypeStruct(contract_weight.shape, F32),
    )
    outs = pl.pallas_call(
        layer_kernel,
        out_shape=grads + (jax.ShapeDtypeStruct((16, 128), F32),),
        in_specs=[sm, vm] + [hb] * 6 + [vm] * 9,
        out_specs=[hb] * 6 + [vm],
        scratch_shapes=scratch,
        compiler_params=pltpu.CompilerParams(
            collective_id=0, has_side_effects=True, vmem_limit_bytes=63 << 20
        ),
    )(
        placement_order, group_lengths.T, tokens, cotangent, attention_in, attention_out,
        expand_weight, contract_weight, first_gain, first_shift, query_bias, value_bias,
        attention_bias, second_gain, second_shift, contract_bias, expand_bias,
    )
    outs = pl.pallas_call(
        finish_kernel,
        out_shape=grads
        + tuple(jax.ShapeDtypeStruct((1, lanes), F32) for _ in range(8))
        + (jax.ShapeDtypeStruct((1, 256), F32),),
        in_specs=[vm] * 7,
        out_specs=[vm] * 15,
    )(*outs)
    layer_out, grad_tokens, g_in, g_out, g_e, g_c = outs[:6]
    v = [item.reshape(-1) for item in outs[6:]]
    return (
        layer_out, grad_tokens, v[0], v[1], g_in, v[2], v[3], g_out,
        v[4], v[5], v[6], g_e, v[8], g_c, v[7],
    )


def solution(mesh):
    in_specs = (
        P("fsdp", "seq", None),
        P("fsdp"),
        P(),
        P("fsdp"),
        P("fsdp"),
        P("fsdp", None),
        P("fsdp"),
        P("fsdp"),
        P("fsdp", None),
        P("fsdp"),
        P("fsdp"),
        P("fsdp"),
        P("fsdp", None),
        P("fsdp"),
        P("fsdp", None),
        P("fsdp"),
        P("fsdp", "seq", None),
    )
    out_specs = (
        P("fsdp", "seq", None),
        P("fsdp", "seq", None),
        P("fsdp"),
        P("fsdp"),
        P("fsdp", None),
        P("fsdp"),
        P("fsdp"),
        P("fsdp", None),
        P("fsdp"),
        P("fsdp"),
        P("fsdp"),
        P("fsdp", None),
        P("fsdp"),
        P("fsdp", None),
        P("fsdp"),
    )
    pick = fast_shards if (mesh.shape["fsdp"], mesh.shape["seq"]) == (8, 4) else shards
    return jax.shard_map(pick, mesh=mesh, in_specs=in_specs, out_specs=out_specs, check_vma=False)
```

```python
import math

import jax
import jax.numpy as jnp
from jax import lax
from jax.experimental import pallas as pl
from jax.experimental.pallas import tpu as pltpu
from jax.sharding import PartitionSpec as P

HD = 64


norm_eps = 1e-05


def layer_norm(values, gain, shift):
    mean = jnp.mean(values, axis=-1, keepdims=True)
    centred = values - mean
    variance = jnp.mean(centred * centred, axis=-1, keepdims=True)
    return centred * lax.rsqrt(variance + norm_eps) * gain + shift


def gelu_tanh(values):
    return jax.nn.gelu(values, approximate=True)


def masked_scores(query_blk, keys, start, segment, scale):
    count = query_blk.shape[0]
    scores = jnp.einsum("qhd,khd->hqk", query_blk, keys, preferred_element_type=jnp.float32) * scale
    query_pos = start + jnp.arange(count, dtype=jnp.int32)
    key_pos = jnp.arange(keys.shape[0], dtype=jnp.int32)
    query_seg = lax.dynamic_slice_in_dim(segment, start, count, 0)
    allowed = (key_pos[None, :] <= query_pos[:, None]) & (
        (segment[None, :] == query_seg[:, None]) | (segment[None, :] == 0)
    )
    return jnp.where(allowed[None], scores, -1e30)


def forward_heads(query, keys, values, segment, block, scale):
    starts = jnp.arange(query.shape[0] // block, dtype=jnp.int32) * block

    def forward_one_block(start):
        query_blk = lax.dynamic_slice_in_dim(query, start, block, 0)
        scores = masked_scores(query_blk, keys, start, segment, scale)
        top = jnp.max(scores, axis=-1, keepdims=True)
        raised = jnp.exp(scores - top)
        total = jnp.sum(raised, axis=-1, keepdims=True)
        weights = (raised / total).astype(jnp.bfloat16)
        mixed = jnp.einsum("hqk,khd->qhd", weights, values, preferred_element_type=jnp.float32)
        return (mixed.astype(jnp.bfloat16), (top + jnp.log(total))[..., 0])

    return lax.map(forward_one_block, starts)


def backward_heads(query, keys, values, segment, log_total, grad_out, block, scale):
    count = query.shape[0] // block
    starts = jnp.arange(count, dtype=jnp.int32) * block
    grad_blocks = grad_out.reshape((count, block) + grad_out.shape[1:])

    def backward_one_block(carry, inputs):
        grad_keys, grad_values = carry
        start, total_blk, grad_blk = inputs
        query_blk = lax.dynamic_slice_in_dim(query, start, block, 0)
        scores = masked_scores(query_blk, keys, start, segment, scale)
        probs = jnp.exp(scores - total_blk[:, :, None])
        grad_probs = jnp.einsum(
            "qhd,khd->hqk", grad_blk, values, preferred_element_type=jnp.float32
        )
        inner = jnp.sum(probs * grad_probs, axis=-1, keepdims=True)
        grad_scores = (probs * (grad_probs - inner)).astype(jnp.bfloat16)
        grad_query = (
            jnp.einsum("hqk,khd->qhd", grad_scores, keys, preferred_element_type=jnp.float32)
            * scale
        )
        grad_keys = (
            grad_keys
            + jnp.einsum("hqk,qhd->khd", grad_scores, query_blk, preferred_element_type=jnp.float32)
            * scale
        )
        grad_values = grad_values + jnp.einsum(
            "hqk,qhd->khd", probs.astype(jnp.bfloat16), grad_blk, preferred_element_type=jnp.float32
        )
        return ((grad_keys, grad_values), grad_query)

    zeros = jnp.zeros(keys.shape, jnp.float32)
    (grad_keys, grad_values), grad_query = lax.scan(
        backward_one_block, (zeros, zeros), (starts, log_total, grad_blocks)
    )
    return (grad_query.reshape(query.shape), grad_keys, grad_values)


def shards(
    tokens,
    placement_order,
    group_lengths,
    first_gain,
    first_shift,
    attention_in,
    query_bias,
    value_bias,
    attention_out,
    attention_bias,
    second_gain,
    second_shift,
    expand_weight,
    expand_bias,
    contract_weight,
    contract_bias,
    cotangent,
):
    batch, rows, width = tokens.shape
    seq_count = lax.axis_size("seq")
    seq_len = rows * seq_count
    block = min(512, seq_len)
    scale = 1.0 / math.sqrt(HD)
    gathered = (
        lax.all_gather(attention_in, "fsdp", axis=0, tiled=True),
        lax.all_gather(attention_out, "fsdp", axis=0, tiled=True),
        lax.all_gather(expand_weight, "fsdp", axis=0, tiled=True),
        lax.all_gather(contract_weight, "fsdp", axis=0, tiled=True),
        lax.all_gather(first_gain, "fsdp", axis=0, tiled=True),
        lax.all_gather(first_shift, "fsdp", axis=0, tiled=True),
        lax.all_gather(query_bias, "fsdp", axis=0, tiled=True),
        lax.all_gather(value_bias, "fsdp", axis=0, tiled=True),
        lax.all_gather(attention_bias, "fsdp", axis=0, tiled=True),
        lax.all_gather(second_gain, "fsdp", axis=0, tiled=True),
        lax.all_gather(second_shift, "fsdp", axis=0, tiled=True),
        lax.all_gather(expand_bias, "fsdp", axis=0, tiled=True),
        lax.all_gather(contract_bias, "fsdp", axis=0, tiled=True),
    )
    in_full, out_full, expand_full, contract_full = (
        gathered[0],
        gathered[1],
        gathered[2],
        gathered[3],
    )
    small = [item.astype(jnp.float32) for item in gathered[4:]]
    (
        gain_one,
        shift_one,
        bias_query,
        bias_value,
        bias_attention,
        gain_two,
        shift_two,
        bias_expand,
        bias_contract,
    ) = small
    groups = group_lengths.shape[0]
    picked = (placement_order[:, None] == jnp.arange(groups, dtype=jnp.int32)[None, :]).astype(
        jnp.int32
    )
    lengths = jnp.sum(picked[:, :, None] * group_lengths[None, :, :], axis=1)
    positions = jnp.arange(seq_len, dtype=jnp.int32)
    first_end = lengths[:, 0:1]
    second_end = first_end + lengths[:, 1:2]
    segment = (positions[None, :] >= first_end).astype(jnp.int32) + (
        positions[None, :] >= second_end
    ).astype(jnp.int32)
    tok_rows = tokens.reshape(batch * rows, width).astype(jnp.float32)
    normed, norm_one_pull = jax.vjp(layer_norm, tok_rows, gain_one, shift_one)
    normed_low = normed.astype(jnp.bfloat16)
    bias_in = jnp.concatenate([bias_query, jnp.zeros((width,), jnp.float32), bias_value])
    projected = (jnp.dot(normed_low, in_full, preferred_element_type=jnp.float32) + bias_in).astype(
        jnp.bfloat16
    )
    heads_in = lax.all_to_all(
        projected.reshape(batch, rows, 3, width), "seq", split_axis=3, concat_axis=1, tiled=True
    )
    head_cols = heads_in.shape[3]
    per_device = head_cols // HD
    mixed_list = []
    total_list = []
    for index in range(batch):
        query = heads_in[index, :, 0].reshape(seq_len, per_device, HD)
        keys = heads_in[index, :, 1].reshape(seq_len, per_device, HD)
        values = heads_in[index, :, 2].reshape(seq_len, per_device, HD)
        mixed_blocks, log_total = forward_heads(query, keys, values, segment[index], block, scale)
        mixed_list.append(mixed_blocks.reshape(seq_len, head_cols))
        total_list.append(log_total)
    mixed = lax.all_to_all(jnp.stack(mixed_list), "seq", split_axis=1, concat_axis=2, tiled=True)
    mixed_rows = mixed.reshape(batch * rows, width)
    hidden = (
        tok_rows
        + jnp.dot(mixed_rows, out_full, preferred_element_type=jnp.float32)
        + bias_attention
    )
    normed_two, norm_two_pull = jax.vjp(layer_norm, hidden, gain_two, shift_two)
    normed_two_low = normed_two.astype(jnp.bfloat16)
    expanded = (
        jnp.dot(normed_two_low, expand_full, preferred_element_type=jnp.float32) + bias_expand
    )
    activated, gelu_pull = jax.vjp(gelu_tanh, expanded)
    activated_low = activated.astype(jnp.bfloat16)
    result = (
        hidden
        + jnp.dot(activated_low, contract_full, preferred_element_type=jnp.float32)
        + bias_contract
    )
    layer_out = result.astype(jnp.bfloat16).reshape(batch, rows, width)
    grad_low = cotangent.reshape(batch * rows, width)
    grad_res = grad_low.astype(jnp.float32)
    grad_contract = jnp.dot(activated_low.T, grad_low, preferred_element_type=jnp.float32)
    grad_bias_contract = jnp.sum(grad_res, axis=0)
    (grad_expanded,) = gelu_pull(
        jnp.dot(grad_low, contract_full.T, preferred_element_type=jnp.float32)
    )
    grad_expanded_low = grad_expanded.astype(jnp.bfloat16)
    grad_expand = jnp.dot(normed_two_low.T, grad_expanded_low, preferred_element_type=jnp.float32)
    grad_bias_expand = jnp.sum(grad_expanded_low.astype(jnp.float32), axis=0)
    grad_hidden, grad_gain_two, grad_shift_two = norm_two_pull(
        jnp.dot(grad_expanded_low, expand_full.T, preferred_element_type=jnp.float32)
    )
    grad_hidden = grad_hidden + grad_res
    grad_branch_low = grad_hidden.astype(jnp.bfloat16)
    grad_out_proj = jnp.dot(mixed_rows.T, grad_branch_low, preferred_element_type=jnp.float32)
    grad_bias_attention = jnp.sum(grad_branch_low.astype(jnp.float32), axis=0)
    grad_mixed = jnp.dot(grad_branch_low, out_full.T, preferred_element_type=jnp.float32).astype(
        jnp.bfloat16
    )
    grad_heads = lax.all_to_all(
        grad_mixed.reshape(batch, rows, width), "seq", split_axis=2, concat_axis=1, tiled=True
    )
    grad_list = []
    for index in range(batch):
        query = heads_in[index, :, 0].reshape(seq_len, per_device, HD)
        keys = heads_in[index, :, 1].reshape(seq_len, per_device, HD)
        values = heads_in[index, :, 2].reshape(seq_len, per_device, HD)
        grad_out = grad_heads[index].reshape(seq_len, per_device, HD)
        grad_query, grad_keys, grad_values = backward_heads(
            query, keys, values, segment[index], total_list[index], grad_out, block, scale
        )
        stacked = jnp.stack(
            [
                grad_query.reshape(seq_len, head_cols),
                grad_keys.reshape(seq_len, head_cols),
                grad_values.reshape(seq_len, head_cols),
            ],
            axis=1,
        )
        grad_list.append(stacked.astype(jnp.bfloat16))
    grad_proj = lax.all_to_all(jnp.stack(grad_list), "seq", split_axis=1, concat_axis=3, tiled=True)
    grad_proj_rows = grad_proj.reshape(batch * rows, 3 * width)
    grad_in_proj = jnp.dot(normed_low.T, grad_proj_rows, preferred_element_type=jnp.float32)
    grad_proj_wide = grad_proj_rows.astype(jnp.float32)
    grad_bias_query = jnp.sum(grad_proj_wide[:, :width], axis=0)
    grad_bias_value = jnp.sum(grad_proj_wide[:, 2 * width :], axis=0)
    grad_tok, grad_gain_one, grad_shift_one = norm_one_pull(
        jnp.dot(grad_proj_rows, in_full.T, preferred_element_type=jnp.float32)
    )
    grad_tokens = (grad_tok + grad_hidden).astype(jnp.bfloat16).reshape(batch, rows, width)
    shares = (
        lax.psum_scatter(
            grad_in_proj.astype(jnp.bfloat16), "fsdp", scatter_dimension=0, tiled=True
        ).astype(jnp.float32),
        lax.psum_scatter(
            grad_out_proj.astype(jnp.bfloat16), "fsdp", scatter_dimension=0, tiled=True
        ).astype(jnp.float32),
        lax.psum_scatter(
            grad_expand.astype(jnp.bfloat16), "fsdp", scatter_dimension=0, tiled=True
        ).astype(jnp.float32),
        lax.psum_scatter(
            grad_contract.astype(jnp.bfloat16), "fsdp", scatter_dimension=0, tiled=True
        ).astype(jnp.float32),
        lax.psum_scatter(
            grad_gain_one.astype(jnp.bfloat16), "fsdp", scatter_dimension=0, tiled=True
        ).astype(jnp.float32),
        lax.psum_scatter(
            grad_shift_one.astype(jnp.bfloat16), "fsdp", scatter_dimension=0, tiled=True
        ).astype(jnp.float32),
        lax.psum_scatter(
            grad_bias_query.astype(jnp.bfloat16), "fsdp", scatter_dimension=0, tiled=True
        ).astype(jnp.float32),
        lax.psum_scatter(
            grad_bias_value.astype(jnp.bfloat16), "fsdp", scatter_dimension=0, tiled=True
        ).astype(jnp.float32),
        lax.psum_scatter(
            grad_bias_attention.astype(jnp.bfloat16), "fsdp", scatter_dimension=0, tiled=True
        ).astype(jnp.float32),
        lax.psum_scatter(
            grad_gain_two.astype(jnp.bfloat16), "fsdp", scatter_dimension=0, tiled=True
        ).astype(jnp.float32),
        lax.psum_scatter(
            grad_shift_two.astype(jnp.bfloat16), "fsdp", scatter_dimension=0, tiled=True
        ).astype(jnp.float32),
        lax.psum_scatter(
            grad_bias_expand.astype(jnp.bfloat16), "fsdp", scatter_dimension=0, tiled=True
        ).astype(jnp.float32),
        lax.psum_scatter(
            grad_bias_contract.astype(jnp.bfloat16), "fsdp", scatter_dimension=0, tiled=True
        ).astype(jnp.float32),
    )
    totals = (
        lax.psum(shares[0].astype(jnp.bfloat16), "seq").astype(jnp.float32),
        lax.psum(shares[1].astype(jnp.bfloat16), "seq").astype(jnp.float32),
        lax.psum(shares[2].astype(jnp.bfloat16), "seq").astype(jnp.float32),
        lax.psum(shares[3].astype(jnp.bfloat16), "seq").astype(jnp.float32),
        lax.psum(shares[4].astype(jnp.bfloat16), "seq").astype(jnp.float32),
        lax.psum(shares[5].astype(jnp.bfloat16), "seq").astype(jnp.float32),
        lax.psum(shares[6].astype(jnp.bfloat16), "seq").astype(jnp.float32),
        lax.psum(shares[7].astype(jnp.bfloat16), "seq").astype(jnp.float32),
        lax.psum(shares[8].astype(jnp.bfloat16), "seq").astype(jnp.float32),
        lax.psum(shares[9].astype(jnp.bfloat16), "seq").astype(jnp.float32),
        lax.psum(shares[10].astype(jnp.bfloat16), "seq").astype(jnp.float32),
        lax.psum(shares[11].astype(jnp.bfloat16), "seq").astype(jnp.float32),
        lax.psum(shares[12].astype(jnp.bfloat16), "seq").astype(jnp.float32),
    )
    return (
        layer_out,
        grad_tokens,
        totals[4],
        totals[5],
        totals[0],
        totals[6],
        totals[7],
        totals[1],
        totals[8],
        totals[9],
        totals[10],
        totals[2],
        totals[11],
        totals[3],
        totals[12],
    )


MESH = pl.DeviceIdType.MESH
BF = jnp.bfloat16
F32 = jnp.float32
NEG = -1e30
GELU_A = math.sqrt(2.0 / math.pi)
GELU_B = 0.044715


def dot_nn(a, b):
    return lax.dot_general(a, b, (((1,), (0,)), ((), ())), preferred_element_type=F32)


def dot_nt(a, b):
    return lax.dot_general(a, b, (((1,), (1,)), ((), ())), preferred_element_type=F32)


def dot_tn(a, b):
    return lax.dot_general(a, b, (((0,), (0,)), ((), ())), preferred_element_type=F32)


def normalize(v):
    mean = jnp.mean(v, axis=-1, keepdims=True)
    centred = v - mean
    var = jnp.mean(centred * centred, axis=-1, keepdims=True)
    rstd = lax.rsqrt(var + norm_eps)
    return centred * rstd, rstd


def normalize_back(grad, gain, hat, rstd):
    g = grad * gain
    return rstd * (
        g
        - jnp.mean(g, axis=-1, keepdims=True)
        - hat * jnp.mean(g * hat, axis=-1, keepdims=True)
    )


def col_sum(v):
    return jnp.sum(v, axis=0, keepdims=True)


def layer_kernel(
    po, gl, tok, cot, win, wout, wexp, wcon, v0, v1, v2, v3, v4, v5, v6, v7, v8,
    lo, gt, h_in, h_out, h_e, h_c, g_sm,
    g_in, g_out, g_e, g_c,
    wi_a, wo_a, we_a, wc_a, sm_a, vec, ebv, lane_mask,
    x_a, e_a, a_a, qkv, bias, p0, p1, p2, p3, o_a, h_own, b_a, g_a, du_a,
    part, db, part_r, db_r, dr_a, dh_own, do_a, dd, acc_k, acc_v, stage,
    vec_g, eb_g,
    gi_acc,
    st_c, st_e, st_o, st_i, rh_c, ry_c, ry_e, ry_o, ry_i,
    rz_c, rz_e, rz_o, rz_i, xb_c, xb_e, xb_o, xb_i,
    rx_c, rx_e, rx_o, rx_i, fc_c, fc_e, fc_o, fc_i, rc_c, rc_e, rc_o, rc_i,
    st_s, rz_s, rx_s, sv_s, sv_r, sw_s, sw_r, su_s, su_r,
    in_s, gr_s, ag_s, ag_r, ax_s, ax_r, tk_s, tk_r, loc, ex_s, ex_r, rs_s, rs_r, cx_s, cx_r, out_s, out_r,
):
    f = lax.axis_index("fsdp")
    s = lax.axis_index("seq")
    z = f // 2
    y = f % 2
    x = s // 2
    c = s % 2
    dev_y = (z * 2 + 1 - y, s)
    dev_x = (f, (1 - x) * 2 + c)
    dev_c = (f, x * 2 + 1 - c)
    chunks, rows, width = x_a.shape
    length = chunks * rows

    def dev_z(zo):
        return (zo * 2 + y, s)

    def rcopy(src, dst, ssem, rsem, dev):
        return pltpu.make_async_remote_copy(
            src_ref=src, dst_ref=dst, send_sem=ssem, recv_sem=rsem, device_id=dev, device_id_type=MESH
        )

    def slot(zz, yy, at=z):
        return ((zz + at) % 2) * 4 + (zz // 2) * 2 + yy

    def owner(b):
        return 2 * ((z + b // 4) % 2 + 2 * ((b % 4) // 2)) + b % 2

    def flip(v, d):
        for bit in (1, 2, 4):
            if d & bit:
                v = v + bit - 2 * bit * ((v // bit) % 2)
        return v

    barrier = pltpu.get_barrier_semaphore()
    for d in range(1, 8):
        pl.semaphore_signal(barrier, inc=1, device_id=(flip(f, d), s), device_id_type=MESH)
    for d in range(1, 4):
        pl.semaphore_signal(barrier, inc=1, device_id=(f, flip(s, d)), device_id_type=MESH)

    def at_col(ref, col):
        return ref.at[:, pl.ds(pl.multiple_of(col, 128), 128)]

    loads = []
    for pr in range(2):
        for part_i in range(3):
            dst = wi_a.at[pr, f, :, part_i * 128 : part_i * 128 + 128]
            loads.append((at_col(win, part_i * width + c * 256 + pr * 128), dst))
    loads.append((wcon.at[pl.ds(pl.multiple_of(c * 128, 128), 128), :], wc_a.at[slot(z, y)]))
    for b in range(8):
        dst = we_a.at[b // 4, f, :, (b % 4) * 128 : (b % 4) * 128 + 128]
        loads.append((at_col(wexp, owner(b) * 256 + c * 128), dst))
    loads.append((wout, wo_a.at[f]))
    loads = [pltpu.make_async_copy(src, dst, in_s.at[i]) for i, (src, dst) in enumerate(loads)]
    for cp in loads:
        cp.start()
    sm_a[f] = jnp.zeros((16, 128), F32)
    for i, ref in enumerate((v0, v1, v2, v3, v4, v5, v6, v7)):
        sm_a[f, i : i + 1, 0:64] = ref[...].astype(F32).reshape(1, 64)
    eb = v8[...].astype(F32)
    sm_a[f, 8:9, :] = eb[0:128].reshape(1, 128)
    sm_a[f, 9:10, :] = eb[128:256].reshape(1, 128)
    for cp in loads:
        cp.wait()
    pl.semaphore_wait(barrier, 10)
    step = [0]
    actions = {}

    def point():
        for name in SCHEDULE[step[0]]:
            key, _, rest = name.partition(":")
            actions[key](*[int(v) for v in rest.split(".") if v])
        step[0] += 1

    col_c = pl.multiple_of(c * 256, 256)

    def view(g, zz, yy, half, at=z):
        o = zz * 2 + yy
        if g in (1, 2):
            return wi_a.at[g - 1, o]
        if g == 3:
            return wc_a.at[slot(zz, yy, at), pl.ds(pl.multiple_of(half * 64, 64), 64), :]
        if g == 5:
            return wo_a.at[o, :, pl.ds(col_c, 256)]
        if g == 4:
            return we_a.at[0, o]
        return we_a.at[1, o, pl.ds(pl.multiple_of(half * 32, 32), 32), :]

    def ag_copy(g, zz, yy, sem, dev, at=z):
        src = view(g, zz, yy, x)
        if g == 4 and at is not z:
            src = we_a.at[(z + at) % 2, zz * 2 + yy]
        if g == 6 and at is not z:
            src = we_a.at[(1 + z + at) % 2, zz * 2 + yy, pl.ds(pl.multiple_of(x * 32, 32), 32), :]
        return rcopy(src, view(g, zz, yy, x, at), ag_s.at[g, sem], ag_r.at[g, zz * 2 + yy], dev)

    def ax_copy(g, zz, yy, sem, half):
        ref = view(g, zz, yy, half)
        return rcopy(ref, ref, ax_s.at[g // 6, sem], ax_r.at[g // 6, zz * 2 + yy], dev_x)

    def small_first(d):
        return rcopy(sm_a.at[f], sm_a.at[f], su_s.at[d], su_r.at[f], (flip(f, d), s))

    def ag_start(g):
        if g == 0:
            for d in range(1, 8):
                small_first(d).start()
            return
        for d in (2,) if g == 3 else (1, 3) if g == 7 else (1, 2, 3):
            zo = (z + d) % 4
            ag_copy(3 if g == 7 else g, z, y, d - 1, dev_z(zo), zo).start()
        if g != 7:
            ag_copy(g, z, y, 3, dev_y).start()

    def ag_from_z(g, d):
        zo = (z + d) % 4
        cp = ag_copy(g, zo, y, 3 + d, dev_y)
        cp.wait_recv()
        cp.start()
        if g in (3, 6):
            ax_copy(g, zo, y, d - 1, x).start()

    def ag_from_y(g, d):
        zo = (z + d) % 4
        ag_copy(g, zo, 1 - y, 3, dev_y).wait_recv()
        ax_copy(g, zo, 1 - y, 3 + d, x).start()

    def ag_finish(g):
        if g in (3, 6, 7):
            for d in {3: (0, 2), 6: (0, 1, 2, 3), 7: (1, 3)}[g]:
                zo = (z + d) % 4
                o = 3 if g == 7 else g
                if d:
                    ax_copy(o, zo, y, d - 1, 1 - x).wait_recv()
                ax_copy(o, zo, 1 - y, 3 + d, 1 - x).wait_recv()
        else:
            for zo in range(4):
                ag_copy(g, zo, 1 - y, 3, dev_y).wait_recv()

    def ag_drain(g):
        for i in range(7):
            ag_copy(g, z, y, i, dev_y).wait_send()
            if g in (3, 6):
                ax_copy(g, z, y, i, x).wait_send()

    def swap_start(n, src, ref):
        rcopy(src.at[1 - x], ref.at[s], tk_s.at[n, 0], tk_r.at[n, 0], dev_x).start()
        rcopy(src.at[x], ref.at[s], tk_s.at[n, 1], tk_r.at[n, 1], dev_c).start()
        pltpu.make_async_copy(src.at[x], ref.at[s], loc.at[n]).start()

    def swap_forward(n, src, ref):
        k = (1 - x) * 2 + c
        rcopy(src.at[1 - x], ref.at[k], tk_s.at[n, 0], tk_r.at[n, 0], dev_x).wait_recv()
        rcopy(ref.at[k], ref.at[k], tk_s.at[n, 2], tk_r.at[n, 2], dev_c).start()

    def swap_finish(n, src, ref):
        rcopy(ref.at[s], ref.at[s], tk_s.at[n, 2], tk_r.at[n, 2], dev_c).wait_recv()

    def swap_near(n, src, ref):
        pltpu.make_async_copy(src.at[x], ref.at[s], loc.at[n]).wait()
        rcopy(src.at[x], ref.at[s], tk_s.at[n, 1], tk_r.at[n, 1], dev_c).wait_recv()

    def swap_drain(n, src, ref):
        rcopy(src.at[1 - x], ref.at[s], tk_s.at[n, 0], tk_r.at[n, 0], dev_x).wait_send()
        rcopy(src.at[x], ref.at[s], tk_s.at[n, 1], tk_r.at[n, 1], dev_c).wait_send()
        rcopy(ref.at[s], ref.at[s], tk_s.at[n, 2], tk_r.at[n, 2], dev_c).wait_send()

    swaps = ((tok, x_a), (cot, e_a))
    actions["start"] = ag_start
    actions["swap"] = lambda n: swap_start(n, *swaps[n])
    actions["share"] = lambda n: swap_forward(n, *swaps[n])
    actions["az"] = ag_from_z
    actions["ay"] = ag_from_y
    point()

    picked = lax.broadcasted_iota(jnp.int32, gl.shape, 1) == po[x]
    lengths = jnp.sum(jnp.where(picked, gl[...], 0), axis=1, keepdims=True)
    first_end = lengths[0:1, :]
    second_end = first_end + lengths[1:2, :]

    def mask_block(k, carry):
        qp = k * rows + lax.broadcasted_iota(jnp.int32, (rows, length), 0)
        kp = lax.broadcasted_iota(jnp.int32, (rows, length), 1)
        hidden_key = (kp >= first_end) & (kp < second_end) & (qp >= second_end)
        bad = (kp > qp) | hidden_key
        bias[k] = jnp.where(bad, NEG, 0.0).astype(F32)
        return carry

    lax.fori_loop(0, chunks, mask_block, 0)
    lanes = lax.broadcasted_iota(jnp.int32, (8, 128), 1)
    lane_row = lax.broadcasted_iota(jnp.int32, (8, 128), 0)
    lane_mask[...] = jnp.where((lanes < 64) == (lane_row < 1), 1.0, 0.0).astype(F32)
    vec_g[...] = jnp.zeros_like(vec_g)
    eb_g[...] = jnp.zeros_like(eb_g)

    point()
    for d in range(1, 8):
        ff = flip(f, d)
        rcopy(sm_a.at[ff], sm_a.at[ff], su_s.at[d], su_r.at[ff], (ff, s)).wait_recv()
    for r in range(4):
        low_half = sm_a[2 * r, 0:8, :]
        high_half = pltpu.roll(sm_a[2 * r + 1, 0:8, :], 64, 1)
        vec[:, r * 128 : r * 128 + 128] = jnp.where(lanes < 64, low_half, high_half)
    for b in range(8):
        ebv[:, b * 128 : b * 128 + 128] = sm_a[owner(b), pl.ds(8 + c, 1), :]
    swap_near(0, tok, x_a)
    point()
    swap_finish(0, tok, x_a)

    def norm_one(k, carry):
        hat, _ = normalize(x_a[k].astype(F32))
        a_a[k] = (hat * vec[0:1, :] + vec[1:2, :]).astype(BF)
        return carry

    lax.fori_loop(0, chunks, norm_one, 0)
    point()

    def project(pr):
        col = pl.multiple_of(c * 256 + pr * 128, 128)
        w = wi_a[pr].reshape(width, 384)
        for k in range(chunks):
            block = pl.ds(k * rows, rows)
            out = dot_nn(a_a[k], w)
            qkv[pr, block, 0:128] = (out[:, 0:128] + vec[2:3, pl.ds(col, 128)]).astype(BF)
            qkv[pr, block, 128:256] = out[:, 128:256].astype(BF)
            qkv[pr, block, 256:384] = (out[:, 256:384] + vec[3:4, pl.ds(col, 128)]).astype(BF)

    probs = (p0, p1, p2, p3)
    masks = [lane_mask[i : i + 1, :] for i in range(2)]
    masks_low = [m.astype(BF) for m in masks]
    scaled_low = [(m * 0.125).astype(BF) for m in masks]

    def split(v, kinds):
        return [v * m for m in kinds]

    def scores(pr, i):
        span = (i + 1) * rows
        q = qkv[pr, i * rows : i * rows + rows, 0:128]
        k = qkv[pr, 0:span, 128:256]
        return [dot_nt(qm, k) + bias[i, :, 0:span] for qm in split(q, scaled_low)]

    def attend(pr, i, sc):
        span = (i + 1) * rows
        v = qkv[pr, 0:span, 256:384]
        weights = []
        for hh in range(2):
            top = jnp.max(sc[hh], axis=-1, keepdims=True)
            ex = jnp.exp(sc[hh] - top)
            tot = jnp.sum(ex, axis=-1, keepdims=True)
            weights.append((ex * (1.0 / tot)).astype(BF))
            probs[i][pr, hh] = weights[hh]
        out = dot_nn(jnp.concatenate(weights, axis=1), jnp.concatenate(split(v, masks_low), axis=0))
        col = pl.multiple_of(c * 256 + pr * 128, 128)
        o_a[i, :, pl.ds(col, 128)] = out.astype(BF)

    def o_copy(pr):
        col = pl.multiple_of(c * 256 + pr * 128, 128)
        ref = o_a.at[:, :, pl.ds(col, 128)]
        return rcopy(ref, ref, ex_s.at[pr], ex_r.at[pr], dev_c)

    def wo_copy():
        ref = wo_a.at[:, :, pl.ds(col_c, 256)]
        return rcopy(ref, ref, ex_s.at[12], ex_r.at[12], dev_c)

    def wo_start():
        ag_finish(5)
        wo_copy().start()

    actions["wo"] = wo_start
    ag_finish(1)
    project(0)
    point()
    sc = scores(0, 0)
    for i in range(chunks):
        if i < chunks - 1:
            ahead = scores(0, i + 1)
        else:
            ag_finish(2)
            project(1)
            ahead = scores(1, 0)
        attend(0, i, sc)
        sc = ahead
        if i == chunks - 1:
            o_copy(0).start()
        point()
    for i in range(chunks):
        ahead = scores(1, i + 1) if i < chunks - 1 else None
        attend(1, i, sc)
        sc = ahead
        if i == chunks - 1:
            o_copy(1).start()
        point()
    for pr in range(2):
        o_copy(pr).wait_recv()
    ref = wo_a.at[:, :, pl.ds(pl.multiple_of((1 - c) * 256, 256), 256)]
    rcopy(ref, ref, ex_s.at[12], ex_r.at[12], dev_c).wait_recv()

    def b_copy(j):
        ref = b_a.at[c + 2 * j]
        return rcopy(ref, ref, ex_s.at[2 + j], ex_r.at[2 + j], dev_c)

    for j in range(2):
        k = c + 2 * j
        out = dot_nn(o_a[k], wo_a[...].reshape(width, width))
        h = x_a[k].astype(F32) + out + vec[4:5, :]
        h_own[j] = h
        hat, _ = normalize(h)
        b_a[k] = (hat * vec[5:6, :] + vec[6:7, :]).astype(BF)
        b_copy(j).start()
        point()
    swap_near(1, cot, e_a)
    swap_finish(1, cot, e_a)
    ag_finish(3)
    ag_finish(4)
    half = we_a.shape[3]

    def hidden(d):
        zi = ((z + d) % 4) // 2
        return d % 2, zi, pl.ds(pl.multiple_of(zi * 256, 256), 256)

    def mlp_chunk(d, j, first):
        k = (c + 2 * j) if j < 2 else (1 - c) + 2 * (j - 2)
        h, zi, cols = hidden(d)
        bias_cols = pl.ds(pl.multiple_of(h * half + zi * 256, 256), 256)
        we = we_a[h, :, :, cols].reshape(width, 256)
        wc = wc_a[pl.ds(4 * h + 2 * zi, 2)].reshape(256, width)
        u = dot_nn(b_a[k], we) + ebv[:, bias_cols]
        u2 = u * u
        th = jnp.tanh(u * (GELU_A + (GELU_A * GELU_B) * u2))
        hf = 0.5 * th + 0.5
        gf = u * hf
        g = gf.astype(BF)
        g_a[h, k, :, cols] = g
        slope = hf + (gf - gf * hf) * ((2.0 * GELU_A) + (6.0 * GELU_A * GELU_B) * u2)
        du = (slope * dot_nt(e_a[k], wc)).astype(BF)
        du_a[h, k, :, cols] = du
        eb_g[:, bias_cols] += col_sum(du.astype(F32))
        new_part = dot_nn(g, wc)
        new_db = dot_nt(du, we)
        if first:
            part[j] = new_part
            db[j] = new_db
        else:
            part[j] += new_part
            db[j] += new_db

    def part_copy(j):
        return rcopy(part.at[j], part_r.at[j - 2], ex_s.at[4 + j - 2], ex_r.at[4 + j - 2], dev_c)

    def db_copy(j):
        return rcopy(db.at[j], db_r.at[j - 2], ex_s.at[6 + j - 2], ex_r.at[6 + j - 2], dev_c)

    def rs_names(g):
        if g == 0:
            return (st_c, ry_c, rz_c, xb_c, rx_c, fc_c, rc_c)
        if g < 5:
            return tuple(r.at[g - 1] for r in (st_e, ry_e, rz_e, xb_e, rx_e, fc_e, rc_e))
        if g == 5:
            return (st_o, ry_o, rz_o, xb_o, rx_o, fc_o, rc_o)
        return tuple(r.at[g - 6] for r in (st_i, ry_i, rz_i, xb_i, rx_i, fc_i, rc_i))

    mine = pl.ds(pl.multiple_of(x * 64, 64), 64)
    theirs = pl.ds(pl.multiple_of((1 - x) * 64, 64), 64)

    def con_x(zt):
        return rcopy(st_c.at[:, zt, theirs], rh_c.at[zt], cx_s.at[zt], cx_r.at[zt], dev_x)

    def con_y(zt):
        return rcopy(st_c.at[1 - y, zt, mine], ry_c.at[zt], rs_s.at[0, zt], rs_r.at[0, zt], dev_y)

    def con_z(zt):
        return rcopy(st_c.at[y, zt, mine], rz_c.at[z], rs_s.at[0, 4 + zt], rs_r.at[0, 4 + z], dev_z(zt))

    def con_y_start(d):
        zt = (z + d) % 4
        con_x(zt).wait_recv()
        for yy in range(2):
            st_c[yy, zt, mine] = (st_c[yy, zt, mine].astype(F32) + rh_c[zt, yy].astype(F32)).astype(BF)
        con_y(zt).start()

    def con_z_start(d):
        zt = (z + d) % 4
        con_y(zt).wait_recv()
        st_c[y, zt, mine] = (st_c[y, zt, mine].astype(F32) + ry_c[zt].astype(F32)).astype(BF)
        if d:
            con_z(zt).start()

    def rs_y(g, zo):
        st, ry = rs_names(g)[:2]
        return rcopy(st.at[1 - y, zo], ry.at[zo], rs_s.at[g, zo], rs_r.at[g, zo], dev_y)

    def rs_z(g, zo):
        st, _, rz = rs_names(g)[:3]
        to = g
        if 0 < g < 5:
            at = (g + 3 + z - zo) % 4
            rz, to = rz_e.at[at], 1 + at
        return rcopy(st.at[y, zo], rz.at[z], rs_s.at[g, 4 + zo], rs_r.at[to, 4 + z], dev_z(zo))

    def rs_x(g):
        xb, rx = rs_names(g)[3:5]
        return rcopy(xb, rx, rs_s.at[g, 8], rs_r.at[g, 8], dev_x)

    def rs_c(g):
        fc, rc = rs_names(g)[5:7]
        return rcopy(fc, rc, rs_s.at[g, 9], rs_r.at[g, 9], dev_c)

    def rs_y_start(g):
        for d in (1, 2, 3, 0):
            rs_y(g, (z + d) % 4).start()

    def rs_z_start(g, d):
        zo = (z + d) % 4
        st, ry = rs_names(g)[:2]
        rs_y(g, zo).wait_recv()
        st[y, zo] = (st[y, zo].astype(F32) + ry[zo].astype(F32)).astype(st.dtype)
        rs_z(g, zo).start()

    def rs_x_start(g):
        st, ry, rz, xb = rs_names(g)[:4]
        if g == 0:
            total = st_c[y, z, mine].astype(F32)
        else:
            rs_y(g, z).wait_recv()
            total = st[y, z].astype(F32) + ry[z].astype(F32)
        for d in range(1, 4):
            zo = (z + d) % 4
            if g == 0:
                cp = rcopy(st_c.at[y, zo, mine], rz.at[zo], rs_s.at[g, 4 + zo], rs_r.at[g, 4 + zo], dev_z(zo))
            else:
                cp = rcopy(st.at[y, zo], rz.at[zo], rs_s.at[g, 4 + zo], rs_r.at[g, 4 + zo], dev_z(zo))
            cp.wait_recv()
            total = total + rz[zo].astype(F32)
        xb[...] = total.astype(xb.dtype)
        rs_x(g).start()

    def write_out(g, side, value):
        if g == 0:
            g_c[pl.ds(pl.multiple_of(side * 128, 128), 128), :] = value
        elif g < 5:
            for yy in range(2):
                ff = 2 * ((z + g - 1) % 4) + yy
                col = pl.multiple_of(ff * 256 + side * 128, 128)
                g_e[:, pl.ds(col, 128)] = value[:, yy * 128 : yy * 128 + 128]
        elif g == 5:
            g_out[:, pl.ds(pl.multiple_of(side * 256, 256), 256)] = value
        else:
            for part_i in range(3):
                col = pl.multiple_of(part_i * width + side * 256 + (g - 6) * 128, 128)
                g_in[:, pl.ds(col, 128)] = value[:, part_i * 128 : part_i * 128 + 128]

    def rs_c_start(g):
        xb, rx, fc = rs_names(g)[3:6]
        rs_x(g).wait_recv()
        if g == 0:
            fc[mine] = xb[...].astype(F32)
            fc[theirs] = rx[...].astype(F32)
        else:
            fc[...] = xb[...].astype(F32) + rx[...].astype(F32)
        rs_c(g).start()
        write_out(g, c, fc[...])

    def rs_finish(g):
        fc, rc = rs_names(g)[5:7]
        rs_c(g).wait_recv()
        write_out(g, 1 - c, rc[...])
        written.append(g)
        for members, src, dst, sem in copies:
            if g in members and all(m in written for m in members):
                pltpu.make_async_copy(src, dst, gr_s.at[sem]).start()

    written = []
    copies = (
        ((0,), g_c, h_c, 0),
        ((1, 2, 3, 4), g_e, h_e, 1),
        ((5,), g_out, h_out, 2),
        ((6, 7), g_in, h_in, 3),
    )

    def rs_drain(g):
        for d in range(4):
            zo = (z + d) % 4
            if g == 0:
                con_x(zo).wait_send()
                con_y(zo).wait_send()
            else:
                rs_y(g, zo).wait_send()
            if d:
                (con_z(zo) if g == 0 else rs_z(g, zo)).wait_send()
        rs_x(g).wait_send()
        rs_c(g).wait_send()

    def grad_con(d):
        zt = (z + d) % 4
        h, _, cols = hidden(d)
        out = dot_tn(g_a[h, :, :, cols].reshape(length, 256), e_a[...].reshape(length, width))
        st_c[0, zt] = out[0:128].astype(BF)
        st_c[1, zt] = out[128:256].astype(BF)
        con_x(zt).start()

    def grad_exp(d):
        h, _, cols = hidden(d)
        out = dot_tn(b_a[...].reshape(length, width), du_a[h, :, :, cols].reshape(length, 256))
        for ff in range(8):
            st_e[d, ff % 2, ff // 2] = out[ff * 64 : ff * 64 + 64].astype(BF)
        rs_y_start(1 + d)

    actions["cy"] = con_y_start
    actions["cz"] = con_z_start
    actions["rz"] = rs_z_start
    actions["rx"] = rs_x_start
    actions["rc"] = rs_c_start
    actions["rf"] = rs_finish
    for d in (2, 0, 1, 3):
        if d == 1:
            ag_finish(7)
            ag_finish(6)
        for n, j in enumerate((0, 1, 2, 3) if d == 2 else (2, 3, 0, 1)):
            if d == 2 and j >= 2:
                ref = b_a.at[1 - c + 2 * (j - 2)]
                rcopy(ref, ref, ex_s.at[j], ex_r.at[j], dev_c).wait_recv()
            mlp_chunk(d, j, d == 2)
            if d == 3 and j >= 2:
                part_copy(j).start()
                db_copy(j).start()
            if n % 2:
                point()
        grad_con(d)
        point()
        grad_exp(d)
        point()

    def send_rows(n, ref, out):
        far = rcopy(stage.at[n, 1 - x], out.at[x], out_s.at[n, 0], out_r.at[n], dev_x)
        near = pltpu.make_async_copy(stage.at[n, x], out.at[x], out_s.at[n, 1])
        return far, near

    def dr_copy(j):
        ref = dr_a.at[c + 2 * j]
        return rcopy(ref, ref, ex_s.at[8 + j], ex_r.at[8 + j], dev_c)

    for j in range(2):
        k = c + 2 * j
        h = h_own[j]
        e = e_a[k].astype(F32)
        rcopy(db.at[j + 2], db_r.at[j], ex_s.at[6 + j], ex_r.at[6 + j], dev_c).wait_recv()
        grad_b = db[j] + db_r[j]
        hat, rstd = normalize(h)
        dh = e + normalize_back(grad_b, vec[5:6, :], hat, rstd)
        dh_own[j] = dh
        dr = dh.astype(BF)
        dr_a[k] = dr
        dr_copy(j).start()
        vec_g[4:5, :] += col_sum(dr.astype(F32))
        vec_g[5:6, :] += col_sum(grad_b * hat)
        vec_g[6:7, :] += col_sum(grad_b)
        vec_g[7:8, :] += col_sum(e)
        rcopy(part.at[j + 2], part_r.at[j], ex_s.at[4 + j], ex_r.at[4 + j], dev_c).wait_recv()
        stage[0, j] = (h + part[j] + part_r[j] + vec[7:8, :]).astype(BF)
        point()
    for cp in send_rows(0, stage, lo):
        cp.start()

    head_row = pl.multiple_of(c * 4, 4)

    def grad_mixed(k):
        w = wo_a[pl.ds(head_row, 4)].reshape(256, width)
        do_a[k] = dot_nt(dr_a[k], w).astype(BF)

    for j in range(2):
        grad_mixed(c + 2 * j)
    point()
    for j in range(2):
        ref = dr_a.at[1 - c + 2 * j]
        rcopy(ref, ref, ex_s.at[8 + j], ex_r.at[8 + j], dev_c).wait_recv()
        grad_mixed(1 - c + 2 * j)
    point()
    out = dot_tn(o_a[...].reshape(length, width), dr_a[:, :, pl.ds(col_c, 256)].reshape(length, 256))
    for ff in range(8):
        st_o[ff % 2, ff // 2] = out[ff * 64 : ff * 64 + 64].astype(BF)
    rs_y_start(5)
    point()

    def grad_probs(pr, i):
        v = qkv[pr, 0 : (i + 1) * rows, 256:384]
        do = do_a[i, :, pr * 128 : pr * 128 + 128]
        return [dot_nt(dom, v) for dom in split(do, masks_low)]

    def attend_back(pr, i, gp):
        span = (i + 1) * rows
        block = pl.ds(i * rows, rows)
        q = qkv[pr, block, 0:128]
        k = qkv[pr, 0:span, 128:256]
        do = do_a[i, :, pr * 128 : pr * 128 + 128]
        ds = []
        for hh in range(2):
            pf = probs[i][pr, hh].astype(F32)
            t = pf * gp[hh]
            inner = jnp.sum(t, axis=-1, keepdims=True)
            ds.append((t - pf * inner).astype(BF))
        both = jnp.concatenate([probs[i][pr, 0], probs[i][pr, 1]], axis=0)
        grad_v = dot_tn(both, jnp.concatenate(split(do, masks_low), axis=0))
        grad_k = dot_tn(jnp.concatenate(ds, axis=0), jnp.concatenate(split(q, scaled_low), axis=0))
        if i == chunks - 1:
            acc_v[...] = grad_v
            acc_k[...] = grad_k
        else:
            acc_v[0:span] += grad_v
            acc_k[0:span] += grad_k
        grad_q = dot_nn(
            jnp.concatenate(ds, axis=1), jnp.concatenate(split(k, scaled_low), axis=0)
        ).astype(BF)
        grad_k = acc_k[block].astype(BF)
        grad_v = acc_v[block].astype(BF)
        dd[pr, block, 0:128] = grad_q
        dd[pr, block, 128:256] = grad_k
        dd[pr, block, 256:384] = grad_v
        col = pl.multiple_of(c * 256 + pr * 128, 128)
        vec_g[2:3, pl.ds(col, 128)] += col_sum(grad_q.astype(F32))
        vec_g[3:4, pl.ds(col, 128)] += col_sum(grad_v.astype(F32))

    def grad_in(pr, out):
        for ff in range(8):
            st_i[pr, ff % 2, ff // 2] = out[ff * 64 : ff * 64 + 64].astype(BF)
        rs_y_start(6 + pr)

    def da_copy(j):
        return rcopy(part.at[j], db_r.at[j - 2], ex_s.at[10 + j - 2], ex_r.at[10 + j - 2], dev_c)

    def grad_a(i):
        total = None
        for pr in range(2):
            p = dot_nt(dd[pr, i * rows : i * rows + rows, :], wi_a[pr].reshape(width, 384))
            total = p if total is None else total + p
        other = (i + c) % 2
        part[i // 2 + 2 * other] = total

        @pl.when(other == 1)
        def _():
            da_copy(2 + i // 2).start()

    def norm_one_back(j):
        k = c + 2 * j
        rcopy(part.at[j + 2], db_r.at[j], ex_s.at[10 + j], ex_r.at[10 + j], dev_c).wait_recv()
        grad = part[j] + db_r[j]
        hat, rstd = normalize(x_a[k].astype(F32))
        vec_g[0:1, :] += col_sum(grad * hat)
        vec_g[1:2, :] += col_sum(grad)
        stage[1, j] = (dh_own[j] + normalize_back(grad, vec[0:1, :], hat, rstd)).astype(BF)

    order = [(pr, i) for pr in range(2) for i in range(chunks - 1, -1, -1)]
    gp = grad_probs(*order[0])
    for n, (pr, i) in enumerate(order):
        ahead = grad_probs(*order[n + 1]) if n < 7 else None
        attend_back(pr, i, gp)
        gp = ahead
        if pr == 0 and i == 0:
            grad_in(0, dot_tn(a_a[...].reshape(length, width), dd[0]))
            for j in range(2, 4):
                part_copy(j).wait_send()
        if pr == 1:
            block = dot_tn(a_a[i], dd[1, i * rows : i * rows + rows, :])
            if i == chunks - 1:
                gi_acc[...] = block
            elif i > 0:
                gi_acc[...] += block
            else:
                grad_in(1, gi_acc[...] + block)
                point()
            grad_a(i)
            if i < 2:
                norm_one_back(i)
        point()
    for cp in send_rows(1, stage, gt):
        cp.start()

    for r in range(4):
        tile = vec_g[:, r * 128 : r * 128 + 128]
        rolled = pltpu.roll(tile, 64, 1)
        for yy in range(2):
            ff = 2 * r + yy
            st_s[ff, 0:8, :] = tile if yy == 0 else rolled
            st_s[ff, 8:16, :] = jnp.zeros((8, 128), F32)
            lane = pl.multiple_of(slot(r, yy) * 128, 128)
            st_s[ff, pl.ds(8 + c, 1), :] = eb_g[:, pl.ds(lane, 128)]

    def small_copy(d):
        ff = flip(f, d)
        return rcopy(st_s.at[ff], rz_s.at[f], sv_s.at[d], sv_r.at[f], (ff, s))

    def small_last(d):
        ss = flip(s, d)
        return rcopy(rx_s.at[s], rx_s.at[s], sw_s.at[d], sw_r.at[s], (f, ss))

    for d in range(1, 8):
        small_copy(d).start()

    def small_sum():
        rz_s[f] = st_s[f]
        for d in range(1, 8):
            ff = flip(f, d)
            rcopy(st_s.at[ff], rz_s.at[ff], sv_s.at[d], sv_r.at[ff], (ff, s)).wait_recv()
        total = rz_s[0]
        for ff in range(1, 8):
            total = total + rz_s[ff]
        rx_s[s] = total
        for d in range(1, 4):
            small_last(d).start()

    def small_end():
        for d in range(1, 4):
            ss = flip(s, d)
            rcopy(rx_s.at[ss], rx_s.at[ss], sw_s.at[d], sw_r.at[ss], (f, ss)).wait_recv()
        g_sm[...] = (rx_s[0] + rx_s[1]) + (rx_s[2] + rx_s[3])

    actions["sb"] = small_sum
    actions["sc"] = small_end
    point()
    for n, out in ((0, lo), (1, gt)):
        far, near = send_rows(n, stage, out)
        near.wait()
        far.wait_send()
        rcopy(stage.at[n, 1 - x], out.at[1 - x], out_s.at[n, 0], out_r.at[n], dev_x).wait_recv()
    for _, src, dst, sem in copies:
        pltpu.make_async_copy(src, dst, gr_s.at[sem]).wait()
    for g in range(1, 7):
        ag_drain(g)
    swap_drain(0, tok, x_a)
    swap_drain(1, cot, e_a)
    wo_copy().wait_send()
    for pr in range(2):
        o_copy(pr).wait_send()
    for j in range(2):
        b_copy(j).wait_send()
        dr_copy(j).wait_send()
        db_copy(j + 2).wait_send()
        da_copy(j + 2).wait_send()
    for g in range(8):
        rs_drain(g)
    for d in range(1, 8):
        small_copy(d).wait_send()
        small_first(d).wait_send()
    for d in range(1, 4):
        small_last(d).wait_send()


SCHEDULE = (
    ("start:3", "start:1", "start:0", "swap:0", "swap:1", "start:2", "start:5", "start:4", "az:3.2", "start:6", "az:1.2",),
    ("az:1.1", "az:1.3", "share:0", "ay:3.2",),
    ("az:2.1", "az:2.3", "az:2.2",),
    ("ay:3.0",),
    ("start:7", "az:5.3", "az:5.2", "az:5.1",),
    ("az:4.3",),
    (),
    ("ay:6.0", "az:4.2", "share:1",),
    ("az:6.1", "az:4.1",),
    (),
    ("az:6.2", "az:6.3",),
    (),
    ("ay:6.1", "wo", "az:3.3", "az:3.1", "ay:6.2",),
    (),
    (),
    ("ay:6.3", "ay:3.3",),
    ("ay:3.1",),
    (),
    (),
    (),
    (),
    (),
    (),
    ("rz:3.1", "rz:3.2", "rz:3.3",),
    (),
    (),
    (),
    ("rz:1.2", "rz:1.1",),
    (),
    (),
    (),
    ("rz:1.3", "rz:2.2", "rz:2.1", "rz:2.3",),
    (),
    ("cy:2",),
    ("cy:1", "rz:4.2", "rz:4.3", "rz:4.1", "cy:3",),
    ("cy:0", "cz:2",),
    (),
    ("cz:1", "rx:4",),
    ("cz:3",),
    ("rz:5.2", "rx:1", "rz:5.1",),
    ("rc:4", "rz:5.3", "rx:2", "cz:0",),
    ("rz:6.1", "rx:0", "rz:6.2",),
    (),
    ("rz:6.3", "rc:2", "rx:5",),
    ("rx:3",),
    ("rz:7.1", "rz:7.2", "rz:7.3", "rc:0", "rc:1", "rc:5", "rx:6", "sb", "rx:7", "rf:4", "rf:1", "rf:2", "rf:0", "rf:5", "rc:3", "rc:6", "rc:7", "rf:3", "rf:6", "sc", "rf:7",),
)


def finish_kernel(*refs):
    gs = refs[6]
    outs = refs[7:]
    for i in range(6):
        outs[i][...] = refs[i][...]
    for i in range(8):
        outs[6 + i][...] = gs[i : i + 1, 0 : outs[6 + i].shape[1]]
    outs[14][:, 0:128] = gs[8:9, :]
    outs[14][:, 128:256] = gs[9:10, :]


def fast_shards(
    tokens, placement_order, group_lengths, first_gain, first_shift, attention_in, query_bias,
    value_bias, attention_out, attention_bias, second_gain, second_shift, expand_weight,
    expand_bias, contract_weight, contract_bias, cotangent,
):
    batch, rows, width = tokens.shape
    lanes = first_gain.shape[0]
    chunks = 4
    length = chunks * rows
    half = expand_weight.shape[1] // 4
    vm = pl.BlockSpec(memory_space=pltpu.VMEM)
    sm = pl.BlockSpec(memory_space=pltpu.SMEM)
    hb = pl.BlockSpec(memory_space=pl.ANY)
    V = pltpu.VMEM
    pieces = (((128, width), None), ((64, 256), 4), ((64, 256), None), ((64, 384), 2))

    def family(lead, dtype, con=128):
        out = []
        for n, (shape, pairs) in enumerate(pieces):
            if n == 0:
                shape = (con, width)
            pre = () if pairs is None else (pairs,)
            out.append(V(pre + lead + shape, dtype))
        return out

    dma = pltpu.SemaphoreType.DMA
    scratch = [
        V(attention_in.shape, F32), V(attention_out.shape, F32), V(expand_weight.shape, F32),
        V(contract_weight.shape, F32),
        V((2, 8, 64, 384), BF), V((8, 64, width), BF), V((2, 8, 64, half), BF), V((8, 128, width), BF),
        V((8, 16, 128), F32), V((8, width), F32), V((1, 2 * half), F32), V((8, 128), F32),
        V((chunks, rows, width), BF), V((chunks, rows, width), BF), V((chunks, rows, width), BF),
        V((2, length, 384), BF), V((chunks, rows, length), F32),
        V((2, 2, rows, rows), BF), V((2, 2, rows, 2 * rows), BF), V((2, 2, rows, 3 * rows), BF),
        V((2, 2, rows, 4 * rows), BF),
        V((chunks, rows, width), BF), V((2, rows, width), F32), V((chunks, rows, width), BF),
        V((2, chunks, rows, half), BF), V((2, chunks, rows, half), BF),
        V((4, rows, width), F32), V((4, rows, width), F32), V((2, rows, width), F32),
        V((2, rows, width), F32), V((chunks, rows, width), BF), V((2, rows, width), F32),
        V((chunks, rows, 256), BF), V((2, length, 384), BF), V((length, 128), F32),
        V((length, 128), F32), V((2, 2, rows, width), BF), V((8, width), F32), V((1, 2 * half), F32),
    ]
    scratch += [V((width, 384), F32)]
    scratch += family((2, 4), BF) + [V((4, 2, 64, width), BF)] + family((4,), BF, 64)
    scratch += family((4,), BF, 64) + family((), BF, 64) + family((), BF, 64)
    scratch += family((), F32) + family((), F32)
    scratch += [V((8, 16, 128), F32), V((8, 16, 128), F32), V((4, 16, 128), F32)]
    scratch += [dma((8,)), dma((8,)), dma((4,)), dma((4,)), dma((8,)), dma((8,))]
    scratch += [
        dma((16,)), dma((6,)), dma((7, 7)), dma((7, 8)), dma((2, 7)), dma((2, 8)), dma((2, 3)), dma((2, 3)), dma((2,)),
        dma((13,)), dma((13,)), dma((8, 10)), dma((8, 10)), dma((4,)), dma((4,)), dma((2, 2)), dma((2,)),
    ]
    grads = (
        jax.ShapeDtypeStruct(tokens.shape, BF),
        jax.ShapeDtypeStruct(tokens.shape, BF),
        jax.ShapeDtypeStruct(attention_in.shape, F32),
        jax.ShapeDtypeStruct(attention_out.shape, F32),
        jax.ShapeDtypeStruct(expand_weight.shape, F32),
        jax.ShapeDtypeStruct(contract_weight.shape, F32),
    )
    outs = pl.pallas_call(
        layer_kernel,
        out_shape=grads + (jax.ShapeDtypeStruct((16, 128), F32),),
        in_specs=[sm, vm] + [hb] * 6 + [vm] * 9,
        out_specs=[hb] * 6 + [vm],
        scratch_shapes=scratch,
        compiler_params=pltpu.CompilerParams(
            collective_id=0, has_side_effects=True, vmem_limit_bytes=63 << 20
        ),
    )(
        placement_order, group_lengths.T, tokens, cotangent, attention_in, attention_out,
        expand_weight, contract_weight, first_gain, first_shift, query_bias, value_bias,
        attention_bias, second_gain, second_shift, contract_bias, expand_bias,
    )

    def rows_of(shape):
        if len(shape) == 3:
            return pl.BlockSpec((shape[0], shape[1] // 2, shape[2]), lambda i: (0, i, 0))
        return pl.BlockSpec((shape[0] // 2, shape[1]), lambda i: (i, 0))

    def whole(shape):
        return pl.BlockSpec(shape, lambda i: (0, 0))

    outs = pl.pallas_call(
        finish_kernel,
        out_shape=grads
        + tuple(jax.ShapeDtypeStruct((1, lanes), F32) for _ in range(8))
        + (jax.ShapeDtypeStruct((1, 256), F32),),
        grid=(2,),
        in_specs=[rows_of(item.shape) for item in grads] + [whole((16, 128))],
        out_specs=[rows_of(item.shape) for item in grads] + [whole((1, lanes))] * 8 + [whole((1, 256))],
    )(*outs)
    layer_out, grad_tokens, g_in, g_out, g_e, g_c = outs[:6]
    v = [item.reshape(-1) for item in outs[6:]]
    return (
        layer_out, grad_tokens, v[0], v[1], g_in, v[2], v[3], g_out,
        v[4], v[5], v[6], g_e, v[8], g_c, v[7],
    )


def solution(mesh):
    in_specs = (
        P("fsdp", "seq", None),
        P("fsdp"),
        P(),
        P("fsdp"),
        P("fsdp"),
        P("fsdp", None),
        P("fsdp"),
        P("fsdp"),
        P("fsdp", None),
        P("fsdp"),
        P("fsdp"),
        P("fsdp"),
        P("fsdp", None),
        P("fsdp"),
        P("fsdp", None),
        P("fsdp"),
        P("fsdp", "seq", None),
    )
    out_specs = (
        P("fsdp", "seq", None),
        P("fsdp", "seq", None),
        P("fsdp"),
        P("fsdp"),
        P("fsdp", None),
        P("fsdp"),
        P("fsdp"),
        P("fsdp", None),
        P("fsdp"),
        P("fsdp"),
        P("fsdp"),
        P("fsdp", None),
        P("fsdp"),
        P("fsdp", None),
        P("fsdp"),
    )
    pick = fast_shards if (mesh.shape["fsdp"], mesh.shape["seq"]) == (8, 4) else shards
    return jax.shard_map(pick, mesh=mesh, in_specs=in_specs, out_specs=out_specs, check_vma=False)
```
